32 devices in a mesh: dp: 4 (over y, core), fsdp: 8 (over z, x).
Axes of the slice: x: 2, y: 2, z: 4, core: 2. Of those that a mesh axis runs over, the one named last changes fastest.
Arguments:
- tokens: bfloat16 [96, 1280, 768], P(('dp', 'fsdp')), may hold values from -6 to 6
- cotangent: bfloat16 [96, 1280, 768], P(('dp', 'fsdp')), may hold values from -6 to 6
- segment_ids: int32 [96, 1280], P(('dp', 'fsdp')), may hold values from 0 to 3, never falling along the last dimension, each value on 1 to 640 neighbouring positions
- routed: int32 [96, 160], P(('dp', 'fsdp')), may hold values from 0 to 1279, as said below
- qkv_weight: float32 [3, 768, 768], P(None, ('dp', 'fsdp')), may hold values from -0.21875 to 0.21875
- qkv_mean: float32 [3, 768, 768], P(None, ('dp', 'fsdp')), may hold values from -384 to 384
- qkv_square: float32 [3, 768, 768], P(None, ('dp', 'fsdp')), may hold values from 3840 to 15360
- qkv_average: float32 [3, 768, 768], P(None, ('dp', 'fsdp')), may hold values from -0.21875 to 0.21875
- out_weight: float32 [768, 768], P(('dp', 'fsdp')), may hold values from -0.625 to 0.625
- out_mean: float32 [768, 768], P(('dp', 'fsdp')), may hold values from -320 to 320
- out_square: float32 [768, 768], P(('dp', 'fsdp')), may hold values from 2457.6 to 9830.4
- out_average: float32 [768, 768], P(('dp', 'fsdp')), may hold values from -0.625 to 0.625
- up_weight: float32 [768, 3072], P(('dp', 'fsdp')), may hold values from -0.21875 to 0.21875
- up_mean: float32 [768, 3072], P(('dp', 'fsdp')), may hold values from -224 to 224
- up_square: float32 [768, 3072], P(('dp', 'fsdp')), may hold values from 1382.4 to 5529.6
- up_average: float32 [768, 3072], P(('dp', 'fsdp')), may hold values from -0.21875 to 0.21875
- down_weight: float32 [3072, 768], P(('dp', 'fsdp')), may hold values from -0.109375 to 0.109375
- down_mean: float32 [3072, 768], P(('dp', 'fsdp')), may hold values from -512 to 512
- down_square: float32 [3072, 768], P(('dp', 'fsdp')), may hold values from 6451.2 to 26112
- down_average: float32 [3072, 768], P(('dp', 'fsdp')), may hold values from -0.109375 to 0.109375
- router_weight: float32 [768], P(('dp', 'fsdp')), may hold values from -0.21875 to 0.21875
- router_mean: float32 [768], P(('dp', 'fsdp')), may hold values from -12288 to 12288
- router_square: float32 [768], P(('dp', 'fsdp')), may hold values from 3932160 to 15728640
- router_average: float32 [768], P(('dp', 'fsdp')), may hold values from -0.21875 to 0.21875
- norm_gains: float32 [2, 768], P(None, ('dp', 'fsdp')), may hold values from 0.5 to 1.5
- gains_mean: float32 [2, 768], P(None, ('dp', 'fsdp')), may hold values from -768 to 768
- gains_square: float32 [2, 768], P(None, ('dp', 'fsdp')), may hold values from 15360 to 61440
- gains_average: float32 [2, 768], P(None, ('dp', 'fsdp')), may hold values from 0.5 to 1.5
Outputs:
- block_out: bfloat16 [96, 1280, 768], P(('dp', 'fsdp'))
- tokens_grad: bfloat16 [96, 1280, 768], P(('dp', 'fsdp'))
- qkv_next: float32 [3, 768, 768], P(None, ('dp', 'fsdp'))
- qkv_mean_next: float32 [3, 768, 768], P(None, ('dp', 'fsdp'))
- qkv_square_next: float32 [3, 768, 768], P(None, ('dp', 'fsdp'))
- qkv_average_next: float32 [3, 768, 768], P(None, ('dp', 'fsdp'))
- out_next: float32 [768, 768], P(('dp', 'fsdp'))
- out_mean_next: float32 [768, 768], P(('dp', 'fsdp'))
- out_square_next: float32 [768, 768], P(('dp', 'fsdp'))
- out_average_next: float32 [768, 768], P(('dp', 'fsdp'))
- up_next: float32 [768, 3072], P(('dp', 'fsdp'))
- up_mean_next: float32 [768, 3072], P(('dp', 'fsdp'))
- up_square_next: float32 [768, 3072], P(('dp', 'fsdp'))
- up_average_next: float32 [768, 3072], P(('dp', 'fsdp'))
- down_next: float32 [3072, 768], P(('dp', 'fsdp'))
- down_mean_next: float32 [3072, 768], P(('dp', 'fsdp'))
- down_square_next: float32 [3072, 768], P(('dp', 'fsdp'))
- down_average_next: float32 [3072, 768], P(('dp', 'fsdp'))
- router_next: float32 [768], P(('dp', 'fsdp'))
- router_mean_next: float32 [768], P(('dp', 'fsdp'))
- router_square_next: float32 [768], P(('dp', 'fsdp'))
- router_average_next: float32 [768], P(('dp', 'fsdp'))
- gains_next: float32 [2, 768], P(None, ('dp', 'fsdp'))
- gains_mean_next: float32 [2, 768], P(None, ('dp', 'fsdp'))
- gains_square_next: float32 [2, 768], P(None, ('dp', 'fsdp'))
- gains_average_next: float32 [2, 768], P(None, ('dp', 'fsdp'))
The draws below stay inside these ranges and needn't reach their ends.
Inputs may be any that keep to these rules, and one draw needn't show every extreme that they name: `routed`: each row holds 160 different positions of its sequence in ascending order.
All inputs are finite; a program needn't handle non-finite values.
Results may differ from the reference program's by a relative error of at most 0.012.
The reference program's roundings to bfloat16 on the way count: a program that leaves them out, or rounds other values in their place, can miss the bound.
Values may be sent and summed in bfloat16 or wider, within the bound.
No kernel may reach another device: no remote copies, remote signals or barrier semaphores. Data moves between devices by JAX's collectives and lax.ppermute only.
A program may use at most 192 MiB of HBM per device.

```python
import math
import jax
import jax.numpy as jnp
import numpy as np
from jax import lax

D = 768
HEADS = 12
HDIM = 64
FF = 3072
LEN = 1280
CAP = 160
SEQS = 96
ROUTED_ALL = 15360


def draw_routed(key, part):
    seq_keys = jax.random.split(key, SEQS)

    def pick_one(seq_key):
        order = jax.random.permutation(seq_key, LEN)
        return jnp.sort(order[:CAP])
    return jax.vmap(pick_one)(seq_keys).astype(jnp.int32)


def block_scale(rng, extent, pieces, low, largest):
    level = 1.0
    for dim, parts in pieces:
        heights = jax.random.uniform(jax.random.fold_in(jax.random.fold_in(rng, 6), dim), (parts,), jnp.float32, low / len(pieces), largest / len(pieces))
        level = level * jnp.repeat(jnp.exp(heights), extent[dim] // parts).reshape((-1,) + (1,) * (len(extent) - 1 - dim))
    return level


def length_profile(number_of, total, limit, skew):
    loads = [(1 << 20) // math.isqrt(rank ** skew) + 1 for rank in range(2, number_of + 1)]
    spare, holding = total - limit - (number_of - 1), [1] * (number_of - 1)
    while spare > 0:
        candidates = [i for i in range(number_of - 1) if holding[i] < limit]
        mass, remaining = sum([loads[i] for i in candidates]), spare
        for i in candidates:
            extra = min(limit - holding[i], max(1, remaining * loads[i] // mass), spare)
            holding[i] = holding[i] + extra
            spare = spare - extra
    return np.array([limit] + holding)


def uneven(rng, amount, total, limit, skew):
    if amount == 2:
        one = jax.random.randint(rng, (), max(1, total - limit), min(limit, total - 1) + 1)
        return jnp.stack([one, total - one])
    lengths = jnp.asarray(length_profile(amount, total, limit, skew), jnp.int32)
    pairs = (amount - 1) // 2
    donor, taker = lengths[1:1 + 2 * pairs:2], lengths[2:2 + 2 * pairs:2]
    slack = jnp.minimum(donor - 1, limit - taker)
    passed = jax.random.randint(jax.random.fold_in(rng, 1), (pairs,), 0, 1 << 20) % (slack + 1)
    lengths = lengths.at[1:1 + 2 * pairs:2].set(donor - passed).at[2:2 + 2 * pairs:2].set(taker + passed)
    return lengths[jax.random.permutation(jax.random.fold_in(rng, 2), amount)]


def centred(stream_key, shape, scale, most, cuts=(), kind=jnp.bfloat16):
    entries = scale * jax.random.normal(stream_key, shape, jnp.float32)
    if cuts:
        entries = entries * block_scale(stream_key, shape, cuts, -0.22, 0.18)
    return jnp.clip(entries, -most, most).astype(kind)


def setup_inputs(seed: int = 0) -> dict:
    key_list = jax.random.split(jax.random.key(seed), 29)
    tokens = centred(key_list[0], (SEQS, LEN, D), 1.0, 6.0, ((0, 32),))
    cotangent = centred(key_list[1], (SEQS, LEN, D), 1.0, 6.0, ((0, 32),))
    segment_ids = jax.vmap(lambda own: jnp.searchsorted(jnp.cumsum(uneven(own, 4, LEN, LEN // 2, 2)), jnp.arange(LEN), side="right"))(jax.random.split(key_list[2], SEQS)).reshape((SEQS, LEN)).astype(jnp.int32)
    routed = draw_routed(jax.random.fold_in(key_list[28], 71), 0)
    qkv_weight = centred(key_list[4], (3, D, D), D ** -0.5, 0.21875, ((1, 32),), jnp.float32)
    qkv_mean = centred(key_list[5], (3, D, D), (0.5 * ROUTED_ALL ** 0.5), 384.0, ((1, 32),), jnp.float32)
    qkv_square = jnp.clip(jnp.exp(math.log(15360.0) - 1.3862944 * jax.random.uniform(key_list[6], (3, D, D), jnp.float32) ** block_scale(key_list[6], (3, D, D), ((1, 32),), -0.2, 0.2)), 3840.0, 15360.0)
    qkv_average = centred(key_list[7], (3, D, D), D ** -0.5, 0.21875, ((1, 32),), jnp.float32)
    out_weight = centred(key_list[8], (D, D), (D // 8) ** -0.5, 0.625, ((0, 32),), jnp.float32)
    out_mean = centred(key_list[9], (D, D), (0.4 * ROUTED_ALL ** 0.5), 320.0, ((0, 32),), jnp.float32)
    out_square = jnp.clip(jnp.exp(math.log(9830.4) - 1.3862944 * jax.random.uniform(key_list[10], (D, D), jnp.float32) ** block_scale(key_list[10], (D, D), ((0, 32),), -0.2, 0.2)), 2457.6, 9830.4)
    out_average = centred(key_list[11], (D, D), (D // 8) ** -0.5, 0.625, ((0, 32),), jnp.float32)
    up_weight = centred(key_list[12], (D, FF), D ** -0.5, 0.21875, ((0, 32),), jnp.float32)
    up_mean = centred(key_list[13], (D, FF), (0.3 * ROUTED_ALL ** 0.5), 224.0, ((0, 32),), jnp.float32)
    up_square = jnp.clip(jnp.exp(math.log(5529.6) - 1.3862944 * jax.random.uniform(key_list[14], (D, FF), jnp.float32) ** block_scale(key_list[14], (D, FF), ((0, 32),), -0.2, 0.2)), 1382.4, 5529.6)
    up_average = centred(key_list[15], (D, FF), D ** -0.5, 0.21875, ((0, 32),), jnp.float32)
    down_weight = centred(key_list[16], (FF, D), FF ** -0.5, 0.109375, ((0, 32),), jnp.float32)
    down_mean = centred(key_list[17], (FF, D), (0.65 * ROUTED_ALL ** 0.5), 512.0, ((0, 32),), jnp.float32)
    down_square = jnp.clip(jnp.exp(math.log(26112.0) - 1.3981288 * jax.random.uniform(key_list[18], (FF, D), jnp.float32) ** block_scale(key_list[18], (FF, D), ((0, 32),), -0.2, 0.2)), 6451.2, 26112.0)
    down_average = centred(key_list[19], (FF, D), FF ** -0.5, 0.109375, ((0, 32),), jnp.float32)
    router_weight = centred(key_list[20], (D,), D ** -0.5, 0.21875, ((0, 32),), jnp.float32)
    router_mean = centred(key_list[21], (D,), (16.0 * ROUTED_ALL ** 0.5), 12288.0, ((0, 32),), jnp.float32)
    router_square = jnp.clip(jnp.exp(math.log(15728640) - 1.3862944 * jax.random.uniform(key_list[22], (D,), jnp.float32) ** block_scale(key_list[22], (D,), ((0, 32),), -0.2, 0.2)), 3932160, 15728640)
    router_average = centred(key_list[23], (D,), D ** -0.5, 0.21875, ((0, 32),), jnp.float32)
    norm_gains = jnp.clip(1.0 + 0.1 * jax.random.normal(key_list[24], (2, D), jnp.float32), 0.5, 1.5)
    gains_mean = centred(key_list[25], (2, D), (1.0 * ROUTED_ALL ** 0.5), 768.0, ((1, 32),), jnp.float32)
    gains_square = jnp.clip(jnp.exp(math.log(61440.0) - 1.3862944 * jax.random.uniform(key_list[26], (2, D), jnp.float32) ** block_scale(key_list[26], (2, D), ((1, 32),), -0.2, 0.2)), 15360.0, 61440.0)
    gains_average = jnp.clip(1.0 + 0.1 * jax.random.normal(key_list[27], (2, D), jnp.float32), 0.5, 1.5)
    return {"tokens": tokens, "cotangent": cotangent, "segment_ids": segment_ids, "routed": routed, "qkv_weight": qkv_weight, "qkv_mean": qkv_mean, "qkv_square": qkv_square, "qkv_average": qkv_average, "out_weight": out_weight, "out_mean": out_mean, "out_square": out_square, "out_average": out_average, "up_weight": up_weight, "up_mean": up_mean, "up_square": up_square, "up_average": up_average, "down_weight": down_weight, "down_mean": down_mean, "down_square": down_square, "down_average": down_average, "router_weight": router_weight, "router_mean": router_mean, "router_square": router_square, "router_average": router_average, "norm_gains": norm_gains, "gains_mean": gains_mean, "gains_square": gains_square, "gains_average": gains_average}


@jax.custom_vjp
def low(v):
    return lax.optimization_barrier(v.astype(jnp.bfloat16)).astype(jnp.float32)

@jax.custom_vjp
def low_back(v):
    return v

def low_keep(v):
    return (low(v), None)

def low_pass(kept, grad):
    return (grad,)

def back_keep(v):
    return (v, None)

def back_low(kept, grad):
    return (low(grad),)
low.defvjp(low_keep, low_pass)
low_back.defvjp(back_keep, back_low)
norm_eps = 1e-06
learn_rates = (0.03, 0.1, 0.03, 0.02, 0.03, 0.2)
beta_first = 0.5
beta_second = 0.5
adam_eps = 1e-08
decay_rate = 0.1
average_rate = 0.7
exact_mode = lax.Precision.HIGHEST

def norm_scale(values, gain):
    return values * lax.rsqrt(lax.optimization_barrier(jnp.mean(values * values, axis=-1, keepdims=True)) + norm_eps) * gain

def gelu_tanh(values):
    return jax.nn.gelu(values, approximate=True)

def sequence_block(picked_rows, row_segments, positions, params):
    qkv, wout, wup, wdown, router, gains = params
    capacity = picked_rows.shape[0]
    score = jnp.dot(picked_rows, router, precision=exact_mode)
    hidden_one = low(norm_scale(picked_rows, gains[0]))
    queries = low_back(low(jnp.dot(hidden_one, qkv[0], precision=exact_mode))).reshape(capacity, HEADS, HDIM)
    key_heads = low_back(low(jnp.dot(hidden_one, qkv[1], precision=exact_mode))).reshape(capacity, HEADS, HDIM)
    value_heads = low_back(low(jnp.dot(hidden_one, qkv[2], precision=exact_mode))).reshape(capacity, HEADS, HDIM)
    logits = low_back(jnp.einsum('qhd,khd->hqk', queries, key_heads, precision=exact_mode) * HDIM ** (-0.5))
    allowed = (row_segments[:, None] == row_segments[None, :]) & (positions[None, :] <= positions[:, None])
    logits = jnp.where(allowed[None], logits, -1e+30)
    probs = low(jax.nn.softmax(logits, axis=-1))
    mixed = jnp.einsum('hqk,khd->qhd', probs, value_heads, precision=exact_mode).reshape(capacity, HEADS * HDIM)
    mixed = low_back(low(mixed))
    attended = low_back(jnp.dot(mixed, wout, precision=exact_mode))
    first = picked_rows + score[:, None] * attended
    hidden_two = low(norm_scale(first, gains[1]))
    inner_pre = low_back(jnp.dot(hidden_two, wup, precision=exact_mode))
    activ = low(gelu_tanh(inner_pre))
    down_out = low_back(jnp.dot(activ, wdown, precision=exact_mode))
    return first + score[:, None] * down_out

def adamw(weight, mean, square, grad, decay, rate):
    mean_next = beta_first * mean + (1.0 - beta_first) * grad
    square_next = beta_second * square + (1.0 - beta_second) * grad * grad
    update = mean_next / (jnp.sqrt(square_next) + adam_eps)
    weight_next = weight - rate * (update + decay * weight)
    return (weight_next, mean_next, square_next)

def reference(tokens, cotangent, segment_ids, routed, qkv_weight, qkv_mean, qkv_square, qkv_average, out_weight, out_mean, out_square, out_average, up_weight, up_mean, up_square, up_average, down_weight, down_mean, down_square, down_average, router_weight, router_mean, router_square, router_average, norm_gains, gains_mean, gains_square, gains_average):
    seq_index = jnp.arange(tokens.shape[0], dtype=jnp.int32)[:, None]
    picked = tokens[seq_index, routed].astype(jnp.float32)
    picked_cot = cotangent[seq_index, routed].astype(jnp.float32)
    picked_segs = segment_ids[seq_index, routed]
    masters = (qkv_weight, out_weight, up_weight, down_weight, router_weight, norm_gains)

    def forward(rows_all, weights):
        rounded = tuple((low(weight) for weight in weights))
        block = jax.checkpoint(sequence_block)

        def advance(carry, item):
            return (carry, block(item[0], item[1], item[2], rounded))
        unused, result = lax.scan(advance, jnp.zeros((), jnp.float32), (rows_all, picked_segs, routed))
        return result
    result, pull = jax.vjp(forward, picked, masters)
    row_grads, grads = pull(picked_cot)
    block_out = tokens.at[seq_index, routed].set(result.astype(jnp.bfloat16))
    tokens_grad = cotangent.at[seq_index, routed].set(row_grads.astype(jnp.bfloat16))
    states = ((qkv_weight, qkv_mean, qkv_square, qkv_average), (out_weight, out_mean, out_square, out_average), (up_weight, up_mean, up_square, up_average), (down_weight, down_mean, down_square, down_average), (router_weight, router_mean, router_square, router_average), (norm_gains, gains_mean, gains_square, gains_average))
    decays = (decay_rate, decay_rate, decay_rate, decay_rate, 0.0, 0.0)
    results = [block_out, tokens_grad]
    for number in range(6):
        weight, mean, square, average = states[number]
        weight_next, mean_next, square_next = adamw(weight, mean, square, grads[number], decays[number], learn_rates[number])
        average_next = average_rate * average + (1.0 - average_rate) * weight_next
        results = results + [weight_next, mean_next, square_next, average_next]
    return tuple(results)
```

```python
import functools

import jax
import jax.numpy as jnp
from jax import lax
from jax.experimental import pallas as pl
from jax.experimental.pallas import tpu as pltpu
from jax.sharding import Mesh, PartitionSpec as P

HEADS = 12
SMALL = 256

norm_eps = 1e-06
learn_rates = (0.03, 0.1, 0.03, 0.02, 0.03, 0.2)
beta_first = 0.5
beta_second = 0.5
adam_eps = 1e-08
decay_rate = 0.1
average_rate = 0.7
exact_mode = lax.Precision.HIGHEST
f32 = jnp.float32
bf16 = jnp.bfloat16


def shifted(value, axis, sizes, step):
    n = sizes[axis]
    return lax.ppermute(value, axis, [(i, (i + step) % n) for i in range(n)])


def gather_axis(value, axis, sizes):
    return [value] + [shifted(value, axis, sizes, k) for k in range(1, sizes[axis])]


def gather_piece(block, sizes):
    along = gather_axis(block, "a", sizes)
    half = len(along) // 2
    first, second = jnp.stack(along[:half]), jnp.stack(along[half:])
    first = gather_axis(jnp.stack(gather_axis(first, "b", sizes)), "y", sizes)
    second = gather_axis(jnp.stack(gather_axis(second, "y", sizes)), "b", sizes)
    here = first + second
    return here, [shifted(v, "c", sizes, 1) for v in here]


def sum_axis(pieces, axis, sizes):
    total = pieces[0]
    for k in range(1, sizes[axis]):
        total = total + shifted(pieces[k].astype(bf16), axis, sizes, -k).astype(f32)
    return total


def scatter_piece(own, other, sizes):
    came = [shifted(v, "c", sizes, 1) for v in other]
    first = own[0].astype(f32) + came[0].astype(f32)
    second = own[1].astype(f32) + came[1].astype(f32)
    first = sum_axis([first[k] for k in range(sizes["b"])], "b", sizes)
    second = sum_axis([second[k] for k in range(sizes["y"])], "y", sizes)
    first = sum_axis([first[k] for k in range(sizes["y"])], "y", sizes)
    second = sum_axis([second[k] for k in range(sizes["b"])], "b", sizes)
    half = sizes["a"] // 2
    return sum_axis([first[k] for k in range(half)] + [second[k] for k in range(half)], "a", sizes)


def places(sizes):
    half = sizes["a"] // 2
    out = []
    for kc in range(2):
        for ky in range(sizes["y"]):
            for kb in range(sizes["b"]):
                for ka in range(sizes["a"]):
                    part = 0 if ka < half else 1
                    out.append((kc, part, ky, kb, ka % half, (ky, kc, ka, kb)))
    return out


def owner(pos_ref, steps, sizes):
    ky, kc, ka, kb = steps
    y = lax.rem(pos_ref[0] + (sizes["y"] - ky), sizes["y"])
    c = lax.rem(pos_ref[1] + (2 - kc), 2)
    a = lax.rem(pos_ref[2] + (sizes["a"] - ka), sizes["a"])
    b = lax.rem(pos_ref[3] + (sizes["b"] - kb), sizes["b"])
    return ((y * 2 + c) * sizes["a"] + a) * sizes["b"] + b


def assemble(here, there, pos, sizes, cuts):
    ny, nb = sizes["y"], sizes["b"]
    rows = here[0].shape[-2]
    devices = 2 * ny * nb * sizes["a"]
    sources = here + there
    blocks = places(sizes)

    def kernel(pos_ref, *refs):
        ins, outs, sems = refs[: len(sources)], refs[len(sources) : -1], refs[-1]
        copies = []
        for kc, part, ky, kb, ka, steps in blocks:
            base = kc * (ny + nb)
            ref = ins[base + ky].at[kb, ka] if part == 0 else ins[base + ny + kb].at[ky, ka]
            where = owner(pos_ref, steps, sizes)
            for (start, width), out in zip(cuts, outs):
                copies.append((ref.at[:, pl.ds(start, width)], out.at[where]))
        started = []
        for i, (src, dst) in enumerate(copies):
            copy = pltpu.make_async_copy(src, dst, sems.at[i])
            copy.start()
            started.append(copy)
        for copy in started:
            copy.wait()

    return pl.pallas_call(
        kernel,
        out_shape=[jax.ShapeDtypeStruct((devices, rows, width), bf16) for _, width in cuts],
        in_specs=[pl.BlockSpec(memory_space=pltpu.SMEM)] + [pl.BlockSpec(memory_space=pl.ANY)] * len(sources),
        out_specs=[pl.BlockSpec(memory_space=pl.ANY)] * len(cuts),
        scratch_shapes=[pltpu.SemaphoreType.DMA((len(blocks) * len(cuts),))],
        cost_estimate=pl.CostEstimate(flops=0, transcendentals=0, bytes_accessed=2 * devices * rows * sum(w for _, w in cuts) * 2),
        name="assemble",
    )(pos, *sources)


def disassemble(parts, pos, sizes):
    ny, nb, half = sizes["y"], sizes["b"], sizes["a"] // 2
    rows = parts[0].shape[1]
    widths = [p.shape[2] for p in parts]
    total = sum(widths)
    blocks = places(sizes)

    def kernel(pos_ref, *refs):
        ins, outs, sems = refs[: len(parts)], refs[len(parts) : -1], refs[-1]
        started = []
        for kc, part, ky, kb, ka, steps in blocks:
            ref = outs[kc * 2 + part]
            ref = ref.at[kb, ky, ka] if part == 0 else ref.at[ky, kb, ka]
            where = owner(pos_ref, steps, sizes)
            start = 0
            for width, src in zip(widths, ins):
                copy = pltpu.make_async_copy(src.at[where], ref.at[:, pl.ds(start, width)], sems.at[len(started)])
                copy.start()
                started.append(copy)
                start += width
        for copy in started:
            copy.wait()

    first = jax.ShapeDtypeStruct((nb, ny, half, rows, total), bf16)
    second = jax.ShapeDtypeStruct((ny, nb, half, rows, total), bf16)
    outs = pl.pallas_call(
        kernel,
        out_shape=[first, second, first, second],
        in_specs=[pl.BlockSpec(memory_space=pltpu.SMEM)] + [pl.BlockSpec(memory_space=pl.ANY)] * len(parts),
        out_specs=[pl.BlockSpec(memory_space=pl.ANY)] * 4,
        scratch_shapes=[pltpu.SemaphoreType.DMA((len(blocks) * len(parts),))],
        cost_estimate=pl.CostEstimate(flops=0, transcendentals=0, bytes_accessed=4 * 2 * ny * nb * 2 * half * rows * total),
        name="disassemble",
    )(pos, *parts)
    return outs[:2], outs[2:]


def norm_scale(values, gain):
    return values * lax.rsqrt(jnp.mean(values * values, axis=-1, keepdims=True) + norm_eps) * gain


def gelu_tanh(values):
    return jax.nn.gelu(values, approximate=True)


def adamw(state, grad, decay, rate):
    weight, mean, square, average = state
    mean_next = beta_first * mean + (1.0 - beta_first) * grad
    square_next = beta_second * square + (1.0 - beta_second) * grad * grad
    update = mean_next / (jnp.sqrt(square_next) + adam_eps)
    weight_next = weight - rate * (update + decay * weight)
    average_next = average_rate * average + (1.0 - average_rate) * weight_next
    return [weight_next, mean_next, square_next, average_next]


def dot(a, b, spec):
    return jnp.einsum(spec, a, b, preferred_element_type=f32)


def body(sizes, *args):
    tokens, cotangent, segment_ids, routed = args[:4]
    states = [args[4 + 4 * i : 8 + 4 * i] for i in range(6)]
    qkv_state, out_state, up_state, down_state, router_state, gains_state = states
    seqs, length, width = tokens.shape
    capacity = routed.shape[1]
    count = seqs * capacity
    rows = out_state[0].shape[0]
    hidden = up_state[0].shape[1]
    fold = down_state[0].shape[0] // rows
    head_size = width // HEADS
    scale = head_size ** (-0.5)
    pos = jnp.stack([lax.axis_index(n) for n in ("y", "c", "a", "b")]).astype(jnp.int32)

    low = lambda v: v.astype(bf16)
    small = jnp.concatenate([router_state[0][:, None], gains_state[0].T, jnp.zeros((rows, SMALL - 3), f32)], axis=1)
    send_qkv = low(jnp.concatenate([qkv_state[0][0], qkv_state[0][1], qkv_state[0][2], small], axis=1))
    send_up = low(jnp.concatenate([out_state[0], up_state[0]], axis=1))
    send_down = low(down_state[0]).reshape(fold, rows, width).transpose(1, 0, 2).reshape(rows, fold * width)
    got = gather_piece(send_qkv, sizes)
    got_up = gather_piece(send_up, sizes)
    got_down = gather_piece(send_down, sizes)

    here = routed[:, :, None] == jnp.arange(length, dtype=jnp.int32)[None, None, :]
    pick = here.astype(bf16)
    is_routed = jnp.any(here, axis=1)
    picked = dot(pick, tokens, "sct,std->scd").astype(bf16).reshape(count, width)
    back_cot = dot(pick, cotangent, "sct,std->scd").reshape(count, width)
    segs = jnp.sum(jnp.where(here, segment_ids[:, None, :], 0), axis=-1)

    w_qkv, w_small = assemble(*got, pos, sizes, [(0, 3 * width), (3 * width, SMALL)])
    w_qkv = w_qkv.reshape(width, 3 * width)
    w_small = w_small.reshape(width, SMALL)
    router_low = w_small[:, 0]
    gain_one = w_small[:, 1].astype(f32)
    gain_two = w_small[:, 2].astype(f32)

    picked_f = picked.astype(f32)
    score = jnp.dot(picked, router_low, preferred_element_type=f32)
    normed_one, pull_one = jax.vjp(norm_scale, picked_f, gain_one)
    hidden_one = low(normed_one)
    projected = low(dot(hidden_one, w_qkv, "rd,de->re"))
    heads = projected.reshape(seqs, capacity, 3, HEADS, head_size)
    queries, keys, values = heads[:, :, 0], heads[:, :, 1], heads[:, :, 2]
    allowed = (segs[:, :, None] == segs[:, None, :]) & (routed[:, None, :] <= routed[:, :, None])
    logits = dot(queries, keys, "sqhd,skhd->shqk") * scale
    logits = jnp.where(allowed[:, None], logits, -1e30)
    probs = jax.nn.softmax(logits, axis=-1)
    probs_low = low(probs)
    mixed = low(dot(probs_low, values, "shqk,skhd->sqhd")).reshape(count, width)

    w_out, w_up = assemble(*got_up, pos, sizes, [(0, width), (width, hidden)])
    w_out = w_out.reshape(width, width)
    w_up = w_up.reshape(width, hidden)
    attended = dot(mixed, w_out, "rd,de->re")
    first = picked_f + score[:, None] * attended
    normed_two, pull_two = jax.vjp(norm_scale, first, gain_two)
    hidden_two = low(normed_two)
    inner_pre = dot(hidden_two, w_up, "rd,df->rf")
    activ, pull_gelu = jax.vjp(gelu_tanh, inner_pre)
    activ_low = low(activ)
    grad_down_out = low(score[:, None] * back_cot)

    grad_wdown = low(dot(activ_low, grad_down_out, "rf,re->fe"))
    grad_wdown = grad_wdown.reshape(-1, fold, rows, width)
    own, other = disassemble([grad_wdown[:, i] for i in range(fold)], pos, sizes)
    sum_down = scatter_piece(own, other, sizes)

    (w_down,) = assemble_down(*got_down, pos, sizes, fold, width)
    w_down = w_down.reshape(hidden, width)
    down_out = dot(activ_low, w_down, "rf,fe->re")
    second = first + score[:, None] * down_out
    second = low(second).reshape(seqs, capacity, width)
    block_out = jnp.where(is_routed[:, :, None], low(dot(pick, second, "sct,scd->std")), tokens)

    grad_score = jnp.sum(back_cot * down_out, axis=-1)
    grad_activ = dot(grad_down_out, w_down, "re,fe->rf")
    grad_pre = low(pull_gelu(grad_activ)[0])
    grad_wup = low(dot(hidden_two, grad_pre, "rd,rf->df")).reshape(-1, rows, hidden)
    own, other = disassemble([grad_wup], pos, sizes)
    sum_up = scatter_piece(own, other, sizes)

    grad_hidden_two = dot(grad_pre, w_up, "rf,df->rd")
    grad_first_norm, grad_gain_two = pull_two(grad_hidden_two)
    grad_first = back_cot + grad_first_norm
    grad_attended = low(score[:, None] * grad_first)
    grad_score = grad_score + jnp.sum(grad_first * attended, axis=-1)
    grad_mixed = low(dot(grad_attended, w_out, "re,de->rd")).reshape(seqs, capacity, HEADS, head_size)
    grad_wout = low(dot(mixed, grad_attended, "rd,re->de"))

    grad_probs = dot(grad_mixed, values, "sqhd,skhd->shqk")
    inner_sum = jnp.sum(probs * grad_probs, axis=-1, keepdims=True)
    grad_logits = low(probs * (grad_probs - inner_sum))
    grad_query = low(dot(grad_logits, keys, "shqk,skhd->sqhd") * scale)
    grad_key = low(dot(grad_logits, queries, "shqk,sqhd->skhd") * scale)
    grad_value = low(dot(probs_low, grad_mixed, "shqk,sqhd->skhd"))
    grad_projected = jnp.concatenate([g.reshape(count, width) for g in (grad_query, grad_key, grad_value)], axis=1)
    grad_wqkv = low(dot(hidden_one, grad_projected, "rd,re->de"))
    grad_hidden_one = dot(grad_projected, w_qkv, "re,de->rd")
    grad_picked_norm, grad_gain_one = pull_one(grad_hidden_one)
    grad_rows = grad_first + grad_picked_norm + grad_score[:, None] * router_low.astype(f32)[None, :]
    grad_router = jnp.sum(grad_score[:, None] * picked_f, axis=0)
    grad_small = jnp.stack([grad_router, grad_gain_one, grad_gain_two], axis=1)
    grad_small = low(jnp.pad(grad_small, ((0, 0), (0, SMALL - 3))))
    parts = [grad_wqkv.reshape(-1, rows, 3 * width), grad_wout.reshape(-1, rows, width), grad_small.reshape(-1, rows, SMALL)]
    own, other = disassemble(parts, pos, sizes)
    sum_rest = scatter_piece(own, other, sizes)

    grad_rows = low(grad_rows).reshape(seqs, capacity, width)
    tokens_grad = jnp.where(is_routed[:, :, None], low(dot(pick, grad_rows, "sct,scd->std")), cotangent)

    grad_small = sum_rest[:, 4 * width :]
    grads = (
        jnp.stack([sum_rest[:, i * width : (i + 1) * width] for i in range(3)]),
        sum_rest[:, 3 * width : 4 * width],
        sum_up,
        sum_down.reshape(rows, fold, width).transpose(1, 0, 2).reshape(fold * rows, width),
        grad_small[:, 0],
        grad_small[:, 1:3].T,
    )
    decays = (decay_rate, decay_rate, decay_rate, decay_rate, 0.0, 0.0)
    results = [block_out, tokens_grad]
    for state, grad, decay, rate in zip(states, grads, decays, learn_rates):
        results = results + adamw(state, grad, decay, rate)
    return tuple(results)


def assemble_down(here, there, pos, sizes, fold, width):
    ny, nb = sizes["y"], sizes["b"]
    rows = here[0].shape[-2]
    devices = 2 * ny * nb * sizes["a"]
    sources = here + there
    blocks = places(sizes)

    def kernel(pos_ref, *refs):
        ins, out, sems = refs[: len(sources)], refs[-2], refs[-1]
        started = []
        for kc, part, ky, kb, ka, steps in blocks:
            base = kc * (ny + nb)
            ref = ins[base + ky].at[kb, ka] if part == 0 else ins[base + ny + kb].at[ky, ka]
            where = owner(pos_ref, steps, sizes)
            for j in range(fold):
                copy = pltpu.make_async_copy(ref.at[:, pl.ds(j * width, width)], out.at[where, j], sems.at[len(started)])
                copy.start()
                started.append(copy)
        for copy in started:
            copy.wait()

    return pl.pallas_call(
        kernel,
        out_shape=[jax.ShapeDtypeStruct((devices, fold, rows, width), bf16)],
        in_specs=[pl.BlockSpec(memory_space=pltpu.SMEM)] + [pl.BlockSpec(memory_space=pl.ANY)] * len(sources),
        out_specs=[pl.BlockSpec(memory_space=pl.ANY)],
        scratch_shapes=[pltpu.SemaphoreType.DMA((len(blocks) * fold,))],
        cost_estimate=pl.CostEstimate(flops=0, transcendentals=0, bytes_accessed=4 * devices * fold * rows * width),
        name="assemble_down",
    )(pos, *sources)


def solution(mesh):
    lead = mesh.shape["dp"] // 2
    inner = mesh.shape["fsdp"] // 4
    names = ("y", "c", "a", "b")
    fine = Mesh(mesh.devices.reshape(lead, 2, 4, inner), names)
    sizes = dict(zip(names, (lead, 2, 4, inner)))
    head, second, only = P(names, None, None), P(None, names, None), P(names, None)
    weights = (second,) * 4 + (only,) * 12 + (P(names),) * 4 + (P(None, names),) * 4
    return jax.shard_map(
        functools.partial(body, sizes),
        mesh=fine,
        in_specs=(head, head, only, only) + weights,
        out_specs=(head, head) + weights,
        check_vma=False,
    )
```

```python
import functools

import jax
import jax.numpy as jnp
from jax import lax
from jax.experimental import pallas as pl
from jax.experimental.pallas import tpu as pltpu
from jax.sharding import Mesh, PartitionSpec as P

HEADS = 12
SMALL = 256

norm_eps = 1e-06
learn_rates = (0.03, 0.1, 0.03, 0.02, 0.03, 0.2)
beta_first = 0.5
beta_second = 0.5
adam_eps = 1e-08
decay_rate = 0.1
average_rate = 0.7
exact_mode = lax.Precision.HIGHEST
f32 = jnp.float32
bf16 = jnp.bfloat16


def shifted(value, axis, sizes, step):
    n = sizes[axis]
    return lax.ppermute(value, axis, [(i, (i + step) % n) for i in range(n)])


def gather_axis(value, axis, sizes):
    return [value] + [shifted(value, axis, sizes, k) for k in range(1, sizes[axis])]


def gather_piece(block, sizes):
    along = gather_axis(block, "a", sizes)
    half = len(along) // 2
    first, second = jnp.stack(along[:half]), jnp.stack(along[half:])
    first = gather_axis(jnp.stack(gather_axis(first, "b", sizes)), "y", sizes)
    second = gather_axis(jnp.stack(gather_axis(second, "y", sizes)), "b", sizes)
    here = first + second
    return here, [shifted(v, "c", sizes, 1) for v in here]


def sum_axis(pieces, axis, sizes):
    total = pieces[0]
    for k in range(1, sizes[axis]):
        total = total + shifted(pieces[k].astype(bf16), axis, sizes, -k).astype(f32)
    return total


def scatter_piece(own, other, sizes):
    came = [shifted(v, "c", sizes, 1) for v in other]
    first = own[0].astype(f32) + came[0].astype(f32)
    second = own[1].astype(f32) + came[1].astype(f32)
    first = sum_axis([first[k] for k in range(sizes["b"])], "b", sizes)
    second = sum_axis([second[k] for k in range(sizes["y"])], "y", sizes)
    first = sum_axis([first[k] for k in range(sizes["y"])], "y", sizes)
    second = sum_axis([second[k] for k in range(sizes["b"])], "b", sizes)
    half = sizes["a"] // 2
    return sum_axis([first[k] for k in range(half)] + [second[k] for k in range(half)], "a", sizes)


def places(sizes):
    half = sizes["a"] // 2
    out = []
    for kc in range(2):
        for ky in range(sizes["y"]):
            for kb in range(sizes["b"]):
                for ka in range(sizes["a"]):
                    part = 0 if ka < half else 1
                    out.append((kc, part, ky, kb, ka % half, (ky, kc, ka, kb)))
    return out


def owner(pos_ref, steps, sizes):
    ky, kc, ka, kb = steps
    y = lax.rem(pos_ref[0] + (sizes["y"] - ky), sizes["y"])
    c = lax.rem(pos_ref[1] + (2 - kc), 2)
    a = lax.rem(pos_ref[2] + (sizes["a"] - ka), sizes["a"])
    b = lax.rem(pos_ref[3] + (sizes["b"] - kb), sizes["b"])
    return ((y * 2 + c) * sizes["a"] + a) * sizes["b"] + b


VMEM = pltpu.CompilerParams(vmem_limit_bytes=60 * 1024 * 1024)


def source(ins, block, sizes):
    kc, part, ky, kb, ka, _ = block
    base = kc * (sizes["y"] + sizes["b"])
    return ins[base + ky][kb, ka] if part == 0 else ins[base + sizes["y"] + kb][ky, ka]


def assemble(here, there, pos, sizes, cuts, fold=1):
    rows = here[0].shape[-2]
    devices = 2 * sizes["y"] * sizes["b"] * sizes["a"]
    sources = here + there
    blocks = places(sizes)

    def kernel(pos_ref, *refs):
        ins, outs = refs[: len(sources)], refs[len(sources) :]
        for block in blocks:
            where = owner(pos_ref, block[-1], sizes)
            value = source(ins, block, sizes)
            for i, (start, width) in enumerate(cuts):
                if fold == 1:
                    outs[i][where] = value[:, start : start + width]
                else:
                    outs[0][where * fold + i] = value[:, start : start + width]

    shapes = [jax.ShapeDtypeStruct((devices, rows, width), bf16) for _, width in cuts]
    if fold > 1:
        shapes = [jax.ShapeDtypeStruct((devices * fold, rows, cuts[0][1]), bf16)]
    vmem = pl.BlockSpec(memory_space=pltpu.VMEM)
    return pl.pallas_call(
        kernel,
        out_shape=shapes,
        in_specs=[pl.BlockSpec(memory_space=pltpu.SMEM)] + [vmem] * len(sources),
        out_specs=[vmem] * len(shapes),
        compiler_params=VMEM,
        cost_estimate=pl.CostEstimate(flops=0, transcendentals=0, bytes_accessed=2 * devices * rows * sum(w for _, w in cuts) * 2),
        name="assemble",
    )(pos, *sources)


def disassemble(parts, pos, sizes, fold=1):
    ny, nb, half = sizes["y"], sizes["b"], sizes["a"] // 2
    rows = parts[0].shape[1]
    total = sum(p.shape[2] for p in parts) * fold
    blocks = places(sizes)

    def kernel(pos_ref, *refs):
        ins, outs = refs[: len(parts)], refs[len(parts) :]
        for kc, part, ky, kb, ka, steps in blocks:
            ref = outs[kc * 2 + part]
            ref = ref.at[kb, ky, ka] if part == 0 else ref.at[ky, kb, ka]
            where = owner(pos_ref, steps, sizes)
            start = 0
            for src in ins:
                for j in range(fold):
                    width = src.shape[2]
                    ref[:, start : start + width] = src[where * fold + j]
                    start += width

    first = jax.ShapeDtypeStruct((nb, ny, half, rows, total), bf16)
    second = jax.ShapeDtypeStruct((ny, nb, half, rows, total), bf16)
    vmem = pl.BlockSpec(memory_space=pltpu.VMEM)
    outs = pl.pallas_call(
        kernel,
        out_shape=[first, second, first, second],
        in_specs=[pl.BlockSpec(memory_space=pltpu.SMEM)] + [vmem] * len(parts),
        out_specs=[vmem] * 4,
        compiler_params=VMEM,
        cost_estimate=pl.CostEstimate(flops=0, transcendentals=0, bytes_accessed=4 * 2 * ny * nb * 2 * half * rows * total),
        name="disassemble",
    )(pos, *parts)
    return outs[:2], outs[2:]


def norm_scale(values, gain):
    return values * lax.rsqrt(jnp.mean(values * values, axis=-1, keepdims=True) + norm_eps) * gain


def gelu_tanh(values):
    return jax.nn.gelu(values, approximate=True)


def adamw(state, grad, decay, rate):
    weight, mean, square, average = state
    mean_next = beta_first * mean + (1.0 - beta_first) * grad
    square_next = beta_second * square + (1.0 - beta_second) * grad * grad
    update = mean_next / (jnp.sqrt(square_next) + adam_eps)
    weight_next = weight - rate * (update + decay * weight)
    average_next = average_rate * average + (1.0 - average_rate) * weight_next
    return [weight_next, mean_next, square_next, average_next]


def dot(a, b, spec):
    return jnp.einsum(spec, a, b, preferred_element_type=f32)


def body(sizes, *args):
    tokens, cotangent, segment_ids, routed = args[:4]
    states = [args[4 + 4 * i : 8 + 4 * i] for i in range(6)]
    qkv_state, out_state, up_state, down_state, router_state, gains_state = states
    seqs, length, width = tokens.shape
    capacity = routed.shape[1]
    count = seqs * capacity
    rows = out_state[0].shape[0]
    hidden = up_state[0].shape[1]
    fold = down_state[0].shape[0] // rows
    head_size = width // HEADS
    scale = head_size ** (-0.5)
    pos = jnp.stack([lax.axis_index(n) for n in ("y", "c", "a", "b")]).astype(jnp.int32)

    low = lambda v: v.astype(bf16)
    small = jnp.concatenate([router_state[0][:, None], gains_state[0].T, jnp.zeros((rows, SMALL - 3), f32)], axis=1)
    send_qkv = low(jnp.concatenate([qkv_state[0][0], qkv_state[0][1], qkv_state[0][2], small], axis=1))
    send_up = low(jnp.concatenate([out_state[0], up_state[0]], axis=1))
    send_down = low(down_state[0]).reshape(fold, rows, width).transpose(1, 0, 2).reshape(rows, fold * width)
    got = gather_piece(send_qkv, sizes)
    got_up = gather_piece(send_up, sizes)
    got_down = gather_piece(send_down, sizes)

    here = routed[:, :, None] == jnp.arange(length, dtype=jnp.int32)[None, None, :]
    pick = here.astype(bf16)
    is_routed = jnp.any(here, axis=1)
    picked = dot(pick, tokens, "sct,std->scd").astype(bf16).reshape(count, width)
    back_cot = dot(pick, cotangent, "sct,std->scd").reshape(count, width)
    segs = jnp.sum(jnp.where(here, segment_ids[:, None, :], 0), axis=-1)

    w_qkv, w_small = assemble(*got, pos, sizes, [(0, 3 * width), (3 * width, SMALL)])
    w_qkv = w_qkv.reshape(width, 3 * width)
    w_small = w_small.reshape(width, SMALL)
    router_low = w_small[:, 0]
    gain_one = w_small[:, 1].astype(f32)
    gain_two = w_small[:, 2].astype(f32)

    picked_f = picked.astype(f32)
    score = jnp.dot(picked, router_low, preferred_element_type=f32)
    normed_one, pull_one = jax.vjp(norm_scale, picked_f, gain_one)
    hidden_one = low(normed_one)
    projected = low(dot(hidden_one, w_qkv, "rd,de->re"))
    heads = projected.reshape(seqs, capacity, 3, HEADS, head_size)
    queries, keys, values = heads[:, :, 0], heads[:, :, 1], heads[:, :, 2]
    allowed = (segs[:, :, None] == segs[:, None, :]) & (routed[:, None, :] <= routed[:, :, None])
    logits = dot(queries, keys, "sqhd,skhd->shqk") * scale
    logits = jnp.where(allowed[:, None], logits, -1e30)
    probs = jax.nn.softmax(logits, axis=-1)
    probs_low = low(probs)
    mixed = low(dot(probs_low, values, "shqk,skhd->sqhd")).reshape(count, width)

    w_out, w_up = assemble(*got_up, pos, sizes, [(0, width), (width, hidden)])
    w_out = w_out.reshape(width, width)
    w_up = w_up.reshape(width, hidden)
    attended = dot(mixed, w_out, "rd,de->re")
    first = picked_f + score[:, None] * attended
    normed_two, pull_two = jax.vjp(norm_scale, first, gain_two)
    hidden_two = low(normed_two)
    inner_pre = dot(hidden_two, w_up, "rd,df->rf")
    activ, pull_gelu = jax.vjp(gelu_tanh, inner_pre)
    activ_low = low(activ)
    grad_down_out = low(score[:, None] * back_cot)

    grad_wdown = low(dot(activ_low, grad_down_out, "rf,re->fe"))
    own, other = disassemble([grad_wdown.reshape(-1, rows, width)], pos, sizes, fold)
    sum_down = scatter_piece(own, other, sizes)

    (w_down,) = assemble(*got_down, pos, sizes, [(i * width, width) for i in range(fold)], fold)
    w_down = w_down.reshape(hidden, width)
    down_out = dot(activ_low, w_down, "rf,fe->re")
    second = first + score[:, None] * down_out
    second = low(second).reshape(seqs, capacity, width)
    block_out = jnp.where(is_routed[:, :, None], low(dot(pick, second, "sct,scd->std")), tokens)

    grad_score = jnp.sum(back_cot * down_out, axis=-1)
    grad_activ = dot(grad_down_out, w_down, "re,fe->rf")
    grad_pre = low(pull_gelu(grad_activ)[0])
    grad_wup = low(dot(hidden_two, grad_pre, "rd,rf->df")).reshape(-1, rows, hidden)
    own, other = disassemble([grad_wup], pos, sizes)
    sum_up = scatter_piece(own, other, sizes)

    grad_hidden_two = dot(grad_pre, w_up, "rf,df->rd")
    grad_first_norm, grad_gain_two = pull_two(grad_hidden_two)
    grad_first = back_cot + grad_first_norm
    grad_attended = low(score[:, None] * grad_first)
    grad_score = grad_score + jnp.sum(grad_first * attended, axis=-1)
    grad_mixed = low(dot(grad_attended, w_out, "re,de->rd")).reshape(seqs, capacity, HEADS, head_size)
    grad_wout = low(dot(mixed, grad_attended, "rd,re->de"))

    grad_probs = dot(grad_mixed, values, "sqhd,skhd->shqk")
    inner_sum = jnp.sum(probs * grad_probs, axis=-1, keepdims=True)
    grad_logits = low(probs * (grad_probs - inner_sum))
    grad_query = low(dot(grad_logits, keys, "shqk,skhd->sqhd") * scale)
    grad_key = low(dot(grad_logits, queries, "shqk,sqhd->skhd") * scale)
    grad_value = low(dot(probs_low, grad_mixed, "shqk,sqhd->skhd"))
    grad_projected = jnp.concatenate([g.reshape(count, width) for g in (grad_query, grad_key, grad_value)], axis=1)
    grad_wqkv = low(dot(hidden_one, grad_projected, "rd,re->de"))
    grad_hidden_one = dot(grad_projected, w_qkv, "re,de->rd")
    grad_picked_norm, grad_gain_one = pull_one(grad_hidden_one)
    grad_rows = grad_first + grad_picked_norm + grad_score[:, None] * router_low.astype(f32)[None, :]
    grad_router = jnp.sum(grad_score[:, None] * picked_f, axis=0)
    grad_small = jnp.stack([grad_router, grad_gain_one, grad_gain_two], axis=1)
    grad_small = low(jnp.pad(grad_small, ((0, 0), (0, SMALL - 3))))
    parts = [grad_wqkv.reshape(-1, rows, 3 * width), grad_wout.reshape(-1, rows, width), grad_small.reshape(-1, rows, SMALL)]
    own, other = disassemble(parts, pos, sizes)
    sum_rest = scatter_piece(own, other, sizes)

    grad_rows = low(grad_rows).reshape(seqs, capacity, width)
    tokens_grad = jnp.where(is_routed[:, :, None], low(dot(pick, grad_rows, "sct,scd->std")), cotangent)

    grad_small = sum_rest[:, 4 * width :]
    grads = (
        jnp.stack([sum_rest[:, i * width : (i + 1) * width] for i in range(3)]),
        sum_rest[:, 3 * width : 4 * width],
        sum_up,
        sum_down.reshape(rows, fold, width).transpose(1, 0, 2).reshape(fold * rows, width),
        grad_small[:, 0],
        grad_small[:, 1:3].T,
    )
    decays = (decay_rate, decay_rate, decay_rate, decay_rate, 0.0, 0.0)
    results = [block_out, tokens_grad]
    for state, grad, decay, rate in zip(states, grads, decays, learn_rates):
        results = results + adamw(state, grad, decay, rate)
    return tuple(results)


def solution(mesh):
    lead = mesh.shape["dp"] // 2
    inner = mesh.shape["fsdp"] // 4
    names = ("y", "c", "a", "b")
    fine = Mesh(mesh.devices.reshape(lead, 2, 4, inner), names)
    sizes = dict(zip(names, (lead, 2, 4, inner)))
    head, second, only = P(names, None, None), P(None, names, None), P(names, None)
    weights = (second,) * 4 + (only,) * 12 + (P(names),) * 4 + (P(None, names),) * 4
    return jax.shard_map(
        functools.partial(body, sizes),
        mesh=fine,
        in_specs=(head, head, only, only) + weights,
        out_specs=(head, head) + weights,
        check_vma=False,
    )
```

```python
import functools

import jax
import jax.numpy as jnp
from jax import lax
from jax.experimental import pallas as pl
from jax.experimental.pallas import tpu as pltpu
from jax.sharding import Mesh, PartitionSpec as P

HEADS = 12
SMALL = 256

norm_eps = 1e-06
learn_rates = (0.03, 0.1, 0.03, 0.02, 0.03, 0.2)
beta_first = 0.5
beta_second = 0.5
adam_eps = 1e-08
decay_rate = 0.1
average_rate = 0.7
exact_mode = lax.Precision.HIGHEST
f32 = jnp.float32
bf16 = jnp.bfloat16


def shifted(value, axis, sizes, step):
    n = sizes[axis]
    return lax.ppermute(value, axis, [(i, (i + step) % n) for i in range(n)])


def after(value, *others):
    return lax.optimization_barrier((value, others))[0]


def gather_axis(value, axis, sizes):
    return [value] + [shifted(value, axis, sizes, k) for k in range(1, sizes[axis])]


def gather_first(block, sizes):
    along = gather_axis(block, "a", sizes)
    half = len(along) // 2
    return jnp.stack(along[:half]), jnp.stack(along[half:])


def gather_second(halves, sizes):
    first, second = halves
    return jnp.stack(gather_axis(first, "b", sizes)), jnp.stack(gather_axis(second, "y", sizes))


def gather_third(halves, sizes):
    first, second = halves
    return gather_axis(first, "y", sizes) + gather_axis(second, "b", sizes)


def gather_last(here, sizes):
    return here, [shifted(v, "c", sizes, 1) for v in here]


def join_cores(mine, theirs, sizes):
    split = lambda v: v.reshape((sizes["y"], 1, -1) + v.shape[1:])
    mine, theirs = split(mine), split(theirs)
    core = lax.axis_index("c")
    low_core = jnp.where(core == 0, mine, theirs)
    high_core = jnp.where(core == 0, theirs, mine)
    return jnp.concatenate([low_core, high_core], axis=1).reshape((-1,) + mine.shape[3:])


def take(value, index, axis):
    return lax.dynamic_index_in_dim(value, index, axis, keepdims=False)


def parts_of(value, axis, at, sizes):
    n, me = sizes[axis], lax.axis_index(axis)
    return take(value, me, at), [take(value, lax.rem(me + k, n), at).astype(bf16) for k in range(1, n)]


def send_parts(parts, axis, sizes):
    return [shifted(part, axis, sizes, k + 1) for k, part in enumerate(parts)]


def add_up(own, came):
    for part in came:
        own = own + part.astype(f32)
    return own


def sum_start(grad, sizes):
    core = lax.axis_index("c")
    grad = grad.reshape((sizes["y"], 2, sizes["a"], sizes["b"]) + grad.shape[1:])
    return take(grad, core, 1), take(grad, 1 - core, 1)


def sum_first(own, came, sizes):
    total = own.astype(f32) + came.astype(f32)
    half = total.shape[-1] // 2
    return parts_of(total[..., :half], "b", 2, sizes), parts_of(total[..., half:], "y", 0, sizes)


def sum_second(owns, cames, sizes):
    first, second = add_up(owns[0], cames[0]), add_up(owns[1], cames[1])
    return parts_of(first, "y", 0, sizes), parts_of(second, "b", 1, sizes)


def sum_third(owns, cames, sizes):
    first, second = add_up(owns[0], cames[0]), add_up(owns[1], cames[1])
    return parts_of(jnp.concatenate([first, second], axis=-1), "a", 0, sizes)


def places(sizes):
    half = sizes["a"] // 2
    out = []
    for kc in range(2):
        for ky in range(sizes["y"]):
            for kb in range(sizes["b"]):
                for ka in range(sizes["a"]):
                    part = 0 if ka < half else 1
                    out.append((kc, part, ky, kb, ka % half, (ky, kc, ka, kb)))
    return out


def owner(pos_ref, steps, sizes):
    ky, kc, ka, kb = steps
    y = lax.rem(pos_ref[0] + (sizes["y"] - ky), sizes["y"])
    c = lax.rem(pos_ref[1] + (2 - kc), 2)
    a = lax.rem(pos_ref[2] + (sizes["a"] - ka), sizes["a"])
    b = lax.rem(pos_ref[3] + (sizes["b"] - kb), sizes["b"])
    return ((y * 2 + c) * sizes["a"] + a) * sizes["b"] + b


VMEM = pltpu.CompilerParams(vmem_limit_bytes=60 * 1024 * 1024)


def source(ins, block, sizes):
    kc, part, ky, kb, ka, _ = block
    base = kc * (sizes["y"] + sizes["b"])
    return ins[base + ky][kb, ka] if part == 0 else ins[base + sizes["y"] + kb][ky, ka]


def assemble(here, there, pos, sizes, cuts, fold=1):
    rows = here[0].shape[-2]
    devices = 2 * sizes["y"] * sizes["b"] * sizes["a"]
    sources = here + there
    blocks = places(sizes)

    def kernel(pos_ref, *refs):
        ins, outs = refs[: len(sources)], refs[len(sources) :]
        for block in blocks:
            where = owner(pos_ref, block[-1], sizes)
            value = source(ins, block, sizes)
            for i, (start, width) in enumerate(cuts):
                if fold == 1:
                    outs[i][where] = value[:, start : start + width]
                else:
                    outs[0][where * fold + i] = value[:, start : start + width]

    shapes = [jax.ShapeDtypeStruct((devices, rows, width), bf16) for _, width in cuts]
    if fold > 1:
        shapes = [jax.ShapeDtypeStruct((devices * fold, rows, cuts[0][1]), bf16)]
    vmem = pl.BlockSpec(memory_space=pltpu.VMEM)
    return pl.pallas_call(
        kernel,
        out_shape=shapes,
        in_specs=[pl.BlockSpec(memory_space=pltpu.SMEM)] + [vmem] * len(sources),
        out_specs=[vmem] * len(shapes),
        compiler_params=VMEM,
        cost_estimate=pl.CostEstimate(flops=0, transcendentals=0, bytes_accessed=2 * devices * rows * sum(w for _, w in cuts) * 2),
        name="assemble",
    )(pos, *sources)


def norm_scale(values, gain):
    return values * lax.rsqrt(jnp.mean(values * values, axis=-1, keepdims=True) + norm_eps) * gain


def gelu_tanh(values):
    return jax.nn.gelu(values, approximate=True)


def adamw(state, grad, decay, rate):
    weight, mean, square, average = state
    mean_next = beta_first * mean + (1.0 - beta_first) * grad
    square_next = beta_second * square + (1.0 - beta_second) * grad * grad
    update = mean_next / (jnp.sqrt(square_next) + adam_eps)
    weight_next = weight - rate * (update + decay * weight)
    average_next = average_rate * average + (1.0 - average_rate) * weight_next
    return [weight_next, mean_next, square_next, average_next]


def dot(a, b, spec):
    return jnp.einsum(spec, a, b, preferred_element_type=f32)


NT = (((1,), (1,)), ((), ()))
TN = (((0,), (0,)), ((), ()))
NN = (((1,), (0,)), ((), ()))


def mm(a, b, dims):
    return lax.dot_general(a, b, dims, preferred_element_type=f32)


def softmax_of(q2, k2, own, allowed, scale):
    logits = mm(jnp.where(own, q2, 0.0).astype(bf16), k2, NT) * scale
    logits = jnp.where(allowed, logits, -1e30)
    exponent = jnp.exp(logits - jnp.max(logits, axis=-1, keepdims=True))
    return exponent / jnp.sum(exponent, axis=-1, keepdims=True)


def mask_of(col_ref, row_ref, n):
    query = lax.broadcasted_iota(jnp.int32, (n, n), 0)
    key = lax.broadcasted_iota(jnp.int32, (n, n), 1)
    return (col_ref[0] == row_ref[0]) & (key <= query)


def attend_kernel(scale, col_ref, row_ref, qkv_ref, out_ref):
    n, width = out_ref.shape
    allowed = mask_of(col_ref, row_ref, n)
    lane = lax.broadcasted_iota(jnp.int32, (n, 128), 1)
    owns = (lane < 64, lane >= 64)
    for p in range(width // 128):
        q2, k2, v2 = (qkv_ref[:, i * width + p * 128 : i * width + (p + 1) * 128] for i in range(3))
        total = jnp.zeros((n, 128), f32)
        for own in owns:
            probs = softmax_of(q2, k2, own, allowed, scale).astype(bf16)
            total += mm(probs, jnp.where(own, v2, 0.0).astype(bf16), NN)
        out_ref[:, p * 128 : (p + 1) * 128] = total.astype(bf16)


def attend_back_kernel(scale, col_ref, row_ref, qkv_ref, grad_ref, out_ref):
    n, width = grad_ref.shape
    allowed = mask_of(col_ref, row_ref, n)
    lane = lax.broadcasted_iota(jnp.int32, (n, 128), 1)
    owns = (lane < 64, lane >= 64)
    for p in range(width // 128):
        q2, k2, v2 = (qkv_ref[:, i * width + p * 128 : i * width + (p + 1) * 128] for i in range(3))
        g2 = grad_ref[:, p * 128 : (p + 1) * 128]
        grads = [jnp.zeros((n, 128), f32) for _ in range(3)]
        for own in owns:
            only = lambda v: jnp.where(own, v, 0.0).astype(bf16)
            probs = softmax_of(q2, k2, own, allowed, scale)
            grad_probs = mm(only(g2), v2, NT)
            inner = jnp.sum(probs * grad_probs, axis=-1, keepdims=True)
            grad_logits = (probs * (grad_probs - inner)).astype(bf16)
            grads[0] += mm(grad_logits, only(k2), NN)
            grads[1] += mm(grad_logits, only(q2), TN)
            grads[2] += mm(probs.astype(bf16), only(g2), TN)
        for i, factor in enumerate((scale, scale, 1.0)):
            out_ref[:, i * width + p * 128 : i * width + (p + 1) * 128] = (grads[i] * factor).astype(bf16)


def attention(kernel, segs, scale, qkv, *more):
    seqs, n = segs.shape
    width = qkv.shape[1] // 3
    out_width = 3 * width if more else width
    rows = lambda w: pl.BlockSpec((n, w), lambda s: (s, 0))
    matmuls = (5 if more else 2) * 2 * seqs * n * n * width
    return pl.pallas_call(
        functools.partial(kernel, scale),
        grid=(seqs,),
        out_shape=jax.ShapeDtypeStruct((seqs * n, out_width), bf16),
        in_specs=[pl.BlockSpec((1, n, 1), lambda s: (s, 0, 0)), pl.BlockSpec((1, 1, n), lambda s: (s, 0, 0)), rows(3 * width)]
        + [rows(width)] * len(more),
        out_specs=rows(out_width),
        compiler_params=VMEM,
        cost_estimate=pl.CostEstimate(flops=10 * matmuls, transcendentals=seqs * HEADS * n * n, bytes_accessed=2 * seqs * n * (3 * width + out_width)),
        name="attention_backward" if more else "attention",
    )(segs[:, :, None], segs[:, None, :], qkv, *more)


def body(sizes, *args):
    tokens, cotangent, segment_ids, routed = args[:4]
    states = [args[4 + 4 * i : 8 + 4 * i] for i in range(6)]
    qkv_state, out_state, up_state, down_state, router_state, gains_state = states
    seqs, length, width = tokens.shape
    capacity = routed.shape[1]
    count = seqs * capacity
    rows = out_state[0].shape[0]
    hidden = up_state[0].shape[1]
    fold = down_state[0].shape[0] // rows
    scale = (width // HEADS) ** (-0.5)
    pos = jnp.stack([lax.axis_index(n) for n in ("y", "c", "a", "b")]).astype(jnp.int32)

    low = lambda v: v.astype(bf16)
    small = jnp.concatenate([router_state[0][:, None], gains_state[0].T, jnp.zeros((rows, SMALL - 3), f32)], axis=1)
    send_qkv = low(jnp.concatenate([qkv_state[0][0], qkv_state[0][1], qkv_state[0][2], small], axis=1))
    send_up = low(jnp.concatenate([out_state[0], up_state[0]], axis=1))
    send_down = low(down_state[0]).reshape(fold, rows, width).transpose(1, 0, 2).reshape(rows, fold * width)
    mine_up = lax.all_gather(send_up, ("y", "a", "b"), axis=0, tiled=False)
    way_qkv = gather_first(send_qkv, sizes)
    way_down = gather_first(send_down, sizes)

    here = routed[:, :, None] == jnp.arange(length, dtype=jnp.int32)[None, None, :]
    pick = here.astype(bf16)
    is_routed = jnp.any(here, axis=1)
    picked = dot(pick, tokens, "sct,std->scd").astype(bf16).reshape(count, width)
    way_qkv = gather_second(after(way_qkv, picked), sizes)
    picked_cot = dot(pick, cotangent, "sct,std->scd").astype(bf16).reshape(count, width)
    segs = jnp.sum(jnp.where(here, segment_ids[:, None, :], 0), axis=-1)
    way_qkv = after(way_qkv, picked_cot, way_down)
    way_down = gather_second(after(way_down, way_qkv), sizes)
    way_qkv = gather_third(way_qkv, sizes)
    got = gather_last(way_qkv, sizes)
    way_down, pos_qkv = lax.optimization_barrier((way_down, pos))
    way_down = gather_third(way_down, sizes)

    w_qkv, w_small = assemble(*got, pos_qkv, sizes, [(0, 3 * width), (3 * width, SMALL)])
    w_qkv = w_qkv.reshape(width, 3 * width)
    w_small = w_small.reshape(width, SMALL)
    router_low = w_small[:, 0]
    gain_one = w_small[:, 1].astype(f32)
    gain_two = w_small[:, 2].astype(f32)

    picked_f = picked.astype(f32)
    back_cot = picked_cot.astype(f32)
    score = jnp.dot(picked, router_low, preferred_element_type=f32)
    normed_one, pull_one = jax.vjp(norm_scale, picked_f, gain_one)
    hidden_one = low(normed_one)
    projected = low(dot(hidden_one, w_qkv, "rd,de->re"))
    mine_up = after(mine_up, projected)
    theirs_up = shifted(mine_up, "c", sizes, 1)
    mixed = attention(attend_kernel, segs, scale, projected)
    mixed, theirs_up, way_down = lax.optimization_barrier((mixed, theirs_up, way_down))
    got_down = gather_last(way_down, sizes)

    w_both = join_cores(mine_up, theirs_up, sizes).reshape(width, width + hidden)
    w_out, w_up = w_both[:, :width], w_both[:, width:]
    attended = dot(mixed, w_out, "rd,de->re")
    first = picked_f + score[:, None] * attended
    normed_two, pull_two = jax.vjp(norm_scale, first, gain_two)
    hidden_two = low(normed_two)
    inner_pre = dot(hidden_two, w_up, "rd,df->rf")
    activ, pull_gelu = jax.vjp(gelu_tanh, inner_pre)
    activ_low = low(activ)
    grad_down_out = low(score[:, None] * back_cot)

    grad_wdown = low(dot(activ_low, grad_down_out, "rf,re->fe"))
    own_1, other_1 = sum_start(grad_wdown.reshape(-1, fold * rows, width), sizes)
    came_1 = shifted(other_1, "c", sizes, 1)

    got_down, pos_down = lax.optimization_barrier((got_down, after(pos, other_1)))
    (w_down,) = assemble(*got_down, pos_down, sizes, [(i * width, width) for i in range(fold)], fold)
    w_down = w_down.reshape(hidden, width)
    grad_activ = dot(grad_down_out, w_down, "re,fe->rf")
    grad_pre = low(pull_gelu(grad_activ)[0])

    grad_pre, came_1 = lax.optimization_barrier((grad_pre, came_1))
    (own_1a, part_1a), (own_1b, part_1b) = sum_first(own_1, came_1, sizes)
    grad_pre, part_1a, part_1b = lax.optimization_barrier((grad_pre, part_1a, part_1b))
    came_1a, came_1b = send_parts(part_1a, "b", sizes), send_parts(part_1b, "y", sizes)
    grad_wup = low(dot(hidden_two, grad_pre, "rd,rf->df")).reshape(-1, rows, hidden)
    own_2, other_2 = sum_start(grad_wup, sizes)
    grad_pre, other_2 = lax.optimization_barrier((grad_pre, other_2))
    came_2 = shifted(other_2, "c", sizes, 1)

    grad_hidden_two = dot(grad_pre, w_up, "rf,df->rd")
    grad_first_norm, grad_gain_two = pull_two(grad_hidden_two)
    grad_first = back_cot + grad_first_norm
    grad_attended = low(score[:, None] * grad_first)

    grad_attended, came_1a, came_1b, came_2 = lax.optimization_barrier((grad_attended, came_1a, came_1b, came_2))
    (own_2a, part_2a), (own_2b, part_2b) = sum_first(own_2, came_2, sizes)
    (own_1a, part_1a), (own_1b, part_1b) = sum_second((own_1a, own_1b), (came_1a, came_1b), sizes)
    grad_attended, part_1a, part_1b, part_2a, part_2b = lax.optimization_barrier((grad_attended, part_1a, part_1b, part_2a, part_2b))
    came_1a, came_1b = send_parts(part_1a, "y", sizes), send_parts(part_1b, "b", sizes)
    came_2a, came_2b = send_parts(part_2a, "b", sizes), send_parts(part_2b, "y", sizes)

    grad_mixed = low(dot(grad_attended, w_out, "re,de->rd"))
    grad_projected = attention(attend_back_kernel, segs, scale, projected, grad_mixed)

    ready = lax.optimization_barrier((grad_projected, came_1a, came_1b, came_2a, came_2b))
    grad_projected, came_1a, came_1b, came_2a, came_2b = ready
    own_1, part_1 = sum_third((own_1a, own_1b), (came_1a, came_1b), sizes)
    (own_2a, part_2a), (own_2b, part_2b) = sum_second((own_2a, own_2b), (came_2a, came_2b), sizes)
    grad_projected, part_1, part_2a, part_2b = lax.optimization_barrier((grad_projected, part_1, part_2a, part_2b))
    came_1 = send_parts(part_1, "a", sizes)
    came_2a, came_2b = send_parts(part_2a, "y", sizes), send_parts(part_2b, "b", sizes)

    grad_wqkv = low(dot(hidden_one, grad_projected, "rd,re->de"))
    grad_wout = low(dot(mixed, after(grad_attended, grad_projected), "rd,re->de"))
    rest = jnp.concatenate([grad_wqkv, grad_wout], axis=1).reshape(-1, rows, 4 * width)
    own_3, other_3 = sum_start(rest, sizes)
    grad_projected, other_3, activ_late = lax.optimization_barrier((grad_projected, other_3, activ_low))
    came_3 = shifted(other_3, "c", sizes, 1)

    down_out = dot(activ_late, w_down, "rf,fe->re")
    second = low(first + score[:, None] * down_out).reshape(seqs, capacity, width)
    grad_score = jnp.sum(back_cot * down_out, axis=-1) + jnp.sum(grad_first * attended, axis=-1)
    grad_hidden_one = dot(grad_projected, w_qkv, "re,de->rd")
    grad_picked_norm, grad_gain_one = pull_one(grad_hidden_one)
    grad_rows = grad_first + grad_picked_norm + grad_score[:, None] * router_low.astype(f32)[None, :]
    grad_rows = low(grad_rows).reshape(seqs, capacity, width)
    grad_router = jnp.sum(grad_score[:, None] * picked_f, axis=0)
    grad_small = jnp.stack([grad_router, grad_gain_one, grad_gain_two], axis=1)
    grad_small = low(jnp.pad(grad_small, ((0, 0), (0, SMALL - 3)))).reshape(-1, rows, SMALL)
    own_s, other_s = sum_start(grad_small, sizes)
    came_s = shifted(other_s, "c", sizes, 1)
    came_3, came_s, second, grad_rows = lax.optimization_barrier((came_3, came_s, second, grad_rows))

    join = lambda a, b: jnp.concatenate([a, b], axis=-1)
    (own_3a, part_3a), (own_3b, part_3b) = sum_first(join(own_3, own_s), join(came_3, came_s), sizes)
    ready = lax.optimization_barrier((part_3a, part_3b, second, grad_rows, came_1, came_2a, came_2b))
    part_3a, part_3b, second, grad_rows, came_1, came_2a, came_2b = ready
    came_3a, came_3b = send_parts(part_3a, "b", sizes), send_parts(part_3b, "y", sizes)
    own_2, part_2 = sum_third((own_2a, own_2b), (came_2a, came_2b), sizes)
    part_2, second = lax.optimization_barrier((part_2, second))
    came_2 = send_parts(part_2, "a", sizes)

    block_out = jnp.where(is_routed[:, :, None], low(dot(pick, second, "sct,scd->std")), tokens)
    came_3a, came_3b, grad_rows, block_out = lax.optimization_barrier((came_3a, came_3b, grad_rows, block_out))
    (own_3a, part_3a), (own_3b, part_3b) = sum_second((own_3a, own_3b), (came_3a, came_3b), sizes)
    part_3a, part_3b, grad_rows, came_1 = lax.optimization_barrier((part_3a, part_3b, grad_rows, came_1))
    came_3a, came_3b = send_parts(part_3a, "y", sizes), send_parts(part_3b, "b", sizes)
    tokens_grad = jnp.where(is_routed[:, :, None], low(dot(pick, grad_rows, "sct,scd->std")), cotangent)
    sum_down = add_up(own_1, came_1)
    came_3a, came_3b, tokens_grad = lax.optimization_barrier((came_3a, came_3b, tokens_grad))
    own_3, part_3 = sum_third((own_3a, own_3b), (came_3a, came_3b), sizes)
    part_3, came_2 = lax.optimization_barrier((part_3, came_2))
    came_3 = send_parts(part_3, "a", sizes)
    sum_up = add_up(own_2, came_2)
    sum_rest = add_up(own_3, came_3)

    total_small = sum_rest[:, 4 * width :]
    grads = (
        jnp.stack([sum_rest[:, i * width : (i + 1) * width] for i in range(3)]),
        sum_rest[:, 3 * width : 4 * width],
        sum_up,
        sum_down,
        total_small[:, 0],
        total_small[:, 1:3].T,
    )
    decays = (decay_rate, decay_rate, decay_rate, decay_rate, 0.0, 0.0)
    results = [block_out, tokens_grad]
    for state, grad, decay, rate in zip(states, grads, decays, learn_rates):
        results = results + adamw(state, grad, decay, rate)
    return tuple(results)


def solution(mesh):
    lead = mesh.shape["dp"] // 2
    inner = mesh.shape["fsdp"] // 4
    names = ("y", "c", "a", "b")
    fine = Mesh(mesh.devices.reshape(lead, 2, 4, inner), names)
    sizes = dict(zip(names, (lead, 2, 4, inner)))
    head, second, only = P(names, None, None), P(None, names, None), P(names, None)
    weights = (second,) * 4 + (only,) * 12 + (P(names),) * 4 + (P(None, names),) * 4
    return jax.shard_map(
        functools.partial(body, sizes),
        mesh=fine,
        in_specs=(head, head, only, only) + weights,
        out_specs=(head, head) + weights,
        check_vma=False,
    )
```

```python
import functools
import math

import jax
import jax.numpy as jnp
from jax import lax
from jax.experimental import pallas as pl
from jax.experimental.pallas import tpu as pltpu
from jax.sharding import Mesh, PartitionSpec as P

HEADS = 12
SMALL = 256

norm_eps = 1e-06
learn_rates = (0.03, 0.1, 0.03, 0.02, 0.03, 0.2)
beta_first = 0.5
beta_second = 0.5
adam_eps = 1e-08
decay_rate = 0.1
average_rate = 0.7
exact_mode = lax.Precision.HIGHEST
f32 = jnp.float32
bf16 = jnp.bfloat16


def shifted(value, axis, sizes, step):
    n = sizes[axis]
    return lax.ppermute(value, axis, [(i, (i + step) % n) for i in range(n)])


def after(value, *others):
    return lax.optimization_barrier((value, others))[0]


def gather_axis(value, axis, sizes):
    return [value] + [shifted(value, axis, sizes, k) for k in range(1, sizes[axis])]


def halves_of(value):
    half = len(value) // 2
    return value[:half], value[half:]


def go_second(halves, sizes):
    return gather_axis(halves[0], "b", sizes), gather_axis(halves[1], "y", sizes)


def go_third(halves, sizes):
    return gather_axis(halves[0], "y", sizes), gather_axis(halves[1], "b", sizes)


def stacked(lists):
    return tuple(jnp.stack(list(v)) for v in lists)


def gather_last(lists, sizes):
    here = lists[0] + lists[1]
    return here, [shifted(v, "c", sizes, 1) for v in here]


def take(value, index, axis):
    return lax.dynamic_index_in_dim(value, index, axis, keepdims=False)


def columns_of(value, core, sizes):
    ny = sizes["y"]
    chunk = value.shape[1] // (2 * ny)
    return jnp.concatenate([lax.dynamic_slice_in_dim(value, (2 * y + core) * chunk, chunk, 1) for y in range(ny)], axis=1)


def swapped(value, sizes):
    return value, shifted(value, "c", sizes, 1)


def add_up(own, came):
    own = own.astype(f32)
    for part in came:
        own = own + part.astype(f32)
    return own


def send_parts(parts, axis, sizes):
    return [shifted(parts[k].astype(bf16), axis, sizes, k + 1) for k in range(sizes[axis] - 1)]


def sum_first(grad, sizes):
    return send_parts(grad[1], "b", sizes), send_parts(grad[3], "y", sizes)


def sum_second(grad, came):
    return add_up(grad[0][1:], [v[1:] for v in came[0]]).astype(bf16), add_up(grad[2][1:], [v[1:] for v in came[1]]).astype(bf16)


def sum_third(grad, came, more):
    first = add_up(grad[0][0], [v[0] for v in came[0]] + more[0])
    second = add_up(grad[2][0], [v[0] for v in came[1]] + more[1])
    total = jnp.concatenate([first, second], axis=-1)
    return total[0], total[1:].astype(bf16)


def send_second(parts, sizes):
    return send_parts(parts[0], "y", sizes), send_parts(parts[1], "b", sizes)


def places(sizes):
    half = sizes["a"] // 2
    out = []
    for kc in range(2):
        for ky in range(sizes["y"]):
            for kb in range(sizes["b"]):
                for ka in range(sizes["a"]):
                    part = 0 if ka < half else 1
                    out.append((kc, part, ky, kb, ka % half, (ky, kc, ka, kb)))
    return out


def owner(pos_ref, steps, sizes, fixed=False):
    ky, kc, ka, kb = steps
    y = lax.rem(pos_ref[0] + (sizes["y"] - ky), sizes["y"])
    c = lax.rem(pos_ref[1] + (2 - kc), 2)
    a = ka if fixed else lax.rem(pos_ref[2] + (sizes["a"] - ka), sizes["a"])
    b = lax.rem(pos_ref[3] + (sizes["b"] - kb), sizes["b"])
    return ((y * 2 + c) * sizes["a"] + a) * sizes["b"] + b


COST = 100


def source(ins, block, sizes):
    kc, part, ky, kb, ka, _ = block
    base = kc * (sizes["y"] + sizes["b"])
    return ins[base + ky][kb, ka] if part == 0 else ins[base + sizes["y"] + kb][ky, ka]


def assemble(here, there, pos, sizes, cuts, fold=1, fixed=False):
    rows = here[0].shape[-2]
    devices = 2 * sizes["y"] * sizes["b"] * sizes["a"]
    sources = here + there
    blocks = places(sizes)

    def kernel(pos_ref, *refs):
        ins, outs = refs[: len(sources)], refs[len(sources) :]
        for block in blocks:
            where = owner(pos_ref, block[-1], sizes, fixed)
            value = source(ins, block, sizes)
            for i, (start, width) in enumerate(cuts):
                if fold == 1:
                    outs[i][where] = value[:, start : start + width]
                else:
                    outs[0][where * fold + i] = value[:, start : start + width]

    shapes = [jax.ShapeDtypeStruct((devices, rows, width), bf16) for _, width in cuts]
    if fold > 1:
        shapes = [jax.ShapeDtypeStruct((devices * fold, rows, cuts[0][1]), bf16)]
    vmem = pl.BlockSpec(memory_space=pltpu.VMEM)
    return pl.pallas_call(
        kernel,
        out_shape=shapes,
        in_specs=[pl.BlockSpec(memory_space=pltpu.SMEM)] + [vmem] * len(sources),
        out_specs=[vmem] * len(shapes),
        name="assemble",
        **params(2 * mib(*sources) + 3, 0, 4 * devices * rows * sum(w for _, w in cuts)),
    )(pos, *sources)


def adamw(state, grad, decay, rate):
    weight, mean, square, average = state
    mean_next = beta_first * mean + (1.0 - beta_first) * grad
    square_next = beta_second * square + (1.0 - beta_second) * grad * grad
    update = mean_next / (jnp.sqrt(square_next) + adam_eps)
    weight_next = weight - rate * (update + decay * weight)
    average_next = average_rate * average + (1.0 - average_rate) * weight_next
    return [weight_next, mean_next, square_next, average_next]


def dot(a, b, spec):
    return jnp.einsum(spec, a, b, preferred_element_type=f32)


NT = (((1,), (1,)), ((), ()))
TN = (((0,), (0,)), ((), ()))
NN = (((1,), (0,)), ((), ()))


def mm(a, b, dims):
    return lax.dot_general(a, b, dims, preferred_element_type=f32)


def only(own, value):
    return jnp.where(own, value, 0.0).astype(bf16)


def heads_of(n):
    lane = lax.broadcasted_iota(jnp.int32, (n, 128), 1)
    return lane < 64, lane >= 64


def attend_kernel(scale, col_ref, row_ref, qkv_ref, out_ref):
    n, width = out_ref.shape
    query = lax.broadcasted_iota(jnp.int32, (n, n), 0)
    key = lax.broadcasted_iota(jnp.int32, (n, n), 1)
    allowed = (col_ref[0] == row_ref[0]) & (key <= query)
    for p in range(width // 128):
        q2, k2, v2 = (qkv_ref[:, i * width + p * 128 : i * width + (p + 1) * 128] for i in range(3))
        total = jnp.zeros((n, 128), f32)
        for own in heads_of(n):
            logits = jnp.where(allowed, mm(only(own, q2 * scale), k2, NT), -1e30)
            exponent = jnp.exp(logits - jnp.max(logits, axis=-1, keepdims=True))
            probs = exponent * (1.0 / jnp.sum(exponent, axis=-1, keepdims=True))
            total += mm(probs.astype(bf16), only(own, v2), NN)
        out_ref[:, p * 128 : (p + 1) * 128] = total.astype(bf16)


def attend_back_kernel(scale, col_ref, row_ref, qkv_ref, grad_ref, out_ref):
    n, width = grad_ref.shape
    key = lax.broadcasted_iota(jnp.int32, (n, n), 0)
    query = lax.broadcasted_iota(jnp.int32, (n, n), 1)
    allowed = (col_ref[0] == row_ref[0]) & (key <= query)
    for p in range(width // 128):
        q2, k2, v2 = (qkv_ref[:, i * width + p * 128 : i * width + (p + 1) * 128] for i in range(3))
        g2 = grad_ref[:, p * 128 : (p + 1) * 128]
        grads = [jnp.zeros((n, 128), f32) for _ in range(3)]
        for own in heads_of(n):
            q_own, g_own = only(own, q2 * scale), only(own, g2)
            logits = jnp.where(allowed, mm(k2, q_own, NT), -1e30)
            exponent = jnp.exp(logits - jnp.max(logits, axis=0, keepdims=True))
            probs = exponent * (1.0 / jnp.sum(exponent, axis=0, keepdims=True))
            grad_probs = mm(v2, g_own, NT)
            inner = jnp.sum(probs * grad_probs, axis=0, keepdims=True)
            grad_logits = (probs * (grad_probs - inner)).astype(bf16)
            grads[0] += mm(grad_logits, only(own, k2 * scale), TN)
            grads[1] += mm(grad_logits, q_own, NN)
            grads[2] += mm(probs.astype(bf16), g_own, NN)
        for i in range(3):
            out_ref[:, i * width + p * 128 : i * width + (p + 1) * 128] = grads[i].astype(bf16)


def attention(kernel, segs, scale, qkv, *more):
    seqs, n = segs.shape
    width = qkv.shape[1] // 3
    out_width = 3 * width if more else width
    rows = lambda w: pl.BlockSpec((n, w), lambda s: (s, 0))
    matmuls = (5 if more else 2) * 2 * seqs * n * n * width
    return pl.pallas_call(
        functools.partial(kernel, scale),
        grid=(seqs,),
        out_shape=jax.ShapeDtypeStruct((seqs * n, out_width), bf16),
        in_specs=[pl.BlockSpec((1, n, 1), lambda s: (s, 0, 0)), pl.BlockSpec((1, 1, n), lambda s: (s, 0, 0)), rows(3 * width)]
        + [rows(width)] * len(more),
        out_specs=rows(out_width),
        name="attention_backward" if more else "attention",
        **params(14, 10 * matmuls, 2 * seqs * n * (3 * width + out_width), seqs * HEADS * n * n),
    )(segs[:, :, None], segs[:, None, :], qkv, *more)


def full(shape):
    return pl.BlockSpec(shape, lambda *_: (0,) * len(shape))


def params(room, flops, moved, transcendentals=0):
    return dict(
        compiler_params=pltpu.CompilerParams(vmem_limit_bytes=int(room * 2**20)),
        cost_estimate=pl.CostEstimate(flops=flops // COST, transcendentals=transcendentals // COST, bytes_accessed=moved // COST),
    )


def mib(*shapes):
    return sum(math.prod(v.shape) * v.dtype.itemsize for v in shapes) / 2**20


def weight_grad(lefts, rights, jobs, shapes, pos, sizes, extra=None):
    ny, na, nb = sizes["y"], sizes["a"], sizes["b"]
    blocks = ny * na * nb
    count = lefts[0][0].shape[0]
    room = max(shapes[job[4]][0] * job[3] for job in jobs)
    room = [(rows, room // rows) for rows in sorted({shapes[job[4]][0] for job in jobs})]

    def kernel(pos_ref, *refs):
        ins, outs = refs[: -4 - len(room) - len(lefts)], refs[-4 - len(room) - len(lefts) : -len(room) - len(lefts)]
        accs, turned = refs[-len(room) - len(lefts) : -len(lefts)], refs[-len(lefts) :]
        right_refs = ins[2 * len(lefts) : 2 * len(lefts) + 2 * len(rights)]
        core = pos_ref[1]

        def columns(ref, y, width):
            if width % 128 == 0:
                return ref[:, pl.ds(pl.multiple_of((2 * y + core) * width, 128), width)]
            both = ref[:, 2 * y * width : 2 * (y + 1) * width]
            return jnp.where(core == 0, both[:, :width], both[:, width:])

        for i, turn in enumerate(turned):
            width = turn.shape[1] // ny
            for side in range(2):
                for y in range(ny):
                    turn[side, y * width : (y + 1) * width, :] = columns(ins[2 * i + side], y, width).T

        def spread(read, part, to, width):
            for ky in range(ny):
                for ka in range(na):
                    for kb in range(nb):
                        y, a, b = lax.rem(pos_ref[0] + ky, ny), lax.rem(pos_ref[2] + ka, na), lax.rem(pos_ref[3] + kb, nb)
                        value = read((y * na + a) * nb + b).astype(bf16)
                        if part == 0:
                            ref = outs[0].at[ky, ka] if kb == 0 else outs[1].at[kb - 1, ky, ka]
                        else:
                            ref = outs[2].at[kb, ka] if ky == 0 else outs[3].at[ky - 1, kb, ka]
                        ref[:, to : to + width] = value

        for left, right, start, width, part, to in jobs:
            rows = shapes[part][0]
            acc = accs[[r for r, _ in room].index(rows)]
            total = mm(turned[left][0], right_refs[2 * right][:, start : start + width], NN)
            total += mm(turned[left][1], right_refs[2 * right + 1][:, start : start + width], NN)
            acc[:, :, :width] = total.reshape(blocks, rows, width)
            spread(lambda i: acc[i, :, :width], part, to, width)
        if extra is not None:
            spread(lambda i: ins[-1][i], extra[1], extra[2], extra[0].shape[-1])

    leads = [(ny, na), (nb - 1, ny, na), (nb, na), (ny - 1, nb, na)]
    outs = [jax.ShapeDtypeStruct(v + shapes[i // 2], bf16) for i, v in enumerate(leads)]
    arrays = [v for pair in lefts for v in pair] + [v for pair in rights for v in pair] + ([extra[0]] if extra else [])
    scratch = [jax.ShapeDtypeStruct((blocks, rows, width), f32) for rows, width in room]
    scratch += [jax.ShapeDtypeStruct((2, pair[0].shape[1] // 2, count), bf16) for pair in lefts]
    vmem = pl.BlockSpec(memory_space=pltpu.VMEM)
    work = sum(4 * count * blocks * shapes[job[4]][0] * job[3] for job in jobs)
    return pl.pallas_call(
        kernel,
        out_shape=outs,
        in_specs=[pl.BlockSpec(memory_space=pltpu.SMEM)] + [vmem] * len(arrays),
        out_specs=[vmem] * 4,
        scratch_shapes=[pltpu.VMEM(v.shape, v.dtype) for v in scratch],
        name="weight_grad",
        **params(mib(*arrays, *outs, *scratch) * 1.1 + 8, work, sum(v.size for v in arrays) * 2 + 2 * blocks * sum(r * c for r, c in shapes)),
    )(pos, *arrays)


def weight_grad_plain(lefts, rights, jobs, shapes, pos, sizes, extra=None):
    ny, na, nb = sizes["y"], sizes["a"], sizes["b"]
    done = ([], [])
    lefts = [[columns_of(v, lax.axis_index("c"), sizes) for v in pair] for pair in lefts]
    for left, right, start, width, part, to in jobs:
        total = sum(dot(lefts[left][i], rights[right][i][:, start : start + width], "rd,re->de") for i in range(2))
        done[part].append((to, total.astype(bf16).reshape(ny, na, nb, -1, width)))
    if extra is not None:
        done[extra[1]].append((extra[2], extra[0].astype(bf16).reshape((ny, na, nb) + extra[0].shape[1:])))
    halves = []
    for part in done:
        value = jnp.concatenate([v for _, v in sorted(part, key=lambda item: item[0])], axis=-1)
        for axis, at in ((0, 0), (1, 2), (2, 3)):
            value = jnp.roll(value, -pos[at], axis)
        halves.append(value)
    first, second = halves[0].transpose(2, 0, 1, 3, 4), halves[1].transpose(0, 2, 1, 3, 4)
    return first[0], first[1:], second[0], second[1:]


def norm_of(value):
    return lax.rsqrt(jnp.mean(value * value, axis=-1, keepdims=True) + norm_eps)


def feed_forward(mixed, picked, score, gain, w_both):
    count, width = picked.shape
    steps = w_both.shape[1] // width

    def kernel(mixed_ref, picked_ref, score_ref, gain_ref, w_ref, attended_ref, first_ref, hidden_ref, activ_ref, slope_ref):
        @pl.when(pl.program_id(0) == 0)
        def _():
            attended = mm(mixed_ref[...], w_ref[...], NN)
            first = picked_ref[...].astype(f32) + score_ref[...] * attended
            attended_ref[...] = attended
            first_ref[...] = first
            hidden_ref[...] = (first * norm_of(first) * gain_ref[...]).astype(bf16)

        @pl.when(pl.program_id(0) > 0)
        def _():
            v = mm(hidden_ref[...], w_ref[...], NN)
            c0 = (2.0 / jnp.pi) ** 0.5
            square = v * v
            t = jnp.tanh(c0 * (v + 0.044715 * (square * v)))
            cdf = 0.5 * (1.0 + t)
            activ_ref[...] = (v * cdf).astype(bf16)
            slope_ref[...] = cdf + (0.5 * v) * (1.0 - t * t) * (c0 + (3.0 * 0.044715 * c0) * square)

    later = lambda j: (0, jnp.maximum(j - 1, 0))
    return pl.pallas_call(
        kernel,
        grid=(steps,),
        out_shape=[jax.ShapeDtypeStruct((count, width), d) for d in (f32, f32, bf16)]
        + [jax.ShapeDtypeStruct((count, (steps - 1) * width), d) for d in (bf16, f32)],
        in_specs=[full((count, width)), full((count, width)), full((count, 1)), full((1, width)), pl.BlockSpec((width, width), lambda j: (0, j))],
        out_specs=[full((count, width))] * 3 + [pl.BlockSpec((count, width), later)] * 2,
        name="feed_forward",
        **params(30, 2 * count * width * width * steps, 2 * width * width * steps + 10 * count * width + 6 * count * width * steps, count * width * steps),
    )(mixed, picked, score, gain, w_both)


def down_both(activ, slope, grad_out, w_down, first, score, back_cot):
    count, width = first.shape
    steps = activ.shape[1] // width

    def kernel(activ_ref, slope_ref, grad_ref, w_ref, first_ref, score_ref, cot_ref, pre_ref, second_ref, dr_ref, acc_ref):
        j = pl.program_id(0)
        pre_ref[...] = (mm(grad_ref[...], w_ref[...], NT) * slope_ref[...]).astype(bf16)
        out = mm(activ_ref[...], w_ref[...], NN)

        @pl.when(j == 0)
        def _():
            acc_ref[...] = out

        @pl.when(j > 0)
        def _():
            acc_ref[...] += out

        @pl.when(j == steps - 1)
        def _():
            total = acc_ref[...]
            second_ref[...] = (first_ref[...] + score_ref[...] * total).astype(bf16)
            dr_ref[...] = jnp.sum(cot_ref[...].astype(f32) * total, axis=-1, keepdims=True)

    tile = pl.BlockSpec((count, width), lambda j: (0, j))
    one = full((count, width))
    return pl.pallas_call(
        kernel,
        grid=(steps,),
        out_shape=[jax.ShapeDtypeStruct(activ.shape, bf16), jax.ShapeDtypeStruct((count, width), bf16), jax.ShapeDtypeStruct((count, 1), f32)],
        in_specs=[tile, tile, one, pl.BlockSpec((width, width), lambda j: (j, 0)), one, full((count, 1)), one],
        out_specs=[tile, one, full((count, 1))],
        scratch_shapes=[pltpu.VMEM((count, width), f32)],
        name="down_both",
        **params(28, 4 * count * width * width * steps, 2 * width * width * steps + 8 * count * width * steps + 10 * count * width),
    )(activ, slope, grad_out, w_down, first, score, back_cot)


def back_of_norm(grad, value, gain):
    inv = norm_of(value)
    normed = value * inv
    scaled = grad * gain
    mean = jnp.mean(scaled * normed, axis=-1, keepdims=True)
    return (scaled - normed * mean) * inv, jnp.sum(grad * normed, axis=0, keepdims=True)


def up_back(grad_pre, w_both, first, attended, score, back_cot, gain):
    count, width = first.shape
    steps = w_both.shape[1] // width

    def kernel(pre_ref, w_ref, first_ref, attended_ref, score_ref, cot_ref, gain_ref, out_ref, low_ref, mixed_ref, dr_ref, dgain_ref, acc_ref):
        j = pl.program_id(0)

        @pl.when(j == 0)
        def _():
            acc_ref[...] = jnp.zeros_like(acc_ref)

        @pl.when(j < steps - 1)
        def _():
            acc_ref[...] += mm(pre_ref[...], w_ref[...], NT)

        @pl.when(j == steps - 1)
        def _():
            grad, dgain = back_of_norm(acc_ref[...], first_ref[...], gain_ref[...])
            grad = cot_ref[...].astype(f32) + grad
            low = (score_ref[...] * grad).astype(bf16)
            out_ref[...] = grad
            low_ref[...] = low
            dgain_ref[...] = dgain
            dr_ref[...] = jnp.sum(grad * attended_ref[...], axis=-1, keepdims=True)
            mixed_ref[...] = mm(low, w_ref[...], NT).astype(bf16)

    one = full((count, width))
    return pl.pallas_call(
        kernel,
        grid=(steps,),
        out_shape=[jax.ShapeDtypeStruct((count, width), d) for d in (f32, bf16, bf16)]
        + [jax.ShapeDtypeStruct((count, 1), f32), jax.ShapeDtypeStruct((1, width), f32)],
        in_specs=[
            pl.BlockSpec((count, width), lambda j: (0, jnp.minimum(j, steps - 2))),
            pl.BlockSpec((width, width), lambda j: (0, lax.rem(j + 1, steps))),
            one,
            one,
            full((count, 1)),
            one,
            full((1, width)),
        ],
        out_specs=[one, one, one, full((count, 1)), full((1, width))],
        scratch_shapes=[pltpu.VMEM((count, width), f32)],
        name="up_back",
        **params(28, 2 * count * width * width * steps, 2 * width * width * steps + 2 * count * width * steps + 18 * count * width),
    )(grad_pre, w_both, first, attended, score, back_cot, gain)


def project_back(grad_projected, w_qkv, picked, gain, router, grad_first, grad_score):
    count, width = picked.shape
    steps = 3

    def kernel(grad_ref, w_ref, picked_ref, gain_ref, router_ref, first_ref, dr_ref, out_ref, dgain_ref, drouter_ref, acc_ref):
        j = pl.program_id(0)

        @pl.when(j == 0)
        def _():
            acc_ref[...] = jnp.zeros_like(acc_ref)

        acc_ref[...] += mm(grad_ref[...], w_ref[...], NT)

        @pl.when(j == steps - 1)
        def _():
            value, dr = picked_ref[...].astype(f32), dr_ref[...]
            grad, dgain = back_of_norm(acc_ref[...], value, gain_ref[...])
            out_ref[...] = (first_ref[...] + grad + dr * router_ref[...]).astype(bf16)
            dgain_ref[...] = dgain
            drouter_ref[...] = jnp.sum(dr * value, axis=0, keepdims=True)

    one, row = full((count, width)), full((1, width))
    return pl.pallas_call(
        kernel,
        grid=(steps,),
        out_shape=[jax.ShapeDtypeStruct((count, width), bf16)] + [jax.ShapeDtypeStruct((1, width), f32)] * 2,
        in_specs=[pl.BlockSpec((count, width), lambda j: (0, j)), pl.BlockSpec((width, width), lambda j: (0, j)), one, row, row, one, full((count, 1))],
        out_specs=[one, row, row],
        scratch_shapes=[pltpu.VMEM((count, width), f32)],
        name="project_back",
        **params(22, 2 * count * width * width * steps, 2 * width * width * steps + 2 * count * width * steps + 10 * count * width),
    )(grad_projected, w_qkv, picked, gain, router, grad_first, grad_score)


def body(sizes, *args):
    tokens, cotangent, segment_ids, routed = args[:4]
    states = [args[4 + 4 * i : 8 + 4 * i] for i in range(6)]
    qkv_state, out_state, up_state, down_state, router_state, gains_state = states
    seqs, length, width = tokens.shape
    capacity = routed.shape[1]
    count = seqs * capacity
    rows = out_state[0].shape[0]
    hidden = up_state[0].shape[1]
    fold = down_state[0].shape[0] // rows
    scale = (width // HEADS) ** (-0.5)
    pos = jnp.stack([lax.axis_index(n) for n in ("y", "c", "a", "b")]).astype(jnp.int32)

    low = lambda v: v.astype(bf16)
    small = jnp.concatenate([router_state[0][:, None], gains_state[0].T, jnp.zeros((rows, SMALL - 3), f32)], axis=1)
    send_qkv = low(jnp.concatenate([qkv_state[0][0], qkv_state[0][1], qkv_state[0][2], small], axis=1))
    fold_down = [down_state[0][i * rows : (i + 1) * rows] for i in range(fold)]
    send_rest = low(jnp.concatenate([out_state[0], up_state[0]] + fold_down, axis=1))
    rest = lax.all_gather(send_rest, "a", axis=0, tiled=True).reshape((-1,) + send_rest.shape)
    barrier = lax.optimization_barrier

    here = routed[:, :, None] == jnp.arange(length, dtype=jnp.int32)[None, None, :]
    pick = here.astype(bf16)
    is_routed = jnp.any(here, axis=1)
    way_qkv = gather_axis(after(send_qkv, send_rest), "a", sizes)
    picked = dot(pick, tokens, "sct,std->scd").astype(bf16).reshape(count, width)
    way_qkv = stacked(halves_of(after(way_qkv, picked)))
    way_qkv = go_second(way_qkv, sizes)
    back_cot = dot(pick, cotangent, "sct,std->scd").astype(bf16).reshape(count, width)
    segs = jnp.sum(jnp.where(here, segment_ids[:, None, :], 0), axis=-1)
    way_qkv = stacked(after(way_qkv, back_cot, segs))
    way_qkv = go_third(way_qkv, sizes)
    rest = after(rest, way_qkv)
    got = gather_last(way_qkv, sizes)
    part_up, part_down = halves_of(rest[..., : width + hidden]), halves_of(rest[..., width + hidden :])
    way_up, way_down = go_second(part_up, sizes), go_second(part_down, sizes)

    w_qkv, w_small = assemble(*got, after(pos, part_up, part_down), sizes, [(0, 3 * width), (3 * width, SMALL)])
    w_qkv, w_small, way_up = barrier((w_qkv, w_small, way_up))
    way_up = stacked(way_up)
    w_qkv, way_up = barrier((w_qkv, way_up))
    way_up = go_third(way_up, sizes)
    w_qkv = w_qkv.reshape(width, 3 * width)
    w_small = w_small.reshape(width, SMALL)
    narrow = w_small[:, :3].astype(f32).T
    router, gain_one, gain_two = narrow[0:1], narrow[1:2], narrow[2:3]

    picked_f = picked.astype(f32)
    score = dot(picked, w_small, "rd,de->re")[:, :1]
    hidden_one = low(picked_f * norm_of(picked_f) * gain_one)
    projected = low(dot(hidden_one, w_qkv, "rd,de->re"))
    projected, way_down = barrier((projected, way_down))
    way_down = stacked(way_down)
    projected, way_down = barrier((projected, way_down))
    way_down = go_third(way_down, sizes)
    mixed = attention(attend_kernel, segs, scale, projected)
    grad_down_out = low(score * back_cot.astype(f32))
    mixed, way_up, grad_down_out = barrier((mixed, way_up, grad_down_out))
    got_up = gather_last(way_up, sizes)
    (w_both,) = assemble(*got_up, pos, sizes, [(0, width + hidden)], fixed=True)
    w_both = w_both.reshape(width, width + hidden)
    attended, first, hidden_two, activ_low, slope = feed_forward(mixed, picked, score, gain_two, w_both)
    make = weight_grad if rows % 8 == 0 else weight_grad_plain

    activ_low, way_down = barrier((activ_low, way_down))
    got_down = gather_last(way_down, sizes)
    activ_pair = swapped(activ_low, sizes)
    grad_down_pair = swapped(grad_down_out, sizes)
    (w_down,) = assemble(*got_down, pos, sizes, [(i * width, width) for i in range(fold)], fold, fixed=True)
    w_down = w_down.reshape(hidden, width)
    grad_pre, second, dr_second = down_both(activ_low, slope, grad_down_out, w_down, first, score, back_cot)

    activ_pair, grad_pre = barrier((activ_pair, grad_pre))
    grad_pre_pair = swapped(grad_pre, sizes)
    hidden_two_pair = swapped(hidden_two, sizes)
    mixed_pair = swapped(mixed, sizes)
    half = width // 2
    jobs = [(0, 0, 0, half, 0, 0), (0, 0, half, half, 1, 0)]
    grad_2 = make([activ_pair], [grad_down_pair], jobs, ((fold * rows, half),) * 2, pos, sizes)
    grad_2, grad_pre = barrier((grad_2, grad_pre))
    came_2 = sum_first(grad_2, sizes)
    grad_first, grad_attended, grad_mixed, dr_first, grad_gain_two = up_back(grad_pre, w_both, first, attended, score, back_cot, gain_two)

    grad_attended_pair = swapped(grad_attended, sizes)
    hidden_one_pair = swapped(hidden_one, sizes)
    grad_attended_pair, grad_pre_pair, hidden_two_pair, mixed_pair = barrier((grad_attended_pair, grad_pre_pair, hidden_two_pair, mixed_pair))
    half = (hidden + width) // 2
    jobs = [(0, 0, 0, width, 0, 0), (0, 0, width, width, 0, width), (0, 0, 2 * width, half - 2 * width, 0, 2 * width)]
    jobs += [(0, 0, half, 3 * width - half, 1, 0), (0, 0, 3 * width, width, 1, 3 * width - half), (1, 1, 0, width, 1, 4 * width - half)]
    grad_1 = make([hidden_two_pair, mixed_pair], [grad_pre_pair, grad_attended_pair], jobs, ((rows, half),) * 2, pos, sizes)
    grad_1, came_2 = barrier((grad_1, came_2))
    more_2 = sum_second(grad_2, came_2)
    grad_1, grad_mixed, more_2 = barrier((grad_1, grad_mixed, more_2))
    came_1 = sum_first(grad_1, sizes)
    more_2 = send_second(more_2, sizes)
    grad_projected = attention(attend_back_kernel, segs, scale, projected, grad_mixed)

    grad_projected, more_2 = barrier((grad_projected, more_2))
    own_2, part_2 = sum_third(grad_2, came_2, more_2)
    grad_projected, part_2 = barrier((grad_projected, part_2))
    last_2 = send_parts(part_2, "a", sizes)
    grad_projected_pair = swapped(grad_projected, sizes)
    grad_rows, grad_gain_one, grad_router = project_back(
        grad_projected, w_qkv, picked, gain_one, router, grad_first, dr_second + dr_first
    )
    grad_small = jnp.concatenate([grad_router, grad_gain_one, grad_gain_two, jnp.zeros((SMALL - 3, width), f32)])
    small_pair = swapped(grad_small, sizes)
    came_1, small_pair, grad_projected_pair = barrier((came_1, small_pair, grad_projected_pair))
    more_1 = sum_second(grad_1, came_1)
    grad_small = columns_of(small_pair[0] + small_pair[1], pos[1], sizes).T.reshape(-1, rows, SMALL)
    more_1, grad_small = barrier((more_1, grad_small))
    more_1 = send_second(more_1, sizes)
    half = 2 * width - width // 3
    jobs = [(0, 0, 0, width, 0, 0), (0, 0, width, half - width, 0, width), (0, 0, half, 2 * width - half, 1, 0), (0, 0, 2 * width, width, 1, 2 * width - half)]
    shapes = ((rows, half), (rows, 3 * width - half + SMALL))
    grad_0 = make([hidden_one_pair], [grad_projected_pair], jobs, shapes, pos, sizes, (grad_small, 1, 3 * width - half))
    grad_0, second, last_2, more_1 = barrier((grad_0, second, last_2, more_1))
    came_0 = sum_first(grad_0, sizes)
    own_1, part_1 = sum_third(grad_1, came_1, more_1)
    part_1, second = barrier((part_1, second))
    last_1 = send_parts(part_1, "a", sizes)

    shape = (seqs, capacity, width)
    block_out = jnp.where(is_routed[:, :, None], low(dot(pick, second.reshape(shape), "sct,scd->std")), tokens)
    came_0, grad_rows, block_out = barrier((came_0, grad_rows, block_out))
    more_0 = sum_second(grad_0, came_0)
    more_0, grad_rows = barrier((more_0, grad_rows))
    more_0 = send_second(more_0, sizes)
    tokens_grad = jnp.where(is_routed[:, :, None], low(dot(pick, grad_rows.reshape(shape), "sct,scd->std")), cotangent)
    more_0, tokens_grad = barrier((more_0, tokens_grad))
    own_0, part_0 = sum_third(grad_0, came_0, more_0)
    part_0, last_1 = barrier((part_0, last_1))
    last_0 = send_parts(part_0, "a", sizes)
    sum_down = add_up(own_2, last_2)
    sum_rest = add_up(own_1, last_1)
    sum_up, sum_out = sum_rest[:, :hidden], sum_rest[:, hidden:]
    sum_first_ones = add_up(own_0, last_0)

    grads = (
        jnp.stack([sum_first_ones[:, i * width : (i + 1) * width] for i in range(3)]),
        sum_out,
        sum_up,
        sum_down,
        sum_first_ones[:, 3 * width],
        sum_first_ones[:, 3 * width + 1 : 3 * width + 3].T,
    )
    decays = (decay_rate, decay_rate, decay_rate, decay_rate, 0.0, 0.0)
    results = [block_out, tokens_grad]
    for state, grad, decay, rate in zip(states, grads, decays, learn_rates):
        results = results + adamw(state, grad, decay, rate)
    return tuple(results)


def solution(mesh):
    lead = mesh.shape["dp"] // 2
    inner = mesh.shape["fsdp"] // 4
    names = ("y", "c", "a", "b")
    fine = Mesh(mesh.devices.reshape(lead, 2, 4, inner), names)
    sizes = dict(zip(names, (lead, 2, 4, inner)))
    head, second, only = P(names, None, None), P(None, names, None), P(names, None)
    weights = (second,) * 4 + (only,) * 12 + (P(names),) * 4 + (P(None, names),) * 4
    return jax.shard_map(
        functools.partial(body, sizes),
        mesh=fine,
        in_specs=(head, head, only, only) + weights,
        out_specs=(head, head) + weights,
        check_vma=False,
    )
```

```python
import functools
import math

import jax
import jax.numpy as jnp
from jax import lax
from jax.experimental import pallas as pl
from jax.experimental.pallas import tpu as pltpu
from jax.sharding import Mesh, PartitionSpec as P

HEADS = 12
SMALL = 128

norm_eps = 1e-06
learn_rates = (0.03, 0.1, 0.03, 0.02, 0.03, 0.2)
beta_first = 0.5
beta_second = 0.5
adam_eps = 1e-08
decay_rate = 0.1
average_rate = 0.7
exact_mode = lax.Precision.HIGHEST
f32 = jnp.float32
bf16 = jnp.bfloat16


def shifted(value, axis, sizes, step):
    n = sizes[axis]
    return lax.ppermute(value, axis, [(i, (i + step) % n) for i in range(n)])


def after(value, *others):
    return lax.optimization_barrier((value, others))[0]


def paired(value, step, sizes):
    return lax.ppermute(value, "a", [(i, i ^ step) for i in range(sizes["a"])])


def hold(lists, *others):
    came, others = lax.optimization_barrier(([v[1:] for v in lists], others))
    return ([v[:1] + c for v, c in zip(lists, came)],) + others


def gather_axis(value, axis, sizes):
    return [value] + [shifted(value, axis, sizes, k) for k in range(1, sizes[axis])]


def halves_of(value):
    half = len(value) // 2
    return value[:half], value[half:]


def go_second(halves, sizes):
    return gather_axis(halves[0], "b", sizes), gather_axis(halves[1], "y", sizes)


def go_third(halves, sizes):
    return gather_axis(halves[0], "y", sizes), gather_axis(halves[1], "b", sizes)


def stacked(lists):
    arrays = [v for some in lists for v in some]

    def kernel(*refs):
        at = 0
        for out, some in zip(refs[len(arrays) :], lists):
            for k in range(len(some)):
                out[k] = refs[at + k][...]
            at += len(some)

    return whole("stacked", kernel, [jax.ShapeDtypeStruct((len(v),) + v[0].shape, v[0].dtype) for v in lists], arrays)


def to_core(lists, sizes):
    return [[shifted(v, "c", sizes, 1) for v in some] for some in lists]


def joined(lists, early, late):
    return lists[0] + lists[1], early[0] + late[0] + early[1] + late[1]


def take(value, index, axis):
    return lax.dynamic_index_in_dim(value, index, axis, keepdims=False)


def columns_of(value, core, sizes):
    ny = sizes["y"]
    chunk = value.shape[1] // (2 * ny)
    return jnp.concatenate([lax.dynamic_slice_in_dim(value, (2 * y + core) * chunk, chunk, 1) for y in range(ny)], axis=1)


def swapped(value, sizes):
    return [value, shifted(value, "c", sizes, 1)]


def add_up(own, came):
    own = own.astype(f32)
    for part in came:
        own = own + part.astype(f32)
    return own


def send_parts(parts, axis, sizes):
    return [shifted(parts[k].astype(bf16), axis, sizes, k + 1) for k in range(sizes[axis] - 1)]


def sum_first(grad, sizes):
    return send_parts(grad[1], "b", sizes), send_parts(grad[3], "y", sizes)


def sum_core(own, came):
    ins = [own[0], came[0], own[1], came[1]]
    shapes = [w for v in own for w in (v.shape[1:], (v.shape[0] - 1,) + v.shape[1:])]

    def kernel(*refs):
        outs = refs[len(ins) :]
        for i in range(2):
            for k in range(own[i].shape[0]):
                total = (refs[2 * i][k].astype(f32) + refs[2 * i + 1][k].astype(f32)).astype(bf16)
                if k == 0:
                    outs[2 * i][...] = total
                else:
                    outs[2 * i + 1][k - 1] = total

    return whole("sum_core", kernel, [jax.ShapeDtypeStruct(v, bf16) for v in shapes], ins)


def sum_second(grads, cames):
    count = len(grads)
    ins = [v for grad, came in zip(grads, cames) for v in [grad[0]] + came[0] + [grad[2]] + came[1]]
    counts = 1 + len(cames[0][0]), 1 + len(cames[0][1])
    shapes = [(grads[0][i].shape[0] - 1, count) + grads[0][i].shape[1:] for i in (0, 2)]

    def kernel(*refs):
        outs, at = refs[len(ins) :], 0
        for n in range(count):
            for out, some in zip(outs, counts):
                for k in range(out.shape[0]):
                    total = refs[at][k + 1].astype(f32)
                    for ref in refs[at + 1 : at + some]:
                        total += ref[k + 1].astype(f32)
                    out[k, n] = total.astype(bf16)
                at += some

    return whole("sum_second", kernel, [jax.ShapeDtypeStruct(v, bf16) for v in shapes], ins)


def sum_third(grads, cames, more):
    count = len(grads)
    ins = [v for grad, came in zip(grads, cames) for v in [grad[0]] + came[0] + [grad[2]] + came[1]] + more[0] + more[1]
    counts = 1 + len(cames[0][0]), 1 + len(cames[0][1])
    na, rows, width = grads[0][0].shape[1:]
    cuts = (0, width), (width, width + grads[0][2].shape[-1])

    def kernel(*refs):
        outs, at, late = refs[len(ins) :], 0, sum(counts) * count
        for n in range(count):
            for part, (some, (start, stop)) in enumerate(zip(counts, cuts)):
                first = late + (len(more[0]) if part else 0)
                for k in range(na):
                    total = refs[at][0, k].astype(f32)
                    for ref in refs[at + 1 : at + some]:
                        total += ref[0, k].astype(f32)
                    for ref in refs[first : first + len(more[part])]:
                        total += ref[n, k].astype(f32)
                    outs[k][n * rows : (n + 1) * rows, start:stop] = total.astype(outs[k].dtype)
                at += some

    shape = count * rows, cuts[1][1]
    outs = whole("sum_third", kernel, [jax.ShapeDtypeStruct(shape, f32 if k == 0 else bf16) for k in range(na)], ins)
    return outs[0], list(outs[1:])


def send_second(parts, sizes):
    return send_parts(parts[0], "y", sizes), send_parts(parts[1], "b", sizes)


def places(sizes):
    half = sizes["a"] // 2
    out = []
    for kc in range(2):
        for ky in range(sizes["y"]):
            for kb in range(sizes["b"]):
                for ka in range(sizes["a"]):
                    part = 0 if ka < half else 1
                    out.append((kc, part, ky, kb, ka % half, (ky, kc, ka, kb)))
    return out


def owner(pos_ref, steps, sizes, crossed=False):
    ky, kc, ka, kb = steps
    y = lax.rem(pos_ref[0] + (sizes["y"] - ky), sizes["y"])
    c = lax.rem(pos_ref[1] + (2 - kc), 2)
    half = sizes["a"] // 2
    a = pos_ref[2] ^ (ka // half + 2 * (ka % half)) if crossed else lax.rem(pos_ref[2] + (sizes["a"] - ka), sizes["a"])
    b = lax.rem(pos_ref[3] + (sizes["b"] - kb), sizes["b"])
    return ((y * 2 + c) * sizes["a"] + a) * sizes["b"] + b


COST = 100


def source(ins, block, sizes):
    kc, part, ky, kb, ka, _ = block
    base = kc * (sizes["y"] + sizes["b"])
    return ins[base + ky][kb, ka] if part == 0 else ins[base + sizes["y"] + kb][ky, ka]


def assemble(here, there, pos, sizes, cuts, fold=1, crossed=False):
    rows = here[0].shape[-2]
    devices = 2 * sizes["y"] * sizes["b"] * sizes["a"]
    sources = here + there
    blocks = places(sizes)

    def kernel(pos_ref, *refs):
        ins, outs = refs[: len(sources)], refs[len(sources) :]
        for block in blocks:
            where = owner(pos_ref, block[-1], sizes, crossed)
            value = source(ins, block, sizes)
            for i, (start, width) in enumerate(cuts):
                if fold == 1:
                    outs[i][where] = value[:, start : start + width]
                else:
                    outs[0][where * fold + i] = value[:, start : start + width]

    shapes = [jax.ShapeDtypeStruct((devices, rows, width), bf16) for _, width in cuts]
    if fold > 1:
        shapes = [jax.ShapeDtypeStruct((devices * fold, rows, cuts[0][1]), bf16)]
    vmem = pl.BlockSpec(memory_space=pltpu.VMEM)
    return pl.pallas_call(
        kernel,
        out_shape=shapes,
        in_specs=[pl.BlockSpec(memory_space=pltpu.SMEM)] + [vmem] * len(sources),
        out_specs=[vmem] * len(shapes),
        name="assemble",
        **params(2 * mib(*sources) + 3, 0, 4 * devices * rows * sum(w for _, w in cuts)),
    )(pos, *sources)


def adamw(state, grad, decay, rate):
    weight, mean, square, average = state
    mean_next = beta_first * mean + (1.0 - beta_first) * grad
    square_next = beta_second * square + (1.0 - beta_second) * grad * grad
    update = mean_next / (jnp.sqrt(square_next) + adam_eps)
    weight_next = weight - rate * (update + decay * weight)
    average_next = average_rate * average + (1.0 - average_rate) * weight_next
    return [weight_next, mean_next, square_next, average_next]


def dot(a, b, spec):
    return jnp.einsum(spec, a, b, preferred_element_type=f32)


NT = (((1,), (1,)), ((), ()))
TN = (((0,), (0,)), ((), ()))
NN = (((1,), (0,)), ((), ()))


def mm(a, b, dims):
    return lax.dot_general(a, b, dims, preferred_element_type=f32)


def only(own, value):
    return jnp.where(own, value, 0.0).astype(bf16)


def heads_of(n):
    lane = lax.broadcasted_iota(jnp.int32, (n, 128), 1)
    return lane < 64, lane >= 64


def same_segment(segs_ref, n):
    row = segs_ref[pl.ds(pl.program_id(0), 1), :]
    return jnp.broadcast_to(row, (8, n)).T[:, :1] == row


def attend_kernel(scale, segs_ref, qkv_ref, out_ref):
    n, width = out_ref.shape
    query = lax.broadcasted_iota(jnp.int32, (n, n), 0)
    key = lax.broadcasted_iota(jnp.int32, (n, n), 1)
    allowed = same_segment(segs_ref, n) & (key <= query)
    for p in range(width // 128):
        q2, k2, v2 = (qkv_ref[:, i * width + p * 128 : i * width + (p + 1) * 128] for i in range(3))
        total = jnp.zeros((n, 128), f32)
        for own in heads_of(n):
            logits = jnp.where(allowed, mm(only(own, q2 * scale), k2, NT), -1e30)
            exponent = jnp.exp(logits - jnp.max(logits, axis=-1, keepdims=True))
            probs = exponent * (1.0 / jnp.sum(exponent, axis=-1, keepdims=True))
            total += mm(probs.astype(bf16), only(own, v2), NN)
        out_ref[:, p * 128 : (p + 1) * 128] = total.astype(bf16)


def attend_back_kernel(scale, segs_ref, qkv_ref, grad_ref, out_ref):
    n, width = grad_ref.shape
    key = lax.broadcasted_iota(jnp.int32, (n, n), 0)
    query = lax.broadcasted_iota(jnp.int32, (n, n), 1)
    allowed = same_segment(segs_ref, n) & (key <= query)
    for p in range(width // 128):
        q2, k2, v2 = (qkv_ref[:, i * width + p * 128 : i * width + (p + 1) * 128] for i in range(3))
        g2 = grad_ref[:, p * 128 : (p + 1) * 128]
        grads = [jnp.zeros((n, 128), f32) for _ in range(3)]
        for own in heads_of(n):
            q_own, g_own = only(own, q2 * scale), only(own, g2)
            logits = jnp.where(allowed, mm(k2, q_own, NT), -1e30)
            exponent = jnp.exp(logits - jnp.max(logits, axis=0, keepdims=True))
            probs = exponent * (1.0 / jnp.sum(exponent, axis=0, keepdims=True))
            grad_probs = mm(v2, g_own, NT)
            inner = jnp.sum(probs * grad_probs, axis=0, keepdims=True)
            grad_logits = (probs * (grad_probs - inner)).astype(bf16)
            grads[0] += mm(grad_logits, only(own, k2 * scale), TN)
            grads[1] += mm(grad_logits, q_own, NN)
            grads[2] += mm(probs.astype(bf16), g_own, NN)
        for i in range(3):
            out_ref[:, i * width + p * 128 : i * width + (p + 1) * 128] = grads[i].astype(bf16)


def attention(kernel, segs, scale, qkv, *more):
    seqs, n = segs.shape
    width = qkv.shape[1] // 3
    out_width = 3 * width if more else width
    rows = lambda w: pl.BlockSpec((n, w), lambda s: (s, 0))
    matmuls = (5 if more else 2) * 2 * seqs * n * n * width
    return pl.pallas_call(
        functools.partial(kernel, scale),
        grid=(seqs,),
        out_shape=jax.ShapeDtypeStruct((seqs * n, out_width), bf16),
        in_specs=[full((seqs, n)), rows(3 * width)]
        + [rows(width)] * len(more),
        out_specs=rows(out_width),
        name="attention_backward" if more else "attention",
        **params(8, 10 * matmuls, 2 * seqs * n * (3 * width + out_width), seqs * HEADS * n * n),
    )(segs, qkv, *more)


def full(shape):
    return pl.BlockSpec(shape, lambda *_: (0,) * len(shape))


def params(room, flops, moved, transcendentals=0):
    return dict(
        compiler_params=pltpu.CompilerParams(vmem_limit_bytes=int(room * 2**20)),
        cost_estimate=pl.CostEstimate(flops=flops // COST, transcendentals=transcendentals // COST, bytes_accessed=moved // COST),
    )


def mib(*shapes):
    return sum(math.prod(v.shape) * v.dtype.itemsize for v in shapes) / 2**20


def whole(name, kernel, shapes, arrays, flops=0, more=0, scratch=()):
    vmem = pl.BlockSpec(memory_space=pltpu.VMEM)
    return pl.pallas_call(
        kernel,
        out_shape=shapes,
        in_specs=[vmem] * len(arrays),
        out_specs=[vmem] * len(shapes),
        scratch_shapes=[pltpu.VMEM(v.shape, v.dtype) for v in scratch],
        name=name,
        **params(1.2 * mib(*arrays, *shapes, *scratch) + 4 + more, flops, sum(v.size for v in arrays) * 4),
    )(*arrays)


def pack(qkv, router, gains):
    rows, width = qkv.shape[1:]
    if rows % 8:
        small = jnp.concatenate([router.T, gains.T, jnp.zeros((rows, SMALL - 3), f32)], axis=1)
        return jnp.concatenate([qkv[0], qkv[1], qkv[2], small], axis=1).astype(bf16)

    def kernel(qkv_ref, router_ref, gains_ref, out_ref, turn_ref):
        for i in range(3):
            out_ref[:, i * width : (i + 1) * width] = qkv_ref[i].astype(bf16)
        turn_ref[...] = jnp.zeros_like(turn_ref)
        turn_ref[0:1, :rows] = router_ref[...]
        turn_ref[1:3, :rows] = gains_ref[...]
        out_ref[:, 3 * width :] = turn_ref[...].T[:rows].astype(bf16)

    out = [jax.ShapeDtypeStruct((rows, 3 * width + SMALL), bf16)]
    return whole("pack", kernel, out, [qkv, router, gains], scratch=[jax.ShapeDtypeStruct((SMALL, SMALL), f32)])[0]


def pack_rest(out, up, down):
    rows, width = out.shape
    hidden, fold = up.shape[1], down.shape[0] // rows
    if rows % 8:
        folded = [down[i * rows : (i + 1) * rows] for i in range(fold)]
        return jnp.concatenate([out, up], axis=1).astype(bf16), jnp.concatenate(folded, axis=1).astype(bf16)

    def kernel(out_ref, up_ref, down_ref, first_ref, second_ref):
        first_ref[:, :width] = out_ref[...].astype(bf16)
        first_ref[:, width:] = up_ref[...].astype(bf16)
        for i in range(fold):
            second_ref[:, i * width : (i + 1) * width] = down_ref[i * rows : (i + 1) * rows].astype(bf16)

    return whole("pack_rest", kernel, [jax.ShapeDtypeStruct((rows, width + hidden), bf16), jax.ShapeDtypeStruct((rows, fold * width), bf16)], [out, up, down])


def project(picked, back_cot, w_qkv, w_small):
    count, width = picked.shape

    def kernel(picked_ref, cot_ref, w_ref, small_ref, hidden_ref, out_ref, score_ref, rows_ref, back_ref):
        @pl.when(pl.program_id(0) == 0)
        def _():
            rows = small_ref[:, :128].astype(f32).T[:8]
            rows_ref[...] = rows
            value = picked_ref[...].astype(f32)
            score = mm(picked_ref[...], small_ref[:, :128], NN)[:, :1]
            score_ref[...] = score
            back_ref[...] = (score * cot_ref[...].astype(f32)).astype(bf16)
            hidden_ref[...] = (value * norm_of(value) * rows[1:2]).astype(bf16)

        out_ref[...] = mm(hidden_ref[...], w_ref[...], NN).astype(bf16)

    one = full((count, width))
    return pl.pallas_call(
        kernel,
        grid=(3,),
        out_shape=[jax.ShapeDtypeStruct((count, width), bf16), jax.ShapeDtypeStruct((count, 3 * width), bf16)]
        + [jax.ShapeDtypeStruct((count, 1), f32), jax.ShapeDtypeStruct((8, width), f32), jax.ShapeDtypeStruct((count, width), bf16)],
        in_specs=[one, one, pl.BlockSpec((width, width), lambda j: (0, j)), full(w_small.shape)],
        out_specs=[one, pl.BlockSpec((count, width), lambda j: (0, j)), full((count, 1)), full((8, width)), one],
        name="project",
        **params(13, 6 * count * width * width, 6 * width * width),
    )(picked, back_cot, w_qkv, w_small)


def devices_of(pos, steps, sizes):
    y, c, a, b = (lax.rem(pos[i] + steps[i], n) for i, n in enumerate((sizes["y"], 2, sizes["a"], sizes["b"])))
    return y, c, a, b


def weight_grad(left, right, jobs, shape, rows, pos, sizes):
    ny, na, nb = sizes["y"], sizes["a"], sizes["b"]
    blocks = ny * na * nb
    count, wide = left[0].shape[0], max(job[1] for job in jobs)

    def kernel(pos_ref, left_ref, left_other, right_ref, right_other, *refs):
        outs, acc, turned = refs[:4], refs[4], refs[5]
        chunk = na * nb * rows

        def columns(ref, y):
            if chunk % 128 == 0:
                return ref[:, pl.ds(pl.multiple_of((2 * y + pos_ref[1]) * chunk, 128), chunk)]
            both = ref[:, 2 * y * chunk : 2 * (y + 1) * chunk]
            return jnp.where(pos_ref[1] == 0, both[:, :chunk], both[:, chunk:])

        for side, ref in enumerate((left_ref, left_other)):
            for y in range(ny):
                turned[side, y * chunk : (y + 1) * chunk, :] = columns(ref, y).T
        for start, width, spots in jobs:
            total = mm(turned[0], right_ref[:, start : start + width], NN)
            total += mm(turned[1], right_other[:, start : start + width], NN)
            acc[:, :, :width] = total.reshape(blocks, rows, width)
            for ky in range(ny):
                for ka in range(na):
                    for kb in range(nb):
                        y, _, a, b = devices_of(pos_ref, (ky, 0, ka, kb), sizes)
                        value = acc[(y * na + a) * nb + b, :, :width].astype(bf16)
                        for column, some, part, row, to in spots:
                            if part == 0:
                                ref = outs[0].at[ky, ka] if kb == 0 else outs[1].at[kb - 1, ky, ka]
                            else:
                                ref = outs[2].at[kb, ka] if ky == 0 else outs[3].at[ky - 1, kb, ka]
                            ref[row : row + rows, to : to + some] = value[:, column : column + some]

    leads = [(ny, na), (nb - 1, ny, na), (nb, na), (ny - 1, nb, na)]
    outs = [jax.ShapeDtypeStruct(v + shape, bf16) for v in leads]
    scratch = [jax.ShapeDtypeStruct((blocks, rows, wide), f32), jax.ShapeDtypeStruct((2, blocks * rows, count), bf16)]
    vmem = pl.BlockSpec(memory_space=pltpu.VMEM)
    arrays = list(left) + list(right)
    return pl.pallas_call(
        kernel,
        out_shape=outs,
        in_specs=[pl.BlockSpec(memory_space=pltpu.SMEM)] + [vmem] * 4,
        out_specs=[vmem] * 4,
        scratch_shapes=[pltpu.VMEM(v.shape, v.dtype) for v in scratch],
        name="weight_grad",
        **params(mib(*arrays, *outs, *scratch) * 1.1 + 8, 4 * count * blocks * rows * right[0].shape[1], sum(v.size for v in arrays) * 2),
    )(pos, *arrays)


def weight_grad_plain(left, right, jobs, shape, rows, pos, sizes):
    ny, na, nb = sizes["y"], sizes["a"], sizes["b"]
    left = [columns_of(v, pos[1], sizes) for v in left]
    total = sum(dot(a, b, "rd,re->de") for a, b in zip(left, right)).astype(bf16).reshape(ny, na, nb, rows, -1)
    for axis, at in ((0, 0), (1, 2), (2, 3)):
        total = jnp.roll(total, -pos[at], axis)
    done = [jnp.zeros((ny, na, nb) + shape, bf16) for _ in range(2)]
    for start, _, spots in jobs:
        for column, some, part, row, to in spots:
            done[part] = done[part].at[..., row : row + rows, to : to + some].set(total[..., start + column : start + column + some])
    first, second = done[0].transpose(2, 0, 1, 3, 4), done[1].transpose(0, 2, 1, 3, 4)
    return first[0], first[1:], second[0], second[1:]


def weight_grad_own(lefts, rights, narrow, halves, pos, sizes):
    ny, na, nb = sizes["y"], sizes["a"], sizes["b"]
    blocks = 2 * ny * na * nb
    count, model = lefts[0].shape
    rows = model // blocks
    wide = max(w for part in halves for _, _, w in part)
    leads = [(nb, ny, na), (ny, nb, na)]
    shapes = [v + (rows, sum(w for _, _, w in part)) for v, part in zip(leads, halves)]
    if rows % 8:
        return weight_grad_own_plain(lefts, rights, narrow, halves, pos, sizes)

    def kernel(pos_ref, *refs):
        ins, outs, acc, turned = refs[: 2 * len(lefts) + 1], refs[2 * len(lefts) + 1 : -2], refs[-2], refs[-1]
        for i in range(len(lefts)):
            turned[i] = ins[i][...].T
        for part, some in enumerate(halves):
            to = 0
            for i, start, width in some:
                if i < 0:
                    value = ins[-1][...]
                    total = jnp.concatenate([value, jnp.zeros((width - value.shape[0], model), f32)]).T
                else:
                    total = mm(turned[i], ins[len(lefts) + i][:, start : start + width], NN)
                acc[:, :, :width] = total.reshape(blocks, rows, width)
                for kc in range(2):
                    for ky in range(ny):
                        for ka in range(na):
                            for kb in range(nb):
                                y, c, a, b = devices_of(pos_ref, (ky, kc, ka, kb), sizes)
                                ref = outs[2 * kc + part]
                                ref = ref.at[kb, ky, ka] if part == 0 else ref.at[ky, kb, ka]
                                ref[:, to : to + width] = acc[((y * 2 + c) * na + a) * nb + b, :, :width].astype(bf16)
                to += width

    outs = [jax.ShapeDtypeStruct(v, bf16) for v in shapes] * 2
    scratch = [jax.ShapeDtypeStruct((blocks, rows, wide), f32), jax.ShapeDtypeStruct((len(lefts), model, count), bf16)]
    vmem = pl.BlockSpec(memory_space=pltpu.VMEM)
    arrays = list(lefts) + list(rights) + [narrow]
    done = pl.pallas_call(
        kernel,
        out_shape=outs,
        in_specs=[pl.BlockSpec(memory_space=pltpu.SMEM)] + [vmem] * len(arrays),
        out_specs=[vmem] * 4,
        scratch_shapes=[pltpu.VMEM(v.shape, v.dtype) for v in scratch],
        name="weight_grad_own",
        **params(mib(*arrays, *outs, *scratch) * 1.1 + 8, 2 * count * model * sum(v.shape[1] for v in rights), sum(v.size for v in arrays) * 2),
    )(pos, *arrays)
    return done[:2], done[2:]


def weight_grad_own_plain(lefts, rights, narrow, halves, pos, sizes):
    ny, na, nb = sizes["y"], sizes["a"], sizes["b"]
    done = []
    for part in halves:
        pieces = []
        for i, start, width in part:
            if i < 0:
                pieces.append(jnp.pad(narrow.T, ((0, 0), (0, width - narrow.shape[0]))))
            else:
                pieces.append(dot(lefts[i], rights[i][:, start : start + width], "rd,re->de"))
        total = jnp.concatenate(pieces, axis=1).astype(bf16)
        total = total.reshape(ny, 2, na, nb, -1, total.shape[1])
        for axis in range(4):
            total = jnp.roll(total, -pos[axis], axis)
        done.append(total)
    return [(done[0][:, kc].transpose(2, 0, 1, 3, 4), done[1][:, kc].transpose(0, 2, 1, 3, 4)) for kc in range(2)]


def norm_of(value):
    return lax.rsqrt(jnp.mean(value * value, axis=-1, keepdims=True) + norm_eps)


def feed_forward(mixed, picked, score, gain, w_both):
    count, width = picked.shape
    steps = w_both.shape[1] // width

    def kernel(mixed_ref, picked_ref, score_ref, gain_ref, w_ref, attended_ref, first_ref, hidden_ref, activ_ref, slope_ref):
        @pl.when(pl.program_id(0) == 0)
        def _():
            attended = mm(mixed_ref[...], w_ref[...], NN)
            first = picked_ref[...].astype(f32) + score_ref[...] * attended
            attended_ref[...] = attended
            first_ref[...] = first
            hidden_ref[...] = (first * norm_of(first) * gain_ref[2:3, :]).astype(bf16)

        @pl.when(pl.program_id(0) > 0)
        def _():
            v = mm(hidden_ref[...], w_ref[...], NN)
            c0 = (2.0 / jnp.pi) ** 0.5
            square = v * v
            t = jnp.tanh(c0 * (v + 0.044715 * (square * v)))
            cdf = 0.5 * (1.0 + t)
            activ_ref[...] = (v * cdf).astype(bf16)
            slope_ref[...] = cdf + (0.5 * v) * (1.0 - t * t) * (c0 + (3.0 * 0.044715 * c0) * square)

    later = lambda j: (0, jnp.maximum(j - 1, 0))
    return pl.pallas_call(
        kernel,
        grid=(steps,),
        out_shape=[jax.ShapeDtypeStruct((count, width), d) for d in (f32, f32, bf16)]
        + [jax.ShapeDtypeStruct((count, (steps - 1) * width), d) for d in (bf16, f32)],
        in_specs=[full((count, width)), full((count, width)), full((count, 1)), full((8, width)), pl.BlockSpec((width, width), lambda j: (0, j))],
        out_specs=[full((count, width))] * 3 + [pl.BlockSpec((count, width), later)] * 2,
        name="feed_forward",
        **params(18, 2 * count * width * width * steps, 2 * width * width * steps + 10 * count * width + 6 * count * width * steps, count * width * steps),
    )(mixed, picked, score, gain, w_both)


def down_both(activ, slope, grad_out, w_down, first, score, back_cot):
    count, width = first.shape
    steps = activ.shape[1] // width

    def kernel(activ_ref, slope_ref, grad_ref, w_ref, first_ref, score_ref, cot_ref, pre_ref, second_ref, dr_ref, acc_ref):
        j = pl.program_id(0)
        pre_ref[...] = (mm(grad_ref[...], w_ref[...], NT) * slope_ref[...]).astype(bf16)
        out = mm(activ_ref[...], w_ref[...], NN)

        @pl.when(j == 0)
        def _():
            acc_ref[...] = out

        @pl.when(j > 0)
        def _():
            acc_ref[...] += out

        @pl.when(j == steps - 1)
        def _():
            total = acc_ref[...]
            second_ref[...] = (first_ref[...] + score_ref[...] * total).astype(bf16)
            dr_ref[...] = jnp.sum(cot_ref[...].astype(f32) * total, axis=-1, keepdims=True)

    tile = pl.BlockSpec((count, width), lambda j: (0, j))
    one = full((count, width))
    return pl.pallas_call(
        kernel,
        grid=(steps,),
        out_shape=[jax.ShapeDtypeStruct(activ.shape, bf16), jax.ShapeDtypeStruct((count, width), bf16), jax.ShapeDtypeStruct((count, 1), f32)],
        in_specs=[tile, tile, one, pl.BlockSpec((width, width), lambda j: (j, 0)), one, full((count, 1)), one],
        out_specs=[tile, one, full((count, 1))],
        scratch_shapes=[pltpu.VMEM((count, width), f32)],
        name="down_both",
        **params(18, 4 * count * width * width * steps, 2 * width * width * steps + 8 * count * width * steps + 10 * count * width),
    )(activ, slope, grad_out, w_down, first, score, back_cot)


def back_of_norm(grad, value, gain):
    inv = norm_of(value)
    normed = value * inv
    scaled = grad * gain
    mean = jnp.mean(scaled * normed, axis=-1, keepdims=True)
    return (scaled - normed * mean) * inv, jnp.sum(grad * normed, axis=0, keepdims=True)


def up_back(grad_pre, w_both, first, attended, score, back_cot, gain):
    count, width = first.shape
    steps = w_both.shape[1] // width

    def kernel(pre_ref, w_ref, first_ref, attended_ref, score_ref, cot_ref, gain_ref, out_ref, low_ref, mixed_ref, dr_ref, dgain_ref, acc_ref):
        j = pl.program_id(0)

        @pl.when(j == 0)
        def _():
            acc_ref[...] = jnp.zeros_like(acc_ref)

        @pl.when(j < steps - 1)
        def _():
            acc_ref[...] += mm(pre_ref[...], w_ref[...], NT)

        @pl.when(j == steps - 1)
        def _():
            grad, dgain = back_of_norm(acc_ref[...], first_ref[...], gain_ref[2:3, :])
            grad = cot_ref[...].astype(f32) + grad
            low = (score_ref[...] * grad).astype(bf16)
            out_ref[...] = grad
            low_ref[...] = low
            dgain_ref[...] = dgain
            dr_ref[...] = jnp.sum(grad * attended_ref[...], axis=-1, keepdims=True)
            mixed_ref[...] = mm(low, w_ref[...], NT).astype(bf16)

    one = full((count, width))
    return pl.pallas_call(
        kernel,
        grid=(steps,),
        out_shape=[jax.ShapeDtypeStruct((count, width), d) for d in (f32, bf16, bf16)]
        + [jax.ShapeDtypeStruct((count, 1), f32), jax.ShapeDtypeStruct((1, width), f32)],
        in_specs=[
            pl.BlockSpec((count, width), lambda j: (0, jnp.minimum(j, steps - 2))),
            pl.BlockSpec((width, width), lambda j: (0, lax.rem(j + 1, steps))),
            one,
            one,
            full((count, 1)),
            one,
            full((8, width)),
        ],
        out_specs=[one, one, one, full((count, 1)), full((1, width))],
        scratch_shapes=[pltpu.VMEM((count, width), f32)],
        name="up_back",
        **params(18, 2 * count * width * width * steps, 2 * width * width * steps + 2 * count * width * steps + 18 * count * width),
    )(grad_pre, w_both, first, attended, score, back_cot, gain)


def project_back(grad_projected, w_qkv, picked, rows, grad_first, drs, dgain_two):
    count, width = picked.shape
    steps = 3

    def kernel(grad_ref, w_ref, picked_ref, rows_ref, first_ref, dr_ref, more_ref, two_ref, out_ref, narrow_ref, acc_ref):
        j = pl.program_id(0)

        @pl.when(j == 0)
        def _():
            acc_ref[...] = jnp.zeros_like(acc_ref)

        acc_ref[...] += mm(grad_ref[...], w_ref[...], NT)

        @pl.when(j == steps - 1)
        def _():
            value, dr = picked_ref[...].astype(f32), dr_ref[...] + more_ref[...]
            grad, dgain = back_of_norm(acc_ref[...], value, rows_ref[1:2, :])
            out_ref[...] = (first_ref[...] + grad + dr * rows_ref[0:1, :]).astype(bf16)
            drouter = jnp.sum(dr * value, axis=0, keepdims=True)
            narrow_ref[...] = jnp.concatenate([drouter, dgain, two_ref[...], jnp.zeros((5, width), f32)])

    one, row, column = full((count, width)), full((1, width)), full((count, 1))
    return pl.pallas_call(
        kernel,
        grid=(steps,),
        out_shape=[jax.ShapeDtypeStruct((count, width), bf16), jax.ShapeDtypeStruct((8, width), f32)],
        in_specs=[pl.BlockSpec((count, width), lambda j: (0, j)), pl.BlockSpec((width, width), lambda j: (0, j)), one, full((8, width)), one]
        + [column, column, row],
        out_specs=[one, full((8, width))],
        scratch_shapes=[pltpu.VMEM((count, width), f32)],
        name="project_back",
        **params(17, 2 * count * width * width * steps, 2 * width * width * steps + 2 * count * width * steps + 10 * count * width),
    )(grad_projected, w_qkv, picked, rows, grad_first, *drs, dgain_two)


def body(sizes, *args):
    tokens, cotangent, segment_ids, routed = args[:4]
    states = [args[4 + 4 * i : 8 + 4 * i] for i in range(6)]
    qkv_state, out_state, up_state, down_state, router_state, gains_state = states
    seqs, length, width = tokens.shape
    capacity = routed.shape[1]
    count = seqs * capacity
    rows = out_state[0].shape[0]
    hidden = up_state[0].shape[1]
    fold = down_state[0].shape[0] // rows
    scale = (width // HEADS) ** (-0.5)
    pos = jnp.stack([lax.axis_index(n) for n in ("y", "c", "a", "b")]).astype(jnp.int32)

    low = lambda v: v.astype(bf16)
    barrier = lax.optimization_barrier
    send_qkv = pack(after(qkv_state[0], pos), router_state[0][None, :], gains_state[0])
    way_qkv = gather_axis(send_qkv, "a", sizes)
    send_up, send_down = pack_rest(out_state[0], up_state[0], down_state[0])

    here = routed[:, :, None] == jnp.arange(length, dtype=jnp.int32)[None, None, :]
    pick = here.astype(bf16)
    is_routed = jnp.any(here, axis=1)
    picked = dot(pick, tokens, "sct,std->scd").astype(bf16).reshape(count, width)
    way_qkv = stacked(halves_of(after(way_qkv, picked)))
    way_qkv, send_up, send_down = barrier((way_qkv, send_up, send_down))
    way_qkv = go_second(way_qkv, sizes)
    far_up = paired(send_up, 2, sizes)
    back_cot = dot(pick, cotangent, "sct,std->scd").astype(bf16).reshape(count, width)
    segs = jnp.sum(jnp.where(here, segment_ids[:, None, :], 0), axis=-1).astype(f32)
    way_qkv, far_up, back_cot, segs = hold(way_qkv, far_up, back_cot, segs)
    way_qkv = stacked(way_qkv)
    (first_up,) = stacked([[send_up, far_up]])
    way_qkv, first_up = barrier((way_qkv, first_up))
    early = to_core([[v] for v in way_qkv], sizes)
    way_qkv = go_third(way_qkv, sizes)
    second_up = paired(first_up, 1, sizes)
    far_down = paired(send_down, 2, sizes)
    way_qkv, second_up, far_down = hold(way_qkv, second_up, far_down)
    (first_down,) = stacked([[send_down, far_down]])
    got = joined(way_qkv, early, to_core([v[1:] for v in way_qkv], sizes))
    way_up = go_second((first_up, second_up), sizes)
    second_down = paired(first_down, 1, sizes)

    w_qkv, w_small = assemble(*got, after(pos, first_down), sizes, [(0, 3 * width), (3 * width, SMALL)])
    w_qkv = w_qkv.reshape(width, 3 * width)
    hidden_one, projected, score, narrow, grad_down_out = project(picked, back_cot, w_qkv, w_small.reshape(width, SMALL))
    way_up, projected, second_down = hold(way_up, projected, second_down)
    way_up = stacked(way_up)
    projected, way_up = barrier((projected, way_up))
    way_down = go_second((first_down, second_down), sizes)
    early_up = to_core([[v] for v in way_up], sizes)
    way_up = go_third(way_up, sizes)
    mixed = attention(attend_kernel, segs, scale, projected)
    way_down, mixed = hold(way_down, mixed)
    way_down = stacked(way_down)
    mixed, way_down = barrier((mixed, way_down))
    early_down = to_core([[v] for v in way_down], sizes)
    way_down = go_third(way_down, sizes)
    way_up, mixed = hold(way_up, mixed)
    got_up = joined(way_up, early_up, to_core([v[1:] for v in way_up], sizes))
    grad_down_pair = swapped(grad_down_out, sizes)
    (grad_down_pair,), pos_up = hold([grad_down_pair], pos)
    (w_both,) = assemble(*got_up, pos_up, sizes, [(0, width + hidden)], crossed=True)
    w_both = w_both.reshape(width, width + hidden)
    attended, first, hidden_two, activ_low, slope = feed_forward(mixed, picked, score, narrow, w_both)

    way_down, activ_low = hold(way_down, activ_low)
    got_down = joined(way_down, early_down, to_core([v[1:] for v in way_down], sizes))
    activ_pair = swapped(after(activ_low, got_down), sizes)
    hidden_two_pair = swapped(hidden_two, sizes)
    (w_down,) = assemble(*got_down, pos, sizes, [(i * width, width) for i in range(fold)], fold, crossed=True)
    w_down = w_down.reshape(hidden, width)
    grad_pre, second, dr_second = down_both(activ_low, slope, grad_down_out, w_down, first, score, back_cot)

    (activ_pair, hidden_two_pair), grad_pre = hold([activ_pair, hidden_two_pair], grad_pre)
    grad_pre_pair = swapped(grad_pre, sizes)
    half = width // 2
    split = fold * rows
    make = weight_grad if rows % 8 == 0 else weight_grad_plain
    jobs = [(i * half, half, [(0, half, i, 0, 0)]) for i in range(2)]
    grad_2 = make(activ_pair, grad_down_pair, jobs, (split, half), split, pos, sizes)
    came_2 = sum_first(grad_2, sizes)
    grad_pre_pair = grad_pre_pair[:1] + after(grad_pre_pair[1:], grad_2)
    spot = lambda i: (i // fold, (i % fold) * rows, 0)
    jobs = [(i * width, width, [(0, half) + spot(2 * i), (half, half) + spot(2 * i + 1)]) for i in range(fold)]
    grad_1 = make(hidden_two_pair, grad_pre_pair, jobs, (split, half), rows, pos, sizes)
    came_1 = sum_first(grad_1, sizes)
    grad_pre = after(grad_pre, grad_1)
    grad_first, grad_attended, grad_mixed, dr_first, grad_gain_two = up_back(grad_pre, w_both, first, attended, score, back_cot, narrow)
    grad_projected = attention(attend_back_kernel, segs, scale, projected, after(grad_mixed, came_2))
    grad_projected, came_1, came_2 = barrier((grad_projected, came_1, came_2))
    more_12 = sum_second([grad_2, grad_1], [came_2, came_1])
    grad_projected, more_12 = barrier((grad_projected, more_12))
    more_12 = send_second(more_12, sizes)
    grad_rows, grad_narrow = project_back(
        grad_projected, w_qkv, picked, narrow, grad_first, (dr_second, dr_first), grad_gain_two
    )
    second, grad_narrow = barrier((second, grad_narrow))
    shape = (seqs, capacity, width)
    block_out = jnp.where(is_routed[:, :, None], low(dot(pick, second.reshape(shape), "sct,scd->std")), tokens)
    grad_narrow, block_out = barrier((grad_narrow, block_out))

    halves = [(0, 0, width), (0, width, width), (-1, 0, SMALL)], [(0, 2 * width, width), (1, 0, width)]
    own_0, other_0 = weight_grad_own([hidden_one, mixed], [grad_projected, grad_attended], grad_narrow, halves, pos, sizes)
    more_12, own_0, other_0 = barrier((more_12, own_0, other_0))
    own_12, part_12 = sum_third([grad_2, grad_1], [came_2, came_1], more_12)
    other_0, part_12 = barrier((other_0, part_12))
    last_12 = send_parts(part_12, "a", sizes)
    came_0 = [shifted(v, "c", sizes, 1) for v in other_0]
    grad_0 = sum_core(own_0, came_0)
    came_0 = sum_first(grad_0, sizes)
    more_0 = sum_second([grad_0], [came_0])
    more_0, grad_rows = barrier((more_0, grad_rows))
    more_0 = send_second(more_0, sizes)
    tokens_grad = jnp.where(is_routed[:, :, None], low(dot(pick, grad_rows.reshape(shape), "sct,scd->std")), cotangent)
    more_0, tokens_grad, last_12 = barrier((more_0, tokens_grad, last_12))
    own_0, part_0 = sum_third([grad_0], [came_0], more_0)
    last_0 = send_parts(part_0, "a", sizes)
    last_12 = after(last_12, part_0)
    total_12 = add_up(own_12, last_12)
    sum_down, folded = total_12[:split], total_12[split:]
    sum_up = jnp.concatenate([folded[i * rows : (i + 1) * rows, j * half : (j + 1) * half] for j in range(2) for i in range(fold)], axis=1)
    total = add_up(own_0, last_0)
    states[4], states[5] = after((states[4], states[5]), part_0)

    grads = (
        jnp.stack([total[:, start : start + width] for start in (0, width, 2 * width + SMALL)]),
        total[:, 3 * width + SMALL :],
        sum_up,
        sum_down,
        total[:, 2 * width],
        total[:, 2 * width + 1 : 2 * width + 3].T,
    )
    decays = (decay_rate, decay_rate, decay_rate, decay_rate, 0.0, 0.0)
    results = [block_out, tokens_grad]
    for state, grad, decay, rate in zip(states, grads, decays, learn_rates):
        results = results + adamw(state, grad, decay, rate)
    return tuple(results)


def solution(mesh):
    lead = mesh.shape["dp"] // 2
    inner = mesh.shape["fsdp"] // 4
    names = ("y", "c", "a", "b")
    fine = Mesh(mesh.devices.reshape(lead, 2, 4, inner), names)
    sizes = dict(zip(names, (lead, 2, 4, inner)))
    head, second, only = P(names, None, None), P(None, names, None), P(names, None)
    weights = (second,) * 4 + (only,) * 12 + (P(names),) * 4 + (P(None, names),) * 4
    return jax.shard_map(
        functools.partial(body, sizes),
        mesh=fine,
        in_specs=(head, head, only, only) + weights,
        out_specs=(head, head) + weights,
        check_vma=False,
    )
```

```python
import functools
import math

import jax
import jax.numpy as jnp
from jax import lax
from jax.experimental import pallas as pl
from jax.experimental.pallas import tpu as pltpu
from jax.sharding import Mesh, PartitionSpec as P

HEADS = 12
SMALL = 128

norm_eps = 1e-06
learn_rates = (0.03, 0.1, 0.03, 0.02, 0.03, 0.2)
beta_first = 0.5
beta_second = 0.5
adam_eps = 1e-08
decay_rate = 0.1
average_rate = 0.7
exact_mode = lax.Precision.HIGHEST
f32 = jnp.float32
bf16 = jnp.bfloat16


def shifted(value, axis, sizes, step):
    n = sizes[axis]
    return lax.ppermute(value, axis, [(i, (i + step) % n) for i in range(n)])


def after(value, *others):
    return lax.optimization_barrier((value, others))[0]


def paired(value, step, sizes):
    return lax.ppermute(value, "a", [(i, i ^ step) for i in range(sizes["a"])])


def hold(lists, *others):
    came, others = lax.optimization_barrier(([v[1:] for v in lists], others))
    return ([v[:1] + c for v, c in zip(lists, came)],) + others


def gather_axis(value, axis, sizes):
    return [value] + [shifted(value, axis, sizes, k) for k in range(1, sizes[axis])]


def halves_of(value):
    half = len(value) // 2
    return value[:half], value[half:]


def go_second(halves, sizes):
    return gather_axis(halves[0], "b", sizes), gather_axis(halves[1], "y", sizes)


def go_third(halves, sizes):
    return gather_axis(halves[0], "y", sizes), gather_axis(halves[1], "b", sizes)


def stacked(lists):
    arrays = [v for some in lists for v in some]

    def kernel(*refs):
        at = 0
        for out, some in zip(refs[len(arrays) :], lists):
            for k in range(len(some)):
                out[k] = refs[at + k][...]
            at += len(some)

    return whole("stacked", kernel, [jax.ShapeDtypeStruct((len(v),) + v[0].shape, v[0].dtype) for v in lists], arrays)


def to_core(lists, sizes):
    return [[shifted(v, "c", sizes, 1) for v in some] for some in lists]


def side_by_side(lists):
    def kernel(*refs):
        at = 0
        for out, some in zip(refs[-2:], lists):
            for k in range(len(some)):
                out[k] = refs[at][...]
                at += 1

    shapes = [jax.ShapeDtypeStruct((len(v),) + v[0].shape, bf16) for v in lists]
    return whole("side_by_side", kernel, shapes, lists[0] + lists[1])


def joined(lists, early, late):
    return lists[0] + lists[1], early[0] + late[0] + early[1] + late[1]


def take(value, index, axis):
    return lax.dynamic_index_in_dim(value, index, axis, keepdims=False)


def columns_of(value, core, sizes):
    ny = sizes["y"]
    chunk = value.shape[1] // (2 * ny)
    return jnp.concatenate([lax.dynamic_slice_in_dim(value, (2 * y + core) * chunk, chunk, 1) for y in range(ny)], axis=1)


def swapped(value, sizes):
    return [value, shifted(value, "c", sizes, 1)]


def add_up(own, came):
    own = own.astype(f32)
    for part in came:
        own = own + part.astype(f32)
    return own


def send_parts(parts, axis, sizes):
    return [shifted(parts[k].astype(bf16), axis, sizes, k + 1) for k in range(sizes[axis] - 1)]


def sum_first(grad, sizes):
    return send_parts(grad[1], "b", sizes), send_parts(grad[3], "y", sizes)


def sum_core(own, came):
    ins = [own[0], came[0], own[1], came[1]]
    shapes = [w for v in own for w in (v.shape[1:], (v.shape[0] - 1,) + v.shape[1:])]

    def kernel(*refs):
        outs = refs[len(ins) :]
        for i in range(2):
            for k in range(own[i].shape[0]):
                total = (refs[2 * i][k].astype(f32) + refs[2 * i + 1][k].astype(f32)).astype(bf16)
                if k == 0:
                    outs[2 * i][...] = total
                else:
                    outs[2 * i + 1][k - 1] = total

    return whole("sum_core", kernel, [jax.ShapeDtypeStruct(v, bf16) for v in shapes], ins)


def sum_second(grads, cames):
    count = len(grads)
    ins = [v for grad, came in zip(grads, cames) for v in [grad[0]] + came[0] + [grad[2]] + came[1]]
    counts = 1 + len(cames[0][0]), 1 + len(cames[0][1])
    shapes = [(grads[0][i].shape[0] - 1, count) + grads[0][i].shape[1:] for i in (0, 2)]

    def kernel(*refs):
        outs, at = refs[len(ins) :], 0
        for n in range(count):
            for out, some in zip(outs, counts):
                for k in range(out.shape[0]):
                    total = refs[at][k + 1].astype(f32)
                    for ref in refs[at + 1 : at + some]:
                        total += ref[k + 1].astype(f32)
                    out[k, n] = total.astype(bf16)
                at += some

    return whole("sum_second", kernel, [jax.ShapeDtypeStruct(v, bf16) for v in shapes], ins)


def sum_third(grads, cames, more):
    count = len(grads)
    ins = [v for grad, came in zip(grads, cames) for v in [grad[0]] + came[0] + [grad[2]] + came[1]] + more[0] + more[1]
    counts = 1 + len(cames[0][0]), 1 + len(cames[0][1])
    na, rows, width = grads[0][0].shape[1:]
    cuts = (0, width), (width, width + grads[0][2].shape[-1])

    def kernel(*refs):
        outs, at, late = refs[len(ins) :], 0, sum(counts) * count
        for n in range(count):
            for part, (some, (start, stop)) in enumerate(zip(counts, cuts)):
                first = late + (len(more[0]) if part else 0)
                for k in range(na):
                    total = refs[at][0, k].astype(f32)
                    for ref in refs[at + 1 : at + some]:
                        total += ref[0, k].astype(f32)
                    for ref in refs[first : first + len(more[part])]:
                        total += ref[n, k].astype(f32)
                    outs[k][n * rows : (n + 1) * rows, start:stop] = total.astype(outs[k].dtype)
                at += some

    shape = count * rows, cuts[1][1]
    outs = whole("sum_third", kernel, [jax.ShapeDtypeStruct(shape, f32 if k == 0 else bf16) for k in range(na)], ins)
    return outs[0], list(outs[1:])


def send_second(parts, sizes):
    return send_parts(parts[0], "y", sizes), send_parts(parts[1], "b", sizes)


def places(sizes):
    half = sizes["a"] // 2
    out = []
    for kc in range(2):
        for ky in range(sizes["y"]):
            for kb in range(sizes["b"]):
                for ka in range(sizes["a"]):
                    part = 0 if ka < half else 1
                    out.append((kc, part, ky, kb, ka % half, (ky, kc, ka, kb)))
    return out


def owner(pos_ref, steps, sizes, crossed=False):
    ky, kc, ka, kb = steps
    y = lax.rem(pos_ref[0] + (sizes["y"] - ky), sizes["y"])
    c = lax.rem(pos_ref[1] + (2 - kc), 2)
    half = sizes["a"] // 2
    a = pos_ref[2] ^ (ka // half + 2 * (ka % half)) if crossed else lax.rem(pos_ref[2] + (sizes["a"] - ka), sizes["a"])
    b = lax.rem(pos_ref[3] + (sizes["b"] - kb), sizes["b"])
    return ((y * 2 + c) * sizes["a"] + a) * sizes["b"] + b


COST = 100


def source(ins, block, sizes):
    kc, part, ky, kb, ka, _ = block
    if len(ins) == 4:
        return ins[2 * kc + part][ky, kb, ka] if part == 0 else ins[2 * kc + part][kb, ky, ka]
    base = kc * (sizes["y"] + sizes["b"])
    return ins[base + ky][kb, ka] if part == 0 else ins[base + sizes["y"] + kb][ky, ka]


def assemble(here, there, pos, sizes, cuts, fold=1, crossed=False):
    rows = here[0].shape[-2]
    devices = 2 * sizes["y"] * sizes["b"] * sizes["a"]
    sources = list(here) + list(there)
    blocks = places(sizes)

    def kernel(pos_ref, *refs):
        ins, outs = refs[: len(sources)], refs[len(sources) :]
        for block in blocks:
            where = owner(pos_ref, block[-1], sizes, crossed)
            value = source(ins, block, sizes)
            for i, (start, width) in enumerate(cuts):
                if fold == 1:
                    outs[i][where] = value[:, start : start + width]
                else:
                    outs[0][where * fold + i] = value[:, start : start + width]

    shapes = [jax.ShapeDtypeStruct((devices, rows, width), bf16) for _, width in cuts]
    if fold > 1:
        shapes = [jax.ShapeDtypeStruct((devices * fold, rows, cuts[0][1]), bf16)]
    vmem = pl.BlockSpec(memory_space=pltpu.VMEM)
    return pl.pallas_call(
        kernel,
        out_shape=shapes,
        in_specs=[pl.BlockSpec(memory_space=pltpu.SMEM)] + [vmem] * len(sources),
        out_specs=[vmem] * len(shapes),
        name="assemble",
        **params(2 * mib(*sources) + 3, 0, 4 * devices * rows * sum(w for _, w in cuts)),
    )(pos, *sources)


def adamw(state, grad, decay, rate):
    weight, mean, square, average = state
    mean_next = beta_first * mean + (1.0 - beta_first) * grad
    square_next = beta_second * square + (1.0 - beta_second) * grad * grad
    update = mean_next / (jnp.sqrt(square_next) + adam_eps)
    weight_next = weight - rate * (update + decay * weight)
    average_next = average_rate * average + (1.0 - average_rate) * weight_next
    return [weight_next, mean_next, square_next, average_next]


def finish(own, came, qkv, out, gains, at):
    rows = own.shape[0]
    width = out[0].shape[1]
    starts = (0, width, 2 * width + SMALL)

    def kernel(*refs):
        ins, outs, turn = refs[: len(arrays)], refs[len(arrays) : -1], refs[-1]
        own_ref, came_refs, states = ins[0], ins[1 : 1 + len(came)], ins[1 + len(came) :]

        def total(start, size):
            value = own_ref[:, start : start + size]
            for ref in came_refs:
                value = value + ref[:, start : start + size].astype(f32)
            return value

        for i, start in enumerate(starts):
            done = adamw([ref[i] for ref in states[:4]], total(start, width), decay_rate, learn_rates[0])
            for ref, value in zip(outs[:4], done):
                ref[i] = value
        done = adamw([ref[...] for ref in states[4:8]], total(3 * width + SMALL, width), decay_rate, learn_rates[1])
        for ref, value in zip(outs[4:8], done):
            ref[...] = value
        turn[...] = jnp.zeros_like(turn)
        turn[:rows, :] = total(at, SMALL)
        turned = turn[...].T
        done = adamw([ref[...] for ref in states[8:12]], turned[1:3, :rows], 0.0, learn_rates[5])
        for ref, value in zip(outs[8:12], done):
            ref[...] = value
        outs[12][...] = turned[0:1, :rows]

    arrays = [own, *came, *qkv, *out, *gains]
    shapes = [jax.ShapeDtypeStruct(v.shape, f32) for v in (*qkv, *out, *gains)] + [jax.ShapeDtypeStruct((1, rows), f32)]
    done = whole("finish", kernel, shapes, arrays, scratch=[jax.ShapeDtypeStruct((SMALL, SMALL), f32)])
    return list(done[:4]), list(done[4:8]), list(done[8:12]), done[12]


def dot(a, b, spec):
    return jnp.einsum(spec, a, b, preferred_element_type=f32)


NT = (((1,), (1,)), ((), ()))
TN = (((0,), (0,)), ((), ()))
NN = (((1,), (0,)), ((), ()))


def mm(a, b, dims):
    return lax.dot_general(a, b, dims, preferred_element_type=f32)


def only(own, value):
    return jnp.where(own, value, 0.0).astype(bf16)


def heads_of(n):
    lane = lax.broadcasted_iota(jnp.int32, (n, 128), 1)
    return lane < 64, lane >= 64


def same_segment(segs_ref, n):
    row = segs_ref[pl.ds(pl.program_id(0), 1), :]
    return jnp.broadcast_to(row, (8, n)).T[:, :1] == row


def attend_kernel(scale, segs_ref, qkv_ref, out_ref):
    n, width = out_ref.shape
    query = lax.broadcasted_iota(jnp.int32, (n, n), 0)
    key = lax.broadcasted_iota(jnp.int32, (n, n), 1)
    allowed = same_segment(segs_ref, n) & (key <= query)
    for p in range(width // 128):
        q2, k2, v2 = (qkv_ref[:, i * width + p * 128 : i * width + (p + 1) * 128] for i in range(3))
        total = jnp.zeros((n, 128), f32)
        for own in heads_of(n):
            logits = jnp.where(allowed, mm(only(own, q2 * scale), k2, NT), -1e30)
            exponent = jnp.exp(logits - jnp.max(logits, axis=-1, keepdims=True))
            probs = exponent * (1.0 / jnp.sum(exponent, axis=-1, keepdims=True))
            total += mm(probs.astype(bf16), only(own, v2), NN)
        out_ref[:, p * 128 : (p + 1) * 128] = total.astype(bf16)


def attend_back_kernel(scale, segs_ref, qkv_ref, grad_ref, out_ref):
    n, width = grad_ref.shape
    key = lax.broadcasted_iota(jnp.int32, (n, n), 0)
    query = lax.broadcasted_iota(jnp.int32, (n, n), 1)
    allowed = same_segment(segs_ref, n) & (key <= query)
    for p in range(width // 128):
        q2, k2, v2 = (qkv_ref[:, i * width + p * 128 : i * width + (p + 1) * 128] for i in range(3))
        g2 = grad_ref[:, p * 128 : (p + 1) * 128]
        grads = [jnp.zeros((n, 128), f32) for _ in range(3)]
        for own in heads_of(n):
            q_own, g_own = only(own, q2 * scale), only(own, g2)
            logits = jnp.where(allowed, mm(k2, q_own, NT), -1e30)
            exponent = jnp.exp(logits - jnp.max(logits, axis=0, keepdims=True))
            probs = exponent * (1.0 / jnp.sum(exponent, axis=0, keepdims=True))
            grad_probs = mm(v2, g_own, NT)
            inner = jnp.sum(probs * grad_probs, axis=0, keepdims=True)
            grad_logits = (probs * (grad_probs - inner)).astype(bf16)
            grads[0] += mm(grad_logits, only(own, k2 * scale), TN)
            grads[1] += mm(grad_logits, q_own, NN)
            grads[2] += mm(probs.astype(bf16), g_own, NN)
        for i in range(3):
            out_ref[:, i * width + p * 128 : i * width + (p + 1) * 128] = grads[i].astype(bf16)


def attention(kernel, segs, scale, qkv, *more):
    seqs, n = segs.shape
    width = qkv.shape[1] // 3
    out_width = 3 * width if more else width
    rows = lambda w: pl.BlockSpec((n, w), lambda s: (s, 0))
    matmuls = (5 if more else 2) * 2 * seqs * n * n * width
    return pl.pallas_call(
        functools.partial(kernel, scale),
        grid=(seqs,),
        out_shape=jax.ShapeDtypeStruct((seqs * n, out_width), bf16),
        in_specs=[full((seqs, n)), rows(3 * width)]
        + [rows(width)] * len(more),
        out_specs=rows(out_width),
        name="attention_backward" if more else "attention",
        **params(8, 10 * matmuls, 2 * seqs * n * (3 * width + out_width), seqs * HEADS * n * n),
    )(segs, qkv, *more)


def full(shape):
    return pl.BlockSpec(shape, lambda *_: (0,) * len(shape))


def params(room, flops, moved, transcendentals=0):
    return dict(
        compiler_params=pltpu.CompilerParams(vmem_limit_bytes=int(room * 2**20)),
        cost_estimate=pl.CostEstimate(flops=flops // COST, transcendentals=transcendentals // COST, bytes_accessed=moved // COST),
    )


def mib(*shapes):
    return sum(math.prod(v.shape) * v.dtype.itemsize for v in shapes) / 2**20


def whole(name, kernel, shapes, arrays, scratch=(), pos=None, room=4):
    vmem = pl.BlockSpec(memory_space=pltpu.VMEM)
    lead = [] if pos is None else [pos]
    limit = 1.2 * mib(*arrays, *shapes, *scratch) + room if room == 4 else 1.1 * mib(*scratch) + room
    return pl.pallas_call(
        kernel,
        out_shape=shapes,
        in_specs=[pl.BlockSpec(memory_space=pltpu.SMEM)] * len(lead) + [vmem] * len(arrays),
        out_specs=[vmem] * len(shapes),
        scratch_shapes=[pltpu.VMEM(v.shape, v.dtype) for v in scratch],
        name=name,
        **params(limit, 0, sum(v.size for v in arrays) * 4),
    )(*lead, *arrays)


def pack(qkv, router, gains, out):
    rows, width = out.shape
    if rows % 8:
        small = jnp.concatenate([router.T, gains.T, jnp.zeros((rows, SMALL - 3), f32)], axis=1)
        return jnp.concatenate([qkv[0], qkv[1], qkv[2], small, out], axis=1).astype(bf16)

    def kernel(qkv_ref, router_ref, gains_ref, out_ref, to_ref, turn_ref):
        for i in range(3):
            to_ref[:, i * width : (i + 1) * width] = qkv_ref[i].astype(bf16)
        turn_ref[...] = jnp.zeros_like(turn_ref)
        turn_ref[0:1, :rows] = router_ref[...]
        turn_ref[1:3, :rows] = gains_ref[...]
        to_ref[:, 3 * width : 3 * width + SMALL] = turn_ref[...].T[:rows].astype(bf16)
        to_ref[:, 3 * width + SMALL :] = out_ref[...].astype(bf16)

    shape = [jax.ShapeDtypeStruct((rows, 4 * width + SMALL), bf16)]
    return whole("pack", kernel, shape, [qkv, router, gains, out], scratch=[jax.ShapeDtypeStruct((SMALL, SMALL), f32)])[0]


def pack_rest(up, down):
    rows = up.shape[0]
    width, fold = down.shape[1], down.shape[0] // rows
    if rows % 8:
        return up.astype(bf16), jnp.concatenate([down[i * rows : (i + 1) * rows] for i in range(fold)], axis=1).astype(bf16)

    def kernel(up_ref, down_ref, first_ref, second_ref):
        first_ref[...] = up_ref[...].astype(bf16)
        for i in range(fold):
            second_ref[:, i * width : (i + 1) * width] = down_ref[i * rows : (i + 1) * rows].astype(bf16)

    return whole("pack_rest", kernel, [jax.ShapeDtypeStruct(up.shape, bf16), jax.ShapeDtypeStruct((rows, fold * width), bf16)], [up, down])


def like(count, width, kind):
    return jax.ShapeDtypeStruct((count, width), kind)


def project(picked, back_cot, w_qkv, w_small, room=8):
    count, width = picked.shape

    def kernel(picked_ref, cot_ref, w_ref, small_ref, hidden_ref, out_ref, score_ref, rows_ref, back_ref):
        rows = small_ref[:, :128].astype(f32).T[:8]
        rows_ref[...] = rows
        value = picked_ref[...].astype(f32)
        score = mm(picked_ref[...], small_ref[:, :128], NN)[:, :1]
        score_ref[...] = score
        back_ref[...] = (score * cot_ref[...].astype(f32)).astype(bf16)
        hidden_ref[...] = (value * norm_of(value) * rows[1:2]).astype(bf16)
        for j in range(3):
            cut = slice(j * width, (j + 1) * width)
            out_ref[:, cut] = mm(hidden_ref[...], w_ref[:, cut], NN).astype(bf16)

    shapes = [like(count, width, bf16), like(count, 3 * width, bf16), like(count, 1, f32), like(8, width, f32), like(count, width, bf16)]
    return whole("project", kernel, shapes, [picked, back_cot, w_qkv, w_small], room=room)


def devices_of(pos, steps, sizes):
    y, c, a, b = (lax.rem(pos[i] + steps[i], n) for i, n in enumerate((sizes["y"], 2, sizes["a"], sizes["b"])))
    return y, c, a, b


def weight_grad(left, right, jobs, shape, rows, pos, sizes):
    ny, na, nb = sizes["y"], sizes["a"], sizes["b"]
    blocks = ny * na * nb
    count, wide = left[0].shape[0], max(job[1] for job in jobs)

    def kernel(pos_ref, left_ref, left_other, right_ref, right_other, *refs):
        outs, acc, turned = refs[:4], refs[4], refs[5]
        chunk = na * nb * rows

        def columns(ref, y):
            if chunk % 128 == 0:
                return ref[:, pl.ds(pl.multiple_of((2 * y + pos_ref[1]) * chunk, 128), chunk)]
            both = ref[:, 2 * y * chunk : 2 * (y + 1) * chunk]
            return jnp.where(pos_ref[1] == 0, both[:, :chunk], both[:, chunk:])

        for side, ref in enumerate((left_ref, left_other)):
            for y in range(ny):
                turned[side, y * chunk : (y + 1) * chunk, :] = columns(ref, y).T
        for start, width, spots in jobs:
            total = mm(turned[0], right_ref[:, start : start + width], NN)
            total += mm(turned[1], right_other[:, start : start + width], NN)
            acc[:, :, :width] = total.reshape(blocks, rows, width)
            for ky in range(ny):
                for ka in range(na):
                    for kb in range(nb):
                        y, _, a, b = devices_of(pos_ref, (ky, 0, ka, kb), sizes)
                        value = acc[(y * na + a) * nb + b, :, :width].astype(bf16)
                        for column, some, part, row, to in spots:
                            if part == 0:
                                ref = outs[0].at[ky, ka] if kb == 0 else outs[1].at[kb - 1, ky, ka]
                            else:
                                ref = outs[2].at[kb, ka] if ky == 0 else outs[3].at[ky - 1, kb, ka]
                            ref[row : row + rows, to : to + some] = value[:, column : column + some]

    leads = [(ny, na), (nb - 1, ny, na), (nb, na), (ny - 1, nb, na)]
    outs = [jax.ShapeDtypeStruct(v + shape, bf16) for v in leads]
    scratch = [jax.ShapeDtypeStruct((blocks, rows, wide), f32), jax.ShapeDtypeStruct((2, blocks * rows, count), bf16)]
    vmem = pl.BlockSpec(memory_space=pltpu.VMEM)
    arrays = list(left) + list(right)
    return pl.pallas_call(
        kernel,
        out_shape=outs,
        in_specs=[pl.BlockSpec(memory_space=pltpu.SMEM)] + [vmem] * 4,
        out_specs=[vmem] * 4,
        scratch_shapes=[pltpu.VMEM(v.shape, v.dtype) for v in scratch],
        name="weight_grad",
        **params(mib(*scratch) * 1.1 + 9, 4 * count * blocks * rows * right[0].shape[1], sum(v.size for v in arrays) * 2),
    )(pos, *arrays)


def weight_grad_plain(left, right, jobs, shape, rows, pos, sizes):
    ny, na, nb = sizes["y"], sizes["a"], sizes["b"]
    left = [columns_of(v, pos[1], sizes) for v in left]
    total = sum(dot(a, b, "rd,re->de") for a, b in zip(left, right)).astype(bf16).reshape(ny, na, nb, rows, -1)
    for axis, at in ((0, 0), (1, 2), (2, 3)):
        total = jnp.roll(total, -pos[at], axis)
    done = [jnp.zeros((ny, na, nb) + shape, bf16) for _ in range(2)]
    for start, _, spots in jobs:
        for column, some, part, row, to in spots:
            done[part] = done[part].at[..., row : row + rows, to : to + some].set(total[..., start + column : start + column + some])
    first, second = done[0].transpose(2, 0, 1, 3, 4), done[1].transpose(0, 2, 1, 3, 4)
    return first[0], first[1:], second[0], second[1:]


def weight_grad_own(lefts, rights, narrow, halves, pos, sizes):
    ny, na, nb = sizes["y"], sizes["a"], sizes["b"]
    blocks = 2 * ny * na * nb
    count, model = lefts[0].shape
    rows = model // blocks
    wide = max(w for part in halves for _, _, w in part)
    leads = [(nb, ny, na), (ny, nb, na)]
    shapes = [v + (rows, sum(w for _, _, w in part)) for v, part in zip(leads, halves)]
    if rows % 8:
        return weight_grad_own_plain(lefts, rights, narrow, halves, pos, sizes)

    def kernel(pos_ref, *refs):
        ins, outs, acc, turned = refs[: 2 * len(lefts) + 1], refs[2 * len(lefts) + 1 : -2], refs[-2], refs[-1]
        for i in range(len(lefts)):
            turned[i] = ins[i][...].T
        for part, some in enumerate(halves):
            to = 0
            for i, start, width in some:
                if i < 0:
                    value = ins[-1][...]
                    total = jnp.concatenate([value, jnp.zeros((width - value.shape[0], model), f32)]).T
                else:
                    total = mm(turned[i], ins[len(lefts) + i][:, start : start + width], NN)
                acc[:, :, :width] = total.reshape(blocks, rows, width)
                for kc in range(2):
                    for ky in range(ny):
                        for ka in range(na):
                            for kb in range(nb):
                                y, c, a, b = devices_of(pos_ref, (ky, kc, ka, kb), sizes)
                                ref = outs[2 * kc + part]
                                ref = ref.at[kb, ky, ka] if part == 0 else ref.at[ky, kb, ka]
                                ref[:, to : to + width] = acc[((y * 2 + c) * na + a) * nb + b, :, :width].astype(bf16)
                to += width

    outs = [jax.ShapeDtypeStruct(v, bf16) for v in shapes] * 2
    scratch = [jax.ShapeDtypeStruct((blocks, rows, wide), f32), jax.ShapeDtypeStruct((len(lefts), model, count), bf16)]
    vmem = pl.BlockSpec(memory_space=pltpu.VMEM)
    arrays = list(lefts) + list(rights) + [narrow]
    done = pl.pallas_call(
        kernel,
        out_shape=outs,
        in_specs=[pl.BlockSpec(memory_space=pltpu.SMEM)] + [vmem] * len(arrays),
        out_specs=[vmem] * 4,
        scratch_shapes=[pltpu.VMEM(v.shape, v.dtype) for v in scratch],
        name="weight_grad_own",
        **params(mib(*scratch) * 1.1 + 9, 2 * count * model * sum(v.shape[1] for v in rights), sum(v.size for v in arrays) * 2),
    )(pos, *arrays)
    return done[:2], done[2:]


def weight_grad_own_plain(lefts, rights, narrow, halves, pos, sizes):
    ny, na, nb = sizes["y"], sizes["a"], sizes["b"]
    done = []
    for part in halves:
        pieces = []
        for i, start, width in part:
            if i < 0:
                pieces.append(jnp.pad(narrow.T, ((0, 0), (0, width - narrow.shape[0]))))
            else:
                pieces.append(dot(lefts[i], rights[i][:, start : start + width], "rd,re->de"))
        total = jnp.concatenate(pieces, axis=1).astype(bf16)
        total = total.reshape(ny, 2, na, nb, -1, total.shape[1])
        for axis in range(4):
            total = jnp.roll(total, -pos[axis], axis)
        done.append(total)
    return [(done[0][:, kc].transpose(2, 0, 1, 3, 4), done[1][:, kc].transpose(0, 2, 1, 3, 4)) for kc in range(2)]


def norm_of(value):
    return lax.rsqrt(jnp.mean(value * value, axis=-1, keepdims=True) + norm_eps)


def feed_forward(mixed, picked, score, gain, w_out, w_up, room=9):
    count, width = picked.shape
    hidden = w_up.shape[1]

    def kernel(mixed_ref, picked_ref, score_ref, gain_ref, wo_ref, w_ref, attended_ref, first_ref, hidden_ref, activ_ref, slope_ref):
        attended = mm(mixed_ref[...], wo_ref[...], NN)
        first = picked_ref[...].astype(f32) + score_ref[...] * attended
        attended_ref[...] = attended
        first_ref[...] = first
        hidden_ref[...] = (first * norm_of(first) * gain_ref[2:3, :]).astype(bf16)
        c0 = (2.0 / math.pi) ** 0.5
        step = width // 2
        for j in range(hidden // step):
            cut = slice(j * step, (j + 1) * step)
            v = mm(hidden_ref[...], w_ref[:, cut], NN)
            square = v * v
            t = jnp.tanh(v * (c0 + (c0 * 0.044715) * square))
            cdf = 0.5 + 0.5 * t
            activ_ref[:, cut] = (v * cdf).astype(bf16)
            slope_ref[:, cut] = cdf + (cdf - cdf * cdf) * (v * (2.0 * c0 + (6.0 * 0.044715 * c0) * square))

    shapes = [like(count, width, f32), like(count, width, f32), like(count, width, bf16), like(count, hidden, bf16), like(count, hidden, f32)]
    return whole("feed_forward", kernel, shapes, [mixed, picked, score, gain, w_out, w_up], room=room)


def down_both(activ, slope, grad_out, w_down, first, score, back_cot, room=8):
    count, width = first.shape
    hidden = activ.shape[1]

    def kernel(activ_ref, slope_ref, grad_ref, w_ref, first_ref, score_ref, cot_ref, pre_ref, second_ref, dr_ref):
        step = width
        for j in range(hidden // step):
            cut = slice(j * step, (j + 1) * step)
            pre_ref[:, cut] = (mm(grad_ref[...], w_ref[cut, :], NT) * slope_ref[:, cut]).astype(bf16)
        total = mm(activ_ref[...], w_ref[...], NN)
        second_ref[...] = (first_ref[...] + score_ref[...] * total).astype(bf16)
        dr_ref[...] = jnp.sum(cot_ref[...].astype(f32) * total, axis=-1, keepdims=True)

    shapes = [like(count, hidden, bf16), like(count, width, bf16), like(count, 1, f32)]
    return whole("down_both", kernel, shapes, [activ, slope, grad_out, w_down, first, score, back_cot], room=room)


def back_of_norm(grad, value, gain):
    inv = norm_of(value)
    normed = value * inv
    scaled = grad * gain
    mean = jnp.mean(scaled * normed, axis=-1, keepdims=True)
    return (scaled - normed * mean) * inv, jnp.sum(grad * normed, axis=0, keepdims=True)


def up_back(grad_pre, w_out, w_up, first, attended, score, back_cot, gain, room=9):
    count, width = first.shape

    def kernel(pre_ref, wo_ref, w_ref, first_ref, attended_ref, score_ref, cot_ref, gain_ref, out_ref, low_ref, mixed_ref, dr_ref, dgain_ref):
        grad, dgain = back_of_norm(mm(pre_ref[...], w_ref[...], NT), first_ref[...], gain_ref[2:3, :])
        grad = cot_ref[...].astype(f32) + grad
        low = (score_ref[...] * grad).astype(bf16)
        out_ref[...] = grad
        low_ref[...] = low
        dgain_ref[...] = dgain
        dr_ref[...] = jnp.sum(grad * attended_ref[...], axis=-1, keepdims=True)
        mixed_ref[...] = mm(low, wo_ref[...], NT).astype(bf16)

    shapes = [like(count, width, f32), like(count, width, bf16), like(count, width, bf16), like(count, 1, f32), like(1, width, f32)]
    return whole("up_back", kernel, shapes, [grad_pre, w_out, w_up, first, attended, score, back_cot, gain], room=room)


def project_back(grad_projected, w_qkv, picked, rows, grad_first, drs, dgain_two, room=9):
    count, width = picked.shape

    def kernel(grad_ref, w_ref, picked_ref, rows_ref, first_ref, dr_ref, more_ref, two_ref, out_ref, narrow_ref):
        value, dr = picked_ref[...].astype(f32), dr_ref[...] + more_ref[...]
        grad, dgain = back_of_norm(mm(grad_ref[...], w_ref[...], NT), value, rows_ref[1:2, :])
        out_ref[...] = (first_ref[...] + grad + dr * rows_ref[0:1, :]).astype(bf16)
        drouter = jnp.sum(dr * value, axis=0, keepdims=True)
        narrow_ref[...] = jnp.concatenate([drouter, dgain, two_ref[...], jnp.zeros((5, width), f32)])

    shapes = [like(count, width, bf16), like(8, width, f32)]
    return whole("project_back", kernel, shapes, [grad_projected, w_qkv, picked, rows, grad_first, *drs, dgain_two], room=room)


def body(sizes, *args):
    tokens, cotangent, segment_ids, routed = args[:4]
    states = [args[4 + 4 * i : 8 + 4 * i] for i in range(6)]
    qkv_state, out_state, up_state, down_state, router_state, gains_state = states
    seqs, length, width = tokens.shape
    capacity = routed.shape[1]
    count = seqs * capacity
    rows = out_state[0].shape[0]
    hidden = up_state[0].shape[1]
    fold = down_state[0].shape[0] // rows
    scale = (width // HEADS) ** (-0.5)
    pos = jnp.stack([lax.axis_index(n) for n in ("y", "c", "a", "b")]).astype(jnp.int32)

    low = lambda v: v.astype(bf16)
    barrier = lax.optimization_barrier
    room = () if rows % 8 == 0 else (40,)
    send_qkv = pack(after(qkv_state[0], pos), router_state[0][None, :], gains_state[0], out_state[0])
    way_qkv = gather_axis(send_qkv, "a", sizes)
    send_up, send_down = pack_rest(up_state[0], down_state[0])

    here = routed[:, :, None] == jnp.arange(length, dtype=jnp.int32)[None, None, :]
    pick = here.astype(bf16)
    is_routed = jnp.any(here, axis=1)
    picked = dot(pick, tokens, "sct,std->scd").astype(bf16).reshape(count, width)
    way_qkv = stacked(halves_of(after(way_qkv, picked)))
    way_qkv, send_up, send_down = barrier((way_qkv, send_up, send_down))
    way_qkv = go_second(way_qkv, sizes)
    far_up = paired(send_up, 2, sizes)
    back_cot = dot(pick, cotangent, "sct,std->scd").astype(bf16).reshape(count, width)
    segs = jnp.sum(jnp.where(here, segment_ids[:, None, :], 0), axis=-1).astype(f32)
    way_qkv, far_up, back_cot, segs = hold(way_qkv, far_up, back_cot, segs)
    way_qkv = stacked(way_qkv)
    (first_up,) = stacked([[send_up, far_up]])
    way_qkv, first_up = barrier((way_qkv, first_up))
    way_qkv = go_third(way_qkv, sizes)
    second_up = paired(first_up, 1, sizes)
    far_down = paired(send_down, 2, sizes)
    way_qkv, second_up, far_down = hold(way_qkv, second_up, far_down)
    (first_down,) = stacked([[send_down, far_down]])
    got = side_by_side(way_qkv)
    got = got, [shifted(v, "c", sizes, 1) for v in got]
    way_up = go_second((first_up, second_up), sizes)
    second_down = paired(first_down, 1, sizes)

    w_qkv, w_small, w_out = assemble(*got, after(pos, first_down), sizes, [(0, 3 * width), (3 * width, SMALL), (3 * width + SMALL, width)])
    w_out = w_out.reshape(width, width)
    w_qkv = w_qkv.reshape(width, 3 * width)
    hidden_one, projected, score, narrow, grad_down_out = project(picked, back_cot, w_qkv, w_small.reshape(width, SMALL), *room)
    way_up, projected = hold(way_up, projected)
    way_up = stacked(way_up)
    projected, way_up = barrier((projected, way_up))
    early_up = to_core([[v] for v in way_up], sizes)
    way_up = go_third(way_up, sizes)
    mixed = attention(attend_kernel, segs, scale, projected)
    way_down = go_second(after((first_down, second_down), mixed), sizes)
    way_up, mixed = hold(way_up, mixed)
    late_up = to_core([v[1:] for v in way_up], sizes)
    came_down = after([v[1:] for v in way_down], [v[1:] for v in way_up])
    way_down = stacked([v[:1] + c for v, c in zip(way_down, came_down)])
    early_down = to_core([[v] for v in way_down], sizes)
    down_there, pos_up = barrier((way_down, pos))
    way_down = go_third(way_down, sizes)
    got_up = joined(way_up, early_up, late_up)
    (w_up,) = assemble(*got_up, pos_up, sizes, [(0, hidden)], crossed=True)
    w_up = w_up.reshape(width, hidden)
    attended, first, hidden_two, activ_low, slope = feed_forward(mixed, picked, score, narrow, w_out, w_up, *room)

    way_down, activ_low = hold(way_down, activ_low)
    got_down = joined(way_down, early_down, to_core([v[1:] for v in way_down], sizes))
    activ_pair = swapped(after(activ_low, got_down), sizes)
    grad_down_pair = swapped(after(grad_down_out, got_down), sizes)
    hidden_two_pair = swapped(hidden_two, sizes)
    (w_down,) = assemble(*got_down, pos, sizes, [(i * width, width) for i in range(fold)], fold, crossed=True)
    w_down = w_down.reshape(hidden, width)
    grad_pre, second, dr_second = down_both(activ_low, slope, grad_down_out, w_down, first, score, back_cot, *room)

    (activ_pair, hidden_two_pair, grad_down_pair), grad_pre = hold([activ_pair, hidden_two_pair, grad_down_pair], grad_pre)
    grad_pre_pair = swapped(grad_pre, sizes)
    half = width // 2
    split = fold * rows
    make = weight_grad if rows % 8 == 0 else weight_grad_plain
    jobs = [(i * half, half, [(0, half, i, 0, 0)]) for i in range(2)]
    grad_2 = make(activ_pair, grad_down_pair, jobs, (split, half), split, pos, sizes)
    came_2 = sum_first(grad_2, sizes)
    grad_pre_pair = grad_pre_pair[:1] + after(grad_pre_pair[1:], grad_2)
    spot = lambda i: (i // fold, (i % fold) * rows, 0)
    jobs = [(i * width, width, [(0, half) + spot(2 * i), (half, half) + spot(2 * i + 1)]) for i in range(fold)]
    grad_1 = make(hidden_two_pair, grad_pre_pair, jobs, (split, half), rows, pos, sizes)
    came_1 = sum_first(grad_1, sizes)
    grad_pre = after(grad_pre, grad_1)
    grad_first, grad_attended, grad_mixed, dr_first, grad_gain_two = up_back(grad_pre, w_out, w_up, first, attended, score, back_cot, narrow, *room)
    grad_projected = attention(attend_back_kernel, segs, scale, projected, after(grad_mixed, came_2))
    grad_projected, came_1, came_2 = barrier((grad_projected, came_1, came_2))
    more_12 = sum_second([grad_2, grad_1], [came_2, came_1])
    grad_projected, more_12 = barrier((grad_projected, more_12))
    more_12 = send_second(more_12, sizes)
    grad_rows, grad_narrow = project_back(
        grad_projected, w_qkv, picked, narrow, grad_first, (dr_second, dr_first), grad_gain_two, *room
    )

    halves = [(0, 0, width), (0, width, width), (-1, 0, SMALL)], [(0, 2 * width, width), (1, 0, width)]
    own_0, other_0 = weight_grad_own([hidden_one, mixed], [grad_projected, grad_attended], grad_narrow, halves, pos, sizes)
    came_first = shifted(other_0[0], "c", sizes, 1)
    more_12 = after(more_12, own_0)
    own_12, part_12 = sum_third([grad_2, grad_1], [came_2, came_1], more_12)
    came_0 = [came_first, shifted(after(other_0[1], part_12), "c", sizes, 1)]
    came_0, part_12 = barrier((came_0, part_12))
    last_12 = send_parts(part_12, "a", sizes)
    grad_0 = sum_core(own_0, came_0)
    came_0 = sum_first(grad_0, sizes)
    shape = (seqs, capacity, width)
    second = after(second, grad_0)
    block_out = jnp.where(is_routed[:, :, None], low(dot(pick, second.reshape(shape), "sct,scd->std")), tokens)
    came_0, grad_rows, block_out = barrier((came_0, grad_rows, block_out))
    more_0 = sum_second([grad_0], [came_0])
    more_0, grad_rows = barrier((more_0, grad_rows))
    more_0 = send_second(more_0, sizes)
    tokens_grad = jnp.where(is_routed[:, :, None], low(dot(pick, grad_rows.reshape(shape), "sct,scd->std")), cotangent)
    more_0, tokens_grad, last_12 = barrier((more_0, tokens_grad, last_12))
    own_0, part_0 = sum_third([grad_0], [came_0], more_0)
    last_0 = send_parts(part_0, "a", sizes)
    last_12 = after(last_12, part_0)
    total_12 = add_up(own_12, last_12)
    sum_down, folded = total_12[:split], total_12[split:]
    sum_up = jnp.concatenate([folded[i * rows : (i + 1) * rows, j * half : (j + 1) * half] for j in range(2) for i in range(fold)], axis=1)
    new_qkv, new_out, new_gains, grad_router = finish(own_0, last_0, qkv_state, out_state, gains_state, 2 * width)
    new_up = adamw(up_state, sum_up, decay_rate, learn_rates[2])
    new_down = adamw(down_state, sum_down, decay_rate, learn_rates[3])
    new_router = adamw(router_state, grad_router[0], 0.0, learn_rates[4])
    return (block_out, tokens_grad, *new_qkv, *new_out, *new_up, *new_down, *new_router, *new_gains)


def solution(mesh):
    lead = mesh.shape["dp"] // 2
    inner = mesh.shape["fsdp"] // 4
    names = ("y", "c", "a", "b")
    fine = Mesh(mesh.devices.reshape(lead, 2, 4, inner), names)
    sizes = dict(zip(names, (lead, 2, 4, inner)))
    head, second, only = P(names, None, None), P(None, names, None), P(names, None)
    weights = (second,) * 4 + (only,) * 12 + (P(names),) * 4 + (P(None, names),) * 4
    return jax.shard_map(
        functools.partial(body, sizes),
        mesh=fine,
        in_specs=(head, head, only, only) + weights,
        out_specs=(head, head) + weights,
        check_vma=False,
    )
```

```python
import functools
import math

import jax
import jax.numpy as jnp
from jax import lax
from jax.experimental import pallas as pl
from jax.experimental.pallas import tpu as pltpu
from jax.sharding import Mesh, PartitionSpec as P

HEADS = 12
SMALL = 128

norm_eps = 1e-06
learn_rates = (0.03, 0.1, 0.03, 0.02, 0.03, 0.2)
beta_first = 0.5
beta_second = 0.5
adam_eps = 1e-08
decay_rate = 0.1
average_rate = 0.7
exact_mode = lax.Precision.HIGHEST
f32 = jnp.float32
bf16 = jnp.bfloat16


def shifted(value, axis, sizes, step):
    n = sizes[axis]
    return lax.ppermute(value, axis, [(i, (i + step) % n) for i in range(n)])


def after(value, *others):
    return lax.optimization_barrier((value, others))[0]


def paired(value, step, sizes):
    return lax.ppermute(value, "a", [(i, i ^ step) for i in range(sizes["a"])])


def hold(lists, *others):
    came, others = lax.optimization_barrier(([v[1:] for v in lists], others))
    return ([v[:1] + c for v, c in zip(lists, came)],) + others


def gather_axis(value, axis, sizes):
    return [value] + [shifted(value, axis, sizes, k) for k in range(1, sizes[axis])]


def halves_of(value):
    half = len(value) // 2
    return value[:half], value[half:]


def go_second(halves, sizes):
    return gather_axis(halves[0], "b", sizes), gather_axis(halves[1], "y", sizes)


def go_third(halves, sizes):
    return gather_axis(halves[0], "y", sizes), gather_axis(halves[1], "b", sizes)


def stacked(lists):
    arrays = [v for some in lists for v in some]

    def kernel(*refs):
        at = 0
        for out, some in zip(refs[len(arrays) :], lists):
            for k in range(len(some)):
                out[k] = refs[at + k][...]
            at += len(some)

    return whole("stacked", kernel, [jax.ShapeDtypeStruct((len(v),) + v[0].shape, v[0].dtype) for v in lists], arrays)


def to_core(lists, sizes):
    return [[shifted(v, "c", sizes, 1) for v in some] for some in lists]


def side_by_side(lists):
    def kernel(*refs):
        at = 0
        for out, some in zip(refs[-2:], lists):
            for k in range(len(some)):
                out[k] = refs[at][...]
                at += 1

    shapes = [jax.ShapeDtypeStruct((len(v),) + v[0].shape, bf16) for v in lists]
    return whole("side_by_side", kernel, shapes, lists[0] + lists[1])


def joined(lists, early, late):
    return lists[0] + lists[1], early[0] + late[0] + early[1] + late[1]


def take(value, index, axis):
    return lax.dynamic_index_in_dim(value, index, axis, keepdims=False)


def columns_of(value, core, sizes):
    ny = sizes["y"]
    chunk = value.shape[1] // (2 * ny)
    return jnp.concatenate([lax.dynamic_slice_in_dim(value, (2 * y + core) * chunk, chunk, 1) for y in range(ny)], axis=1)


def swapped(value, sizes):
    return [value, shifted(value, "c", sizes, 1)]


def add_up(own, came):
    own = own.astype(f32)
    for part in came:
        own = own + part.astype(f32)
    return own


def send_parts(parts, axis, sizes):
    return [shifted(parts[k].astype(bf16), axis, sizes, k + 1) for k in range(sizes[axis] - 1)]


def sum_first(grad, sizes):
    return send_parts(grad[1], "b", sizes), send_parts(grad[3], "y", sizes)


def sum_core(own, came):
    ins = [own[0], came[0], own[1], came[1]]
    shapes = [w for v in own for w in (v.shape[1:], (v.shape[0] - 1,) + v.shape[1:])]

    def kernel(*refs):
        outs = refs[len(ins) :]
        for i in range(2):
            for k in range(own[i].shape[0]):
                total = (refs[2 * i][k].astype(f32) + refs[2 * i + 1][k].astype(f32)).astype(bf16)
                if k == 0:
                    outs[2 * i][...] = total
                else:
                    outs[2 * i + 1][k - 1] = total

    return whole("sum_core", kernel, [jax.ShapeDtypeStruct(v, bf16) for v in shapes], ins)


def sum_second(grads, cames):
    count = len(grads)
    ins = [v for grad, came in zip(grads, cames) for v in [grad[0]] + came[0] + [grad[2]] + came[1]]
    counts = 1 + len(cames[0][0]), 1 + len(cames[0][1])
    shapes = [(grads[0][i].shape[0] - 1, count) + grads[0][i].shape[1:] for i in (0, 2)]

    def kernel(*refs):
        outs, at = refs[len(ins) :], 0
        for n in range(count):
            for out, some in zip(outs, counts):
                for k in range(out.shape[0]):
                    total = refs[at][k + 1].astype(f32)
                    for ref in refs[at + 1 : at + some]:
                        total += ref[k + 1].astype(f32)
                    out[k, n] = total.astype(bf16)
                at += some

    return whole("sum_second", kernel, [jax.ShapeDtypeStruct(v, bf16) for v in shapes], ins)


def sum_third(grads, cames, more):
    count = len(grads)
    ins = [v for grad, came in zip(grads, cames) for v in [grad[0]] + came[0] + [grad[2]] + came[1]] + more[0] + more[1]
    counts = 1 + len(cames[0][0]), 1 + len(cames[0][1])
    na, rows, width = grads[0][0].shape[1:]
    cuts = (0, width), (width, width + grads[0][2].shape[-1])

    def kernel(*refs):
        outs, at, late = refs[len(ins) :], 0, sum(counts) * count
        for n in range(count):
            for part, (some, (start, stop)) in enumerate(zip(counts, cuts)):
                first = late + (len(more[0]) if part else 0)
                for k in range(na):
                    total = refs[at][0, k].astype(f32)
                    for ref in refs[at + 1 : at + some]:
                        total += ref[0, k].astype(f32)
                    for ref in refs[first : first + len(more[part])]:
                        total += ref[n, k].astype(f32)
                    outs[k][n * rows : (n + 1) * rows, start:stop] = total.astype(outs[k].dtype)
                at += some

    shape = count * rows, cuts[1][1]
    outs = whole("sum_third", kernel, [jax.ShapeDtypeStruct(shape, f32 if k == 0 else bf16) for k in range(na)], ins)
    return outs[0], list(outs[1:])


def send_second(parts, sizes):
    return send_parts(parts[0], "y", sizes), send_parts(parts[1], "b", sizes)


def places(sizes):
    half = sizes["a"] // 2
    out = []
    for kc in range(2):
        for ky in range(sizes["y"]):
            for kb in range(sizes["b"]):
                for ka in range(sizes["a"]):
                    part = 0 if ka < half else 1
                    out.append((kc, part, ky, kb, ka % half, (ky, kc, ka, kb)))
    return out


def owner(pos_ref, steps, sizes, crossed=False):
    ky, kc, ka, kb = steps
    y = lax.rem(pos_ref[0] + (sizes["y"] - ky), sizes["y"])
    c = lax.rem(pos_ref[1] + (2 - kc), 2)
    half = sizes["a"] // 2
    a = pos_ref[2] ^ (ka // half + 2 * (ka % half)) if crossed else lax.rem(pos_ref[2] + (sizes["a"] - ka), sizes["a"])
    b = lax.rem(pos_ref[3] + (sizes["b"] - kb), sizes["b"])
    return ((y * 2 + c) * sizes["a"] + a) * sizes["b"] + b


COST = 100


def source(ins, block, sizes):
    kc, part, ky, kb, ka, _ = block
    if len(ins) == 4:
        return ins[2 * kc + part][ky, kb, ka] if part == 0 else ins[2 * kc + part][kb, ky, ka]
    base = kc * (sizes["y"] + sizes["b"])
    return ins[base + ky][kb, ka] if part == 0 else ins[base + sizes["y"] + kb][ky, ka]


def assemble(here, there, pos, sizes, cuts, fold=1, crossed=False):
    rows = here[0].shape[-2]
    devices = 2 * sizes["y"] * sizes["b"] * sizes["a"]
    sources = list(here) + list(there)
    blocks = places(sizes)

    def kernel(pos_ref, *refs):
        ins, outs = refs[: len(sources)], refs[len(sources) :]
        for block in blocks:
            where = owner(pos_ref, block[-1], sizes, crossed)
            value = source(ins, block, sizes)
            for i, (start, width) in enumerate(cuts):
                if fold == 1:
                    outs[i][where] = value[:, start : start + width]
                else:
                    outs[0][where * fold + i] = value[:, start : start + width]

    shapes = [jax.ShapeDtypeStruct((devices, rows, width), bf16) for _, width in cuts]
    if fold > 1:
        shapes = [jax.ShapeDtypeStruct((devices * fold, rows, cuts[0][1]), bf16)]
    vmem = pl.BlockSpec(memory_space=pltpu.VMEM)
    return pl.pallas_call(
        kernel,
        out_shape=shapes,
        in_specs=[pl.BlockSpec(memory_space=pltpu.SMEM)] + [vmem] * len(sources),
        out_specs=[vmem] * len(shapes),
        name="assemble",
        **params(2 * mib(*sources) + 3, 0, 4 * devices * rows * sum(w for _, w in cuts)),
    )(pos, *sources)


def adamw(state, grad, decay, rate):
    weight, mean, square, average = state
    mean_next = beta_first * mean + (1.0 - beta_first) * grad
    square_next = beta_second * square + (1.0 - beta_second) * grad * grad
    update = mean_next / (jnp.sqrt(square_next) + adam_eps)
    weight_next = weight - rate * (update + decay * weight)
    average_next = average_rate * average + (1.0 - average_rate) * weight_next
    return [weight_next, mean_next, square_next, average_next]


def finish(own, came, qkv, out, gains, at):
    rows = own.shape[0]
    width = out[0].shape[1]
    starts = (0, width, 2 * width + SMALL)

    def kernel(*refs):
        ins, outs, turn = refs[: len(arrays)], refs[len(arrays) : -1], refs[-1]
        own_ref, came_refs, states = ins[0], ins[1 : 1 + len(came)], ins[1 + len(came) :]

        def total(start, size):
            value = own_ref[:, start : start + size]
            for ref in came_refs:
                value = value + ref[:, start : start + size].astype(f32)
            return value

        for i, start in enumerate(starts):
            done = adamw([ref[i] for ref in states[:4]], total(start, width), decay_rate, learn_rates[0])
            for ref, value in zip(outs[:4], done):
                ref[i] = value
        done = adamw([ref[...] for ref in states[4:8]], total(3 * width + SMALL, width), decay_rate, learn_rates[1])
        for ref, value in zip(outs[4:8], done):
            ref[...] = value
        turn[...] = jnp.zeros_like(turn)
        turn[:rows, :] = total(at, SMALL)
        turned = turn[...].T
        done = adamw([ref[...] for ref in states[8:12]], turned[1:3, :rows], 0.0, learn_rates[5])
        for ref, value in zip(outs[8:12], done):
            ref[...] = value
        outs[12][...] = turned[0:1, :rows]

    arrays = [own, *came, *qkv, *out, *gains]
    shapes = [jax.ShapeDtypeStruct(v.shape, f32) for v in (*qkv, *out, *gains)] + [jax.ShapeDtypeStruct((1, rows), f32)]
    done = whole("finish", kernel, shapes, arrays, scratch=[jax.ShapeDtypeStruct((SMALL, SMALL), f32)])
    return list(done[:4]), list(done[4:8]), list(done[8:12]), done[12]


def dot(a, b, spec):
    return jnp.einsum(spec, a, b, preferred_element_type=f32)


NT = (((1,), (1,)), ((), ()))
TN = (((0,), (0,)), ((), ()))
NN = (((1,), (0,)), ((), ()))


def mm(a, b, dims):
    return lax.dot_general(a, b, dims, preferred_element_type=f32)


def only(own, value):
    return jnp.where(own, value, 0.0).astype(bf16)


def heads_of(n):
    lane = lax.broadcasted_iota(jnp.int32, (n, 128), 1)
    return lane < 64, lane >= 64


def same_segment(segs_ref, n):
    row = segs_ref[pl.ds(pl.program_id(0), 1), :]
    return jnp.broadcast_to(row, (8, n)).T[:, :1] == row


def attend_kernel(scale, segs_ref, qkv_ref, out_ref):
    n, width = out_ref.shape
    query = lax.broadcasted_iota(jnp.int32, (n, n), 0)
    key = lax.broadcasted_iota(jnp.int32, (n, n), 1)
    allowed = same_segment(segs_ref, n) & (key <= query)
    for p in range(width // 128):
        q2, k2, v2 = (qkv_ref[:, i * width + p * 128 : i * width + (p + 1) * 128] for i in range(3))
        total = jnp.zeros((n, 128), f32)
        for own in heads_of(n):
            logits = jnp.where(allowed, mm(only(own, q2 * scale), k2, NT), -1e30)
            exponent = jnp.exp(logits - jnp.max(logits, axis=-1, keepdims=True))
            probs = exponent * (1.0 / jnp.sum(exponent, axis=-1, keepdims=True))
            total += mm(probs.astype(bf16), only(own, v2), NN)
        out_ref[:, p * 128 : (p + 1) * 128] = total.astype(bf16)


def attend_back_kernel(scale, segs_ref, qkv_ref, grad_ref, out_ref):
    n, width = grad_ref.shape
    key = lax.broadcasted_iota(jnp.int32, (n, n), 0)
    query = lax.broadcasted_iota(jnp.int32, (n, n), 1)
    allowed = same_segment(segs_ref, n) & (key <= query)
    for p in range(width // 128):
        q2, k2, v2 = (qkv_ref[:, i * width + p * 128 : i * width + (p + 1) * 128] for i in range(3))
        g2 = grad_ref[:, p * 128 : (p + 1) * 128]
        grads = [jnp.zeros((n, 128), f32) for _ in range(3)]
        for own in heads_of(n):
            q_own, g_own = only(own, q2 * scale), only(own, g2)
            logits = jnp.where(allowed, mm(k2, q_own, NT), -1e30)
            exponent = jnp.exp(logits - jnp.max(logits, axis=0, keepdims=True))
            probs = exponent * (1.0 / jnp.sum(exponent, axis=0, keepdims=True))
            grad_probs = mm(v2, g_own, NT)
            inner = jnp.sum(probs * grad_probs, axis=0, keepdims=True)
            grad_logits = (probs * (grad_probs - inner)).astype(bf16)
            grads[0] += mm(grad_logits, only(own, k2 * scale), TN)
            grads[1] += mm(grad_logits, q_own, NN)
            grads[2] += mm(probs.astype(bf16), g_own, NN)
        for i in range(3):
            out_ref[:, i * width + p * 128 : i * width + (p + 1) * 128] = grads[i].astype(bf16)


def attention(kernel, segs, scale, qkv, *more):
    seqs, n = segs.shape
    width = qkv.shape[1] // 3
    out_width = 3 * width if more else width
    rows = lambda w: pl.BlockSpec((n, w), lambda s: (s, 0))
    matmuls = (5 if more else 2) * 2 * seqs * n * n * width
    return pl.pallas_call(
        functools.partial(kernel, scale),
        grid=(seqs,),
        out_shape=jax.ShapeDtypeStruct((seqs * n, out_width), bf16),
        in_specs=[full((seqs, n)), rows(3 * width)]
        + [rows(width)] * len(more),
        out_specs=rows(out_width),
        name="attention_backward" if more else "attention",
        **params(8, 10 * matmuls, 2 * seqs * n * (3 * width + out_width), seqs * HEADS * n * n),
    )(segs, qkv, *more)


def full(shape):
    return pl.BlockSpec(shape, lambda *_: (0,) * len(shape))


def params(room, flops, moved, transcendentals=0):
    return dict(
        compiler_params=pltpu.CompilerParams(vmem_limit_bytes=int(room * 2**20)),
        cost_estimate=pl.CostEstimate(flops=flops // COST, transcendentals=transcendentals // COST, bytes_accessed=moved // COST),
    )


def mib(*shapes):
    return sum(math.prod(v.shape) * v.dtype.itemsize for v in shapes) / 2**20


def fetched(name, kernel, shapes, arrays, scratch=()):
    count = len(arrays)

    def body(*refs):
        outs, held, sems = refs[count : count + len(shapes)], refs[count + len(shapes) : 2 * count + len(shapes)], refs[2 * count + len(shapes)]
        copies = [pltpu.make_async_copy(src, dst, sems.at[i]) for i, (src, dst) in enumerate(zip(refs[:count], held))]
        for copy in copies:
            copy.start()
        for copy in copies:
            copy.wait()
        kernel(*held, *outs, *refs[2 * count + len(shapes) + 1 :])

    return pl.pallas_call(
        body,
        out_shape=shapes,
        in_specs=[pl.BlockSpec(memory_space=pltpu.HBM)] * count,
        out_specs=[pl.BlockSpec(memory_space=pltpu.VMEM)] * len(shapes),
        scratch_shapes=[pltpu.VMEM(v.shape, v.dtype) for v in arrays] + [pltpu.SemaphoreType.DMA((count,))] + [pltpu.VMEM(v.shape, v.dtype) for v in scratch],
        name=name,
        **params(58, 0, sum(v.size for v in arrays) * 4),
    )(*arrays)


def whole(name, kernel, shapes, arrays, scratch=(), pos=None, room=4):
    vmem = pl.BlockSpec(memory_space=pltpu.VMEM)
    lead = [] if pos is None else [pos]
    limit = 1.2 * mib(*arrays, *shapes, *scratch) + room if room == 4 else 1.1 * mib(*scratch) + room
    return pl.pallas_call(
        kernel,
        out_shape=shapes,
        in_specs=[pl.BlockSpec(memory_space=pltpu.SMEM)] * len(lead) + [vmem] * len(arrays),
        out_specs=[vmem] * len(shapes),
        scratch_shapes=[pltpu.VMEM(v.shape, v.dtype) for v in scratch],
        name=name,
        **params(limit, 0, sum(v.size for v in arrays) * 4),
    )(*lead, *arrays)


def pack(qkv, router, gains, out):
    rows, width = out.shape
    if rows % 8:
        small = jnp.concatenate([router.T, gains.T, jnp.zeros((rows, SMALL - 3), f32)], axis=1)
        return jnp.concatenate([qkv[0], qkv[1], qkv[2], small, out], axis=1).astype(bf16)

    def kernel(qkv_ref, router_ref, gains_ref, out_ref, to_ref, turn_ref):
        for i in range(3):
            to_ref[:, i * width : (i + 1) * width] = qkv_ref[i].astype(bf16)
        turn_ref[...] = jnp.zeros_like(turn_ref)
        turn_ref[0:1, :rows] = router_ref[...]
        turn_ref[1:3, :rows] = gains_ref[...]
        to_ref[:, 3 * width : 3 * width + SMALL] = turn_ref[...].T[:rows].astype(bf16)
        to_ref[:, 3 * width + SMALL :] = out_ref[...].astype(bf16)

    shape = [jax.ShapeDtypeStruct((rows, 4 * width + SMALL), bf16)]
    return fetched("pack", kernel, shape, [qkv, router, gains, out], scratch=[jax.ShapeDtypeStruct((SMALL, SMALL), f32)])[0]


def pack_rest(up, down):
    rows = up.shape[0]
    width, fold = down.shape[1], down.shape[0] // rows
    if rows % 8:
        return up.astype(bf16), jnp.concatenate([down[i * rows : (i + 1) * rows] for i in range(fold)], axis=1).astype(bf16)

    def kernel(up_ref, down_ref, first_ref, second_ref):
        first_ref[...] = up_ref[...].astype(bf16)
        for i in range(fold):
            second_ref[:, i * width : (i + 1) * width] = down_ref[i * rows : (i + 1) * rows].astype(bf16)

    return whole("pack_rest", kernel, [jax.ShapeDtypeStruct(up.shape, bf16), jax.ShapeDtypeStruct((rows, fold * width), bf16)], [up, down])


def like(count, width, kind):
    return jax.ShapeDtypeStruct((count, width), kind)


def project(picked, back_cot, w_qkv, w_small, room=8):
    count, width = picked.shape

    def kernel(picked_ref, cot_ref, w_ref, small_ref, hidden_ref, out_ref, score_ref, rows_ref, back_ref):
        rows = small_ref[:, :128].astype(f32).T[:8]
        rows_ref[...] = rows
        value = picked_ref[...].astype(f32)
        score = mm(picked_ref[...], small_ref[:, :128], NN)[:, :1]
        score_ref[...] = score
        back_ref[...] = (score * cot_ref[...].astype(f32)).astype(bf16)
        hidden_ref[...] = (value * norm_of(value) * rows[1:2]).astype(bf16)
        for j in range(3):
            cut = slice(j * width, (j + 1) * width)
            out_ref[:, cut] = mm(hidden_ref[...], w_ref[:, cut], NN).astype(bf16)

    shapes = [like(count, width, bf16), like(count, 3 * width, bf16), like(count, 1, f32), like(8, width, f32), like(count, width, bf16)]
    return whole("project", kernel, shapes, [picked, back_cot, w_qkv, w_small], room=room)


def devices_of(pos, steps, sizes):
    y, c, a, b = (lax.rem(pos[i] + steps[i], n) for i, n in enumerate((sizes["y"], 2, sizes["a"], sizes["b"])))
    return y, c, a, b


def weight_grad(left, right, jobs, shape, rows, pos, sizes):
    ny, na, nb = sizes["y"], sizes["a"], sizes["b"]
    blocks = ny * na * nb
    count, wide = left[0].shape[0], max(job[1] for job in jobs)

    def kernel(pos_ref, left_ref, left_other, right_ref, right_other, *refs):
        outs, acc, turned = refs[:4], refs[4], refs[5]
        chunk = na * nb * rows

        def columns(ref, y):
            if chunk % 128 == 0:
                return ref[:, pl.ds(pl.multiple_of((2 * y + pos_ref[1]) * chunk, 128), chunk)]
            both = ref[:, 2 * y * chunk : 2 * (y + 1) * chunk]
            return jnp.where(pos_ref[1] == 0, both[:, :chunk], both[:, chunk:])

        for side, ref in enumerate((left_ref, left_other)):
            for y in range(ny):
                chosen = ref.shape[1] == ny * chunk
                turned[side, y * chunk : (y + 1) * chunk, :] = (ref[:, y * chunk : (y + 1) * chunk] if chosen else columns(ref, y)).T
        for start, width, spots in jobs:
            total = mm(turned[0], right_ref[:, start : start + width], NN)
            total += mm(turned[1], right_other[:, start : start + width], NN)
            acc[:, :, :width] = total.reshape(blocks, rows, width)
            for ky in range(ny):
                for ka in range(na):
                    for kb in range(nb):
                        y, _, a, b = devices_of(pos_ref, (ky, 0, ka, kb), sizes)
                        value = acc[(y * na + a) * nb + b, :, :width].astype(bf16)
                        for column, some, part, row, to in spots:
                            if part == 0:
                                ref = outs[0].at[ky, ka] if kb == 0 else outs[1].at[kb - 1, ky, ka]
                            else:
                                ref = outs[2].at[kb, ka] if ky == 0 else outs[3].at[ky - 1, kb, ka]
                            ref[row : row + rows, to : to + some] = value[:, column : column + some]

    leads = [(ny, na), (nb - 1, ny, na), (nb, na), (ny - 1, nb, na)]
    outs = [jax.ShapeDtypeStruct(v + shape, bf16) for v in leads]
    scratch = [jax.ShapeDtypeStruct((blocks, rows, wide), f32), jax.ShapeDtypeStruct((2, blocks * rows, count), bf16)]
    vmem = pl.BlockSpec(memory_space=pltpu.VMEM)
    arrays = list(left) + list(right)
    return pl.pallas_call(
        kernel,
        out_shape=outs,
        in_specs=[pl.BlockSpec(memory_space=pltpu.SMEM)] + [vmem] * 4,
        out_specs=[vmem] * 4,
        scratch_shapes=[pltpu.VMEM(v.shape, v.dtype) for v in scratch],
        name="weight_grad",
        **params(mib(*scratch) * 1.1 + 9, 4 * count * blocks * rows * right[0].shape[1], sum(v.size for v in arrays) * 2),
    )(pos, *arrays)


def weight_grad_plain(left, right, jobs, shape, rows, pos, sizes):
    ny, na, nb = sizes["y"], sizes["a"], sizes["b"]
    left = [v if v.shape[1] == ny * na * nb * rows else columns_of(v, pos[1], sizes) for v in left]
    total = sum(dot(a, b, "rd,re->de") for a, b in zip(left, right)).astype(bf16).reshape(ny, na, nb, rows, -1)
    for axis, at in ((0, 0), (1, 2), (2, 3)):
        total = jnp.roll(total, -pos[at], axis)
    done = [jnp.zeros((ny, na, nb) + shape, bf16) for _ in range(2)]
    for start, _, spots in jobs:
        for column, some, part, row, to in spots:
            done[part] = done[part].at[..., row : row + rows, to : to + some].set(total[..., start + column : start + column + some])
    first, second = done[0].transpose(2, 0, 1, 3, 4), done[1].transpose(0, 2, 1, 3, 4)
    return first[0], first[1:], second[0], second[1:]


def weight_grad_own(lefts, rights, narrow, halves, pos, sizes):
    ny, na, nb = sizes["y"], sizes["a"], sizes["b"]
    blocks = 2 * ny * na * nb
    count, model = lefts[0].shape
    rows = model // blocks
    wide = max(w for part in halves for _, _, w in part)
    leads = [(nb, ny, na), (ny, nb, na)]
    shapes = [v + (rows, sum(w for _, _, w in part)) for v, part in zip(leads, halves)]
    if rows % 8:
        return weight_grad_own_plain(lefts, rights, narrow, halves, pos, sizes)

    def kernel(pos_ref, *refs):
        ins, outs, acc, turned = refs[: 2 * len(lefts) + 1], refs[2 * len(lefts) + 1 : -2], refs[-2], refs[-1]
        for i in range(len(lefts)):
            turned[i] = ins[i][...].T
        for part, some in enumerate(halves):
            to = 0
            for i, start, width in some:
                if i < 0:
                    value = ins[-1][...]
                    total = jnp.concatenate([value, jnp.zeros((width - value.shape[0], model), f32)]).T
                else:
                    total = mm(turned[i], ins[len(lefts) + i][:, start : start + width], NN)
                acc[:, :, :width] = total.reshape(blocks, rows, width)
                for kc in range(2):
                    for ky in range(ny):
                        for ka in range(na):
                            for kb in range(nb):
                                y, c, a, b = devices_of(pos_ref, (ky, kc, ka, kb), sizes)
                                ref = outs[2 * kc + part]
                                ref = ref.at[kb, ky, ka] if part == 0 else ref.at[ky, kb, ka]
                                ref[:, to : to + width] = acc[((y * 2 + c) * na + a) * nb + b, :, :width].astype(bf16)
                to += width

    outs = [jax.ShapeDtypeStruct(v, bf16) for v in shapes] * 2
    scratch = [jax.ShapeDtypeStruct((blocks, rows, wide), f32), jax.ShapeDtypeStruct((len(lefts), model, count), bf16)]
    vmem = pl.BlockSpec(memory_space=pltpu.VMEM)
    arrays = list(lefts) + list(rights) + [narrow]
    done = pl.pallas_call(
        kernel,
        out_shape=outs,
        in_specs=[pl.BlockSpec(memory_space=pltpu.SMEM)] + [vmem] * len(arrays),
        out_specs=[vmem] * 4,
        scratch_shapes=[pltpu.VMEM(v.shape, v.dtype) for v in scratch],
        name="weight_grad_own",
        **params(mib(*scratch) * 1.1 + 9, 2 * count * model * sum(v.shape[1] for v in rights), sum(v.size for v in arrays) * 2),
    )(pos, *arrays)
    return done[:2], done[2:]


def weight_grad_own_plain(lefts, rights, narrow, halves, pos, sizes):
    ny, na, nb = sizes["y"], sizes["a"], sizes["b"]
    done = []
    for part in halves:
        pieces = []
        for i, start, width in part:
            if i < 0:
                pieces.append(jnp.pad(narrow.T, ((0, 0), (0, width - narrow.shape[0]))))
            else:
                pieces.append(dot(lefts[i], rights[i][:, start : start + width], "rd,re->de"))
        total = jnp.concatenate(pieces, axis=1).astype(bf16)
        total = total.reshape(ny, 2, na, nb, -1, total.shape[1])
        for axis in range(4):
            total = jnp.roll(total, -pos[axis], axis)
        done.append(total)
    return [(done[0][:, kc].transpose(2, 0, 1, 3, 4), done[1][:, kc].transpose(0, 2, 1, 3, 4)) for kc in range(2)]


def norm_of(value):
    return lax.rsqrt(jnp.mean(value * value, axis=-1, keepdims=True) + norm_eps)


def feed_forward(mixed, picked, score, gain, w_out, w_up, pos, ny, room=9):
    count, width = picked.shape
    hidden = w_up.shape[1]

    def kernel(pos_ref, mixed_ref, picked_ref, score_ref, gain_ref, wo_ref, w_ref, attended_ref, first_ref, hidden_ref, activ_ref, slope_ref, cross_ref):
        attended = mm(mixed_ref[...], wo_ref[...], NN)
        first = picked_ref[...].astype(f32) + score_ref[...] * attended
        attended_ref[...] = attended
        first_ref[...] = first
        hidden_ref[...] = (first * norm_of(first) * gain_ref[2:3, :]).astype(bf16)
        c0 = (2.0 / math.pi) ** 0.5
        step = width // 2
        for j in range(hidden // step):
            cut = slice(j * step, (j + 1) * step)
            v = mm(hidden_ref[...], w_ref[:, cut], NN)
            square = v * v
            t = jnp.tanh(v * (c0 + (c0 * 0.044715) * square))
            cdf = 0.5 + 0.5 * t
            activ_ref[:, cut] = (v * cdf).astype(bf16)
            slope_ref[:, cut] = cdf + (cdf - cdf * cdf) * (v * (2.0 * c0 + (6.0 * 0.044715 * c0) * square))
        chunk = hidden // (2 * ny)
        for y in range(ny):
            start = pl.multiple_of((2 * y + 1 - pos_ref[1]) * chunk, 128)
            cross_ref[:, y * chunk : (y + 1) * chunk] = activ_ref[:, pl.ds(start, chunk)]

    shapes = [like(count, width, f32), like(count, width, f32), like(count, width, bf16), like(count, hidden, bf16), like(count, hidden, f32)]
    shapes += [like(count, hidden // 2, bf16)]
    return whole("feed_forward", kernel, shapes, [mixed, picked, score, gain, w_out, w_up], pos=pos, room=room)


def down_both(activ, slope, grad_out, w_down, first, score, back_cot, room=8):
    count, width = first.shape
    hidden = activ.shape[1]

    def kernel(activ_ref, slope_ref, grad_ref, w_ref, first_ref, score_ref, cot_ref, pre_ref, second_ref, dr_ref):
        step = width
        for j in range(hidden // step):
            cut = slice(j * step, (j + 1) * step)
            pre_ref[:, cut] = (mm(grad_ref[...], w_ref[cut, :], NT) * slope_ref[:, cut]).astype(bf16)
        total = mm(activ_ref[...], w_ref[...], NN)
        second_ref[...] = (first_ref[...] + score_ref[...] * total).astype(bf16)
        dr_ref[...] = jnp.sum(cot_ref[...].astype(f32) * total, axis=-1, keepdims=True)

    shapes = [like(count, hidden, bf16), like(count, width, bf16), like(count, 1, f32)]
    return whole("down_both", kernel, shapes, [activ, slope, grad_out, w_down, first, score, back_cot], room=room)


def back_of_norm(grad, value, gain):
    inv = norm_of(value)
    normed = value * inv
    scaled = grad * gain
    mean = jnp.mean(scaled * normed, axis=-1, keepdims=True)
    return (scaled - normed * mean) * inv, jnp.sum(grad * normed, axis=0, keepdims=True)


def up_back(grad_pre, w_out, w_up, first, attended, score, back_cot, gain, room=9):
    count, width = first.shape

    def kernel(pre_ref, wo_ref, w_ref, first_ref, attended_ref, score_ref, cot_ref, gain_ref, out_ref, low_ref, mixed_ref, dr_ref, dgain_ref):
        grad, dgain = back_of_norm(mm(pre_ref[...], w_ref[...], NT), first_ref[...], gain_ref[2:3, :])
        grad = cot_ref[...].astype(f32) + grad
        low = (score_ref[...] * grad).astype(bf16)
        out_ref[...] = grad
        low_ref[...] = low
        dgain_ref[...] = dgain
        dr_ref[...] = jnp.sum(grad * attended_ref[...], axis=-1, keepdims=True)
        mixed_ref[...] = mm(low, wo_ref[...], NT).astype(bf16)

    shapes = [like(count, width, f32), like(count, width, bf16), like(count, width, bf16), like(count, 1, f32), like(1, width, f32)]
    return whole("up_back", kernel, shapes, [grad_pre, w_out, w_up, first, attended, score, back_cot, gain], room=room)


def project_back(grad_projected, w_qkv, picked, rows, grad_first, drs, dgain_two, room=9):
    count, width = picked.shape

    def kernel(grad_ref, w_ref, picked_ref, rows_ref, first_ref, dr_ref, more_ref, two_ref, out_ref, narrow_ref):
        value, dr = picked_ref[...].astype(f32), dr_ref[...] + more_ref[...]
        grad, dgain = back_of_norm(mm(grad_ref[...], w_ref[...], NT), value, rows_ref[1:2, :])
        out_ref[...] = (first_ref[...] + grad + dr * rows_ref[0:1, :]).astype(bf16)
        drouter = jnp.sum(dr * value, axis=0, keepdims=True)
        narrow_ref[...] = jnp.concatenate([drouter, dgain, two_ref[...], jnp.zeros((5, width), f32)])

    shapes = [like(count, width, bf16), like(8, width, f32)]
    return whole("project_back", kernel, shapes, [grad_projected, w_qkv, picked, rows, grad_first, *drs, dgain_two], room=room)


def body(sizes, *args):
    tokens, cotangent, segment_ids, routed = args[:4]
    states = [args[4 + 4 * i : 8 + 4 * i] for i in range(6)]
    qkv_state, out_state, up_state, down_state, router_state, gains_state = states
    seqs, length, width = tokens.shape
    capacity = routed.shape[1]
    count = seqs * capacity
    rows = out_state[0].shape[0]
    hidden = up_state[0].shape[1]
    fold = down_state[0].shape[0] // rows
    scale = (width // HEADS) ** (-0.5)
    pos = jnp.stack([lax.axis_index(n) for n in ("y", "c", "a", "b")]).astype(jnp.int32)

    low = lambda v: v.astype(bf16)
    barrier = lax.optimization_barrier
    room = () if rows % 8 == 0 else (40,)
    send_qkv = pack(after(qkv_state[0], pos), router_state[0][None, :], gains_state[0], out_state[0])
    way_qkv = gather_axis(send_qkv, "a", sizes)
    send_up, send_down = pack_rest(up_state[0], down_state[0])

    here = routed[:, :, None] == jnp.arange(length, dtype=jnp.int32)[None, None, :]
    pick = here.astype(bf16)
    is_routed = jnp.any(here, axis=1)
    picked = dot(pick, tokens, "sct,std->scd").astype(bf16).reshape(count, width)
    back_cot = dot(pick, cotangent, "sct,std->scd").astype(bf16).reshape(count, width)
    way_qkv = stacked(halves_of(after(way_qkv, picked, back_cot)))
    way_qkv, send_up, send_down = barrier((way_qkv, send_up, send_down))
    way_qkv = go_second(way_qkv, sizes)
    far_up = paired(send_up, 2, sizes)
    segs = jnp.sum(jnp.where(here, segment_ids[:, None, :], 0), axis=-1).astype(f32)
    way_qkv, far_up, segs = hold(way_qkv, far_up, segs)
    way_qkv = stacked(way_qkv)
    (first_up,) = stacked([[send_up, far_up]])
    way_qkv, first_up = barrier((way_qkv, first_up))
    way_qkv = go_third(way_qkv, sizes)
    second_up = paired(first_up, 1, sizes)
    far_down = paired(send_down, 2, sizes)
    way_qkv, second_up, far_down = hold(way_qkv, second_up, far_down)
    (first_down,) = stacked([[send_down, far_down]])
    got = side_by_side(way_qkv)
    got = got, [shifted(v, "c", sizes, 1) for v in got]
    way_up = go_second((first_up, second_up), sizes)
    second_down = paired(first_down, 1, sizes)

    w_qkv, w_small, w_out = assemble(*got, after(pos, first_down), sizes, [(0, 3 * width), (3 * width, SMALL), (3 * width + SMALL, width)])
    w_out = w_out.reshape(width, width)
    w_qkv = w_qkv.reshape(width, 3 * width)
    hidden_one, projected, score, narrow, grad_down_out = project(picked, back_cot, w_qkv, w_small.reshape(width, SMALL), *room)
    way_up, projected = hold(way_up, projected)
    way_up = stacked(way_up)
    projected, way_up = barrier((projected, way_up))
    early_up = to_core([[v] for v in way_up], sizes)
    way_up = go_third(way_up, sizes)
    mixed = attention(attend_kernel, segs, scale, projected)
    way_down = go_second(after((first_down, second_down), mixed), sizes)
    way_up, mixed = hold(way_up, mixed)
    late_up = to_core([v[1:] for v in way_up], sizes)
    came_down = after([v[1:] for v in way_down], [v[1:] for v in way_up])
    way_down = stacked([v[:1] + c for v, c in zip(way_down, came_down)])
    early_down = to_core([[v] for v in way_down], sizes)
    down_there, pos_up = barrier((way_down, pos))
    way_down = go_third(way_down, sizes)
    got_up = joined(way_up, early_up, late_up)
    (w_up,) = assemble(*got_up, pos_up, sizes, [(0, hidden)], crossed=True)
    w_up = w_up.reshape(width, hidden)
    attended, first, hidden_two, activ_low, slope, activ_cross = feed_forward(
        mixed, picked, score, narrow, w_out, w_up, pos, sizes["y"], *room
    )

    way_down, activ_low = hold(way_down, activ_low)
    got_down = joined(way_down, early_down, to_core([v[1:] for v in way_down], sizes))
    activ_pair = [activ_low, shifted(after(activ_cross, got_down), "c", sizes, 1)]
    grad_down_pair = swapped(after(grad_down_out, got_down), sizes)
    hidden_two_pair = swapped(hidden_two, sizes)
    (w_down,) = assemble(*got_down, pos, sizes, [(i * width, width) for i in range(fold)], fold, crossed=True)
    w_down = w_down.reshape(hidden, width)
    grad_pre, second, dr_second = down_both(activ_low, slope, grad_down_out, w_down, first, score, back_cot, *room)

    (activ_pair, hidden_two_pair, grad_down_pair), grad_pre = hold([activ_pair, hidden_two_pair, grad_down_pair], grad_pre)
    grad_pre_pair = swapped(grad_pre, sizes)
    half = width // 2
    split = fold * rows
    make = weight_grad if rows % 8 == 0 else weight_grad_plain
    jobs = [(i * half, half, [(0, half, i, 0, 0)]) for i in range(2)]
    grad_2 = make(activ_pair, grad_down_pair, jobs, (split, half), split, pos, sizes)
    came_2 = sum_first(grad_2, sizes)
    grad_pre_pair = grad_pre_pair[:1] + after(grad_pre_pair[1:], grad_2)
    spot = lambda i: (i // fold, (i % fold) * rows, 0)
    jobs = [(i * width, width, [(0, half) + spot(2 * i), (half, half) + spot(2 * i + 1)]) for i in range(fold)]
    grad_1 = make(hidden_two_pair, grad_pre_pair, jobs, (split, half), rows, pos, sizes)
    came_1 = sum_first(grad_1, sizes)
    grad_pre = after(grad_pre, grad_1)
    grad_first, grad_attended, grad_mixed, dr_first, grad_gain_two = up_back(grad_pre, w_out, w_up, first, attended, score, back_cot, narrow, *room)
    grad_projected = attention(attend_back_kernel, segs, scale, projected, after(grad_mixed, came_2))
    grad_projected, came_1, came_2 = barrier((grad_projected, came_1, came_2))
    more_12 = sum_second([grad_2, grad_1], [came_2, came_1])
    grad_projected, more_12 = barrier((grad_projected, more_12))
    more_12 = send_second(more_12, sizes)
    grad_rows, grad_narrow = project_back(
        grad_projected, w_qkv, picked, narrow, grad_first, (dr_second, dr_first), grad_gain_two, *room
    )

    halves = [(0, 0, width), (0, width, width), (-1, 0, SMALL)], [(0, 2 * width, width), (1, 0, width)]
    own_0, other_0 = weight_grad_own([hidden_one, mixed], [grad_projected, grad_attended], grad_narrow, halves, pos, sizes)
    came_first = shifted(other_0[0], "c", sizes, 1)
    more_12 = after(more_12, own_0)
    own_12, part_12 = sum_third([grad_2, grad_1], [came_2, came_1], more_12)
    came_0 = [came_first, shifted(after(other_0[1], part_12), "c", sizes, 1)]
    came_0, part_12 = barrier((came_0, part_12))
    last_12 = send_parts(part_12, "a", sizes)
    grad_0 = sum_core(own_0, came_0)
    came_0 = sum_first(grad_0, sizes)
    shape = (seqs, capacity, width)
    second = after(second, grad_0)
    block_out = jnp.where(is_routed[:, :, None], low(dot(pick, second.reshape(shape), "sct,scd->std")), tokens)
    came_0, grad_rows, block_out = barrier((came_0, grad_rows, block_out))
    more_0 = sum_second([grad_0], [came_0])
    more_0, grad_rows = barrier((more_0, grad_rows))
    more_0 = send_second(more_0, sizes)
    tokens_grad = jnp.where(is_routed[:, :, None], low(dot(pick, grad_rows.reshape(shape), "sct,scd->std")), cotangent)
    more_0, tokens_grad, last_12 = barrier((more_0, tokens_grad, last_12))
    own_0, part_0 = sum_third([grad_0], [came_0], more_0)
    last_0 = send_parts(part_0, "a", sizes)
    last_12 = after(last_12, part_0)
    total_12 = add_up(own_12, last_12)
    sum_down, folded = total_12[:split], total_12[split:]
    sum_up = jnp.concatenate([folded[i * rows : (i + 1) * rows, j * half : (j + 1) * half] for j in range(2) for i in range(fold)], axis=1)
    new_qkv, new_out, new_gains, grad_router = finish(own_0, last_0, qkv_state, out_state, gains_state, 2 * width)
    new_up = adamw(up_state, sum_up, decay_rate, learn_rates[2])
    new_down = adamw(down_state, sum_down, decay_rate, learn_rates[3])
    new_router = adamw(router_state, grad_router[0], 0.0, learn_rates[4])
    return (block_out, tokens_grad, *new_qkv, *new_out, *new_up, *new_down, *new_router, *new_gains)


def solution(mesh):
    lead = mesh.shape["dp"] // 2
    inner = mesh.shape["fsdp"] // 4
    names = ("y", "c", "a", "b")
    fine = Mesh(mesh.devices.reshape(lead, 2, 4, inner), names)
    sizes = dict(zip(names, (lead, 2, 4, inner)))
    head, second, only = P(names, None, None), P(None, names, None), P(names, None)
    weights = (second,) * 4 + (only,) * 12 + (P(names),) * 4 + (P(None, names),) * 4
    return jax.shard_map(
        functools.partial(body, sizes),
        mesh=fine,
        in_specs=(head, head, only, only) + weights,
        out_specs=(head, head) + weights,
        check_vma=False,
    )
```

```python
import functools
import math

import jax
import jax.numpy as jnp
from jax import lax
from jax.experimental import pallas as pl
from jax.experimental.pallas import tpu as pltpu
from jax.sharding import Mesh, PartitionSpec as P

HEADS = 12
SMALL = 128

norm_eps = 1e-06
learn_rates = (0.03, 0.1, 0.03, 0.02, 0.03, 0.2)
beta_first = 0.5
beta_second = 0.5
adam_eps = 1e-08
decay_rate = 0.1
average_rate = 0.7
exact_mode = lax.Precision.HIGHEST
f32 = jnp.float32
bf16 = jnp.bfloat16


def shifted(value, axis, sizes, step):
    n = sizes[axis]
    return lax.ppermute(value, axis, [(i, (i + step) % n) for i in range(n)])


def after(value, *others):
    return lax.optimization_barrier((value, others))[0]


def paired(value, step, sizes):
    return lax.ppermute(value, "a", [(i, i ^ step) for i in range(sizes["a"])])


def hold(lists, *others):
    came, others = lax.optimization_barrier(([v[1:] for v in lists], others))
    return ([v[:1] + c for v, c in zip(lists, came)],) + others


def gather_axis(value, axis, sizes):
    return [value] + [shifted(value, axis, sizes, k) for k in range(1, sizes[axis])]


def halves_of(value):
    half = len(value) // 2
    return value[:half], value[half:]


def go_second(halves, sizes):
    return gather_axis(halves[0], "b", sizes), gather_axis(halves[1], "y", sizes)


def go_third(halves, sizes):
    return gather_axis(halves[0], "y", sizes), gather_axis(halves[1], "b", sizes)


def stacked(lists):
    arrays = [v for some in lists for v in some]

    def kernel(*refs):
        at = 0
        for out, some in zip(refs[len(arrays) :], lists):
            for k in range(len(some)):
                out[k] = refs[at + k][...]
            at += len(some)

    return whole("stacked", kernel, [jax.ShapeDtypeStruct((len(v),) + v[0].shape, v[0].dtype) for v in lists], arrays)


def to_core(lists, sizes):
    return [[shifted(v, "c", sizes, 1) for v in some] for some in lists]


def side_by_side(lists):
    def kernel(*refs):
        at = 0
        for out, some in zip(refs[-2:], lists):
            for k in range(len(some)):
                out[k] = refs[at][...]
                at += 1

    shapes = [jax.ShapeDtypeStruct((len(v),) + v[0].shape, bf16) for v in lists]
    return whole("side_by_side", kernel, shapes, lists[0] + lists[1])


def joined(lists, early, late):
    return lists[0] + lists[1], early[0] + late[0] + early[1] + late[1]


def take(value, index, axis):
    return lax.dynamic_index_in_dim(value, index, axis, keepdims=False)


def columns_of(value, core, sizes):
    ny = sizes["y"]
    chunk = value.shape[1] // (2 * ny)
    return jnp.concatenate([lax.dynamic_slice_in_dim(value, (2 * y + core) * chunk, chunk, 1) for y in range(ny)], axis=1)


def swapped(value, sizes):
    return [value, shifted(value, "c", sizes, 1)]


def add_up(own, came):
    own = own.astype(f32)
    for part in came:
        own = own + part.astype(f32)
    return own


def send_parts(parts, axis, sizes):
    return [shifted(parts[k].astype(bf16), axis, sizes, k + 1) for k in range(sizes[axis] - 1)]


def sum_first(grad, sizes):
    return send_parts(grad[1], "b", sizes), send_parts(grad[3], "y", sizes)


def sum_core(own, came):
    ins = [own[0], came[0], own[1], came[1]]
    shapes = [w for v in own for w in (v.shape[1:], (v.shape[0] - 1,) + v.shape[1:])]

    def kernel(*refs):
        outs = refs[len(ins) :]
        for i in range(2):
            for k in range(own[i].shape[0]):
                total = (refs[2 * i][k].astype(f32) + refs[2 * i + 1][k].astype(f32)).astype(bf16)
                if k == 0:
                    outs[2 * i][...] = total
                else:
                    outs[2 * i + 1][k - 1] = total

    return whole("sum_core", kernel, [jax.ShapeDtypeStruct(v, bf16) for v in shapes], ins)


def sum_second(grads, cames):
    count = len(grads)
    ins = [v for grad, came in zip(grads, cames) for v in [grad[0]] + came[0] + [grad[2]] + came[1]]
    counts = 1 + len(cames[0][0]), 1 + len(cames[0][1])
    shapes = [(grads[0][i].shape[0] - 1, count) + grads[0][i].shape[1:] for i in (0, 2)]

    def kernel(*refs):
        outs, at = refs[len(ins) :], 0
        for n in range(count):
            for out, some in zip(outs, counts):
                for k in range(out.shape[0]):
                    total = refs[at][k + 1].astype(f32)
                    for ref in refs[at + 1 : at + some]:
                        total += ref[k + 1].astype(f32)
                    out[k, n] = total.astype(bf16)
                at += some

    return whole("sum_second", kernel, [jax.ShapeDtypeStruct(v, bf16) for v in shapes], ins)


def sum_third(grads, cames, more, pos):
    count = len(grads)
    ins = [v for grad, came in zip(grads, cames) for v in [grad[0]] + came[0] + [grad[2]] + came[1]] + more[0] + more[1]
    counts = 1 + len(cames[0][0]), 1 + len(cames[0][1])
    na, rows, width = grads[0][0].shape[1:]
    cuts = (0, width), (width, width + grads[0][2].shape[-1])

    def kernel(pos_ref, *refs):
        odd = lax.rem(pos_ref[2], 2)
        wanted = (0, 1 + 2 * odd, 2, 3 - 2 * odd)
        outs, at, late = refs[len(ins) :], 0, sum(counts) * count
        for n in range(count):
            for part, (some, (start, stop)) in enumerate(zip(counts, cuts)):
                first = late + (len(more[0]) if part else 0)
                for out, k in zip(outs, wanted):
                    total = refs[at][0, k].astype(f32)
                    for ref in refs[at + 1 : at + some]:
                        total += ref[0, k].astype(f32)
                    for ref in refs[first : first + len(more[part])]:
                        total += ref[n, k].astype(f32)
                    out[n * rows : (n + 1) * rows, start:stop] = total.astype(out.dtype)
                at += some

    shape = count * rows, cuts[1][1]
    outs = whole("sum_third", kernel, [jax.ShapeDtypeStruct(shape, f32 if k == 0 else bf16) for k in range(na)], ins, pos=pos)
    return outs[0], list(outs[1:])


def sum_third_mixed(grads, cames, more, pos):
    ins = [v for grad, came in zip(grads, cames) for v in [grad[0]] + came[0] + [grad[2]] + came[1]] + more[0] + more[1]
    counts = 1 + len(cames[0][0]), 1 + len(cames[0][1])
    rows, width = grads[0][0].shape[2:]
    cuts = (0, width), (width, width + grads[0][2].shape[-1])

    def kernel(pos_ref, *refs):
        outs, at, late = refs[len(ins) :], 0, sum(counts) * 2
        odd = lax.rem(pos_ref[2], 2)
        near, far = 1 + 2 * odd, 3 - 2 * odd
        wanted = (
            ((outs[0], 0), (outs[4], 2), (outs[5].at[0], near), (outs[5].at[1], far)),
            ((outs[6], 0), (outs[1], near), (outs[2], 2), (outs[3], far)),
        )
        for n in range(2):
            for part, (some, (start, stop)) in enumerate(zip(counts, cuts)):
                first = late + (len(more[0]) if part else 0)
                for out, k in wanted[n]:
                    total = refs[at][0, k].astype(f32)
                    for ref in refs[at + 1 : at + some]:
                        total += ref[0, k].astype(f32)
                    for ref in refs[first : first + len(more[part])]:
                        total += ref[n, k].astype(f32)
                    out[:, start:stop] = total.astype(out.dtype)
                at += some

    wide = cuts[1][1]
    one = jax.ShapeDtypeStruct((rows, wide), bf16)
    own = jax.ShapeDtypeStruct((rows, wide), f32)
    shapes = [own, one, one, one, own, jax.ShapeDtypeStruct((2, rows, wide), bf16), own]
    done = whole("sum_third", kernel, shapes, ins, pos=pos)
    return (done[0], done[6]), done[1:4], done[4], done[5]


def sum_fourth(next_own, came):
    def kernel(next_ref, came_ref, send_ref):
        send_ref[...] = (next_ref[...] + came_ref[1].astype(f32)).astype(bf16)

    return whole("sum_fourth", kernel, [jax.ShapeDtypeStruct(next_own.shape, bf16)], [next_own, came])[0]


def send_second(parts, sizes):
    return send_parts(parts[0], "y", sizes), send_parts(parts[1], "b", sizes)


def places(sizes):
    half = sizes["a"] // 2
    out = []
    for kc in range(2):
        for ky in range(sizes["y"]):
            for kb in range(sizes["b"]):
                for ka in range(sizes["a"]):
                    part = 0 if ka < half else 1
                    out.append((kc, part, ky, kb, ka % half, (ky, kc, ka, kb)))
    return out


def owner(pos_ref, steps, sizes, crossed=False):
    ky, kc, ka, kb = steps
    y = lax.rem(pos_ref[0] + (sizes["y"] - ky), sizes["y"])
    c = lax.rem(pos_ref[1] + (2 - kc), 2)
    half = sizes["a"] // 2
    a = pos_ref[2] ^ (ka // half + 2 * (ka % half)) if crossed else lax.rem(pos_ref[2] + (sizes["a"] - ka), sizes["a"])
    b = lax.rem(pos_ref[3] + (sizes["b"] - kb), sizes["b"])
    return ((y * 2 + c) * sizes["a"] + a) * sizes["b"] + b


COST = 100


def source(ins, block, sizes):
    kc, part, ky, kb, ka, _ = block
    if len(ins) == 4:
        return ins[2 * kc + part][ky, kb, ka] if part == 0 else ins[2 * kc + part][kb, ky, ka]
    base = kc * (sizes["y"] + sizes["b"])
    return ins[base + ky][kb, ka] if part == 0 else ins[base + sizes["y"] + kb][ky, ka]


def assemble(here, there, pos, sizes, cuts, fold=1, crossed=False):
    rows = here[0].shape[-2]
    devices = 2 * sizes["y"] * sizes["b"] * sizes["a"]
    sources = list(here) + list(there)
    blocks = places(sizes)

    def kernel(pos_ref, *refs):
        ins, outs = refs[: len(sources)], refs[len(sources) :]
        for block in blocks:
            where = owner(pos_ref, block[-1], sizes, crossed)
            value = source(ins, block, sizes)
            for i, (start, width) in enumerate(cuts):
                if fold == 1:
                    outs[i][where] = value[:, start : start + width]
                else:
                    outs[0][where * fold + i] = value[:, start : start + width]

    shapes = [jax.ShapeDtypeStruct((devices, rows, width), bf16) for _, width in cuts]
    if fold > 1:
        shapes = [jax.ShapeDtypeStruct((devices * fold, rows, cuts[0][1]), bf16)]
    vmem = pl.BlockSpec(memory_space=pltpu.VMEM)
    return pl.pallas_call(
        kernel,
        out_shape=shapes,
        in_specs=[pl.BlockSpec(memory_space=pltpu.SMEM)] + [vmem] * len(sources),
        out_specs=[vmem] * len(shapes),
        name="assemble",
        **params(2 * mib(*sources) + 3, 0, 4 * devices * rows * sum(w for _, w in cuts)),
    )(pos, *sources)


def adamw(state, grad, decay, rate):
    weight, mean, square, average = state
    mean_next = beta_first * mean + (1.0 - beta_first) * grad
    square_next = beta_second * square + (1.0 - beta_second) * grad * grad
    update = mean_next / (jnp.sqrt(square_next) + adam_eps)
    weight_next = weight - rate * (update + decay * weight)
    average_next = average_rate * average + (1.0 - average_rate) * weight_next
    return [weight_next, mean_next, square_next, average_next]


def finish(own, came, qkv, out, gains, at):
    rows = own.shape[0]
    width = out[0].shape[1]
    starts = (0, width, 2 * width + SMALL)

    def kernel(*refs):
        ins, outs, turn = refs[: len(arrays)], refs[len(arrays) : -1], refs[-1]
        own_ref, came_refs, states = ins[0], ins[1 : 1 + len(came)], ins[1 + len(came) :]

        def total(start, size):
            value = own_ref[:, start : start + size]
            for ref in came_refs:
                value = value + ref[:, start : start + size].astype(f32)
            return value

        for i, start in enumerate(starts):
            done = adamw([ref[i] for ref in states[:4]], total(start, width), decay_rate, learn_rates[0])
            for ref, value in zip(outs[:4], done):
                ref[i] = value
        done = adamw([ref[...] for ref in states[4:8]], total(3 * width + SMALL, width), decay_rate, learn_rates[1])
        for ref, value in zip(outs[4:8], done):
            ref[...] = value
        turn[...] = jnp.zeros_like(turn)
        turn[:rows, :] = total(at, SMALL)
        turned = turn[...].T
        done = adamw([ref[...] for ref in states[8:12]], turned[1:3, :rows], 0.0, learn_rates[5])
        for ref, value in zip(outs[8:12], done):
            ref[...] = value
        outs[12][...] = turned[0:1, :rows]

    arrays = [own, *came, *qkv, *out, *gains]
    shapes = [jax.ShapeDtypeStruct(v.shape, f32) for v in (*qkv, *out, *gains)] + [jax.ShapeDtypeStruct((1, rows), f32)]
    done = whole("finish", kernel, shapes, arrays, scratch=[jax.ShapeDtypeStruct((SMALL, SMALL), f32)])
    return list(done[:4]), list(done[4:8]), list(done[8:12]), done[12]


def dot(a, b, spec):
    return jnp.einsum(spec, a, b, preferred_element_type=f32)


NT = (((1,), (1,)), ((), ()))
TN = (((0,), (0,)), ((), ()))
NN = (((1,), (0,)), ((), ()))


def mm(a, b, dims):
    return lax.dot_general(a, b, dims, preferred_element_type=f32)


def only(own, value):
    return jnp.where(own, value, 0.0).astype(bf16)


def heads_of(n):
    lane = lax.broadcasted_iota(jnp.int32, (n, 128), 1)
    return lane < 64, lane >= 64


def same_segment(segs_ref, n):
    row = segs_ref[pl.ds(pl.program_id(0), 1), :]
    return jnp.broadcast_to(row, (8, n)).T[:, :1] == row


def attend_kernel(scale, segs_ref, qkv_ref, out_ref):
    n, width = out_ref.shape
    query = lax.broadcasted_iota(jnp.int32, (n, n), 0)
    key = lax.broadcasted_iota(jnp.int32, (n, n), 1)
    allowed = same_segment(segs_ref, n) & (key <= query)
    for p in range(width // 128):
        q2, k2, v2 = (qkv_ref[:, i * width + p * 128 : i * width + (p + 1) * 128] for i in range(3))
        total = jnp.zeros((n, 128), f32)
        for own in heads_of(n):
            logits = jnp.where(allowed, mm(only(own, q2 * scale), k2, NT), -1e30)
            exponent = jnp.exp(logits - jnp.max(logits, axis=-1, keepdims=True))
            probs = exponent * (1.0 / jnp.sum(exponent, axis=-1, keepdims=True))
            total += mm(probs.astype(bf16), only(own, v2), NN)
        out_ref[:, p * 128 : (p + 1) * 128] = total.astype(bf16)


def attend_back_kernel(scale, segs_ref, qkv_ref, grad_ref, out_ref):
    n, width = grad_ref.shape
    key = lax.broadcasted_iota(jnp.int32, (n, n), 0)
    query = lax.broadcasted_iota(jnp.int32, (n, n), 1)
    allowed = same_segment(segs_ref, n) & (key <= query)
    for p in range(width // 128):
        q2, k2, v2 = (qkv_ref[:, i * width + p * 128 : i * width + (p + 1) * 128] for i in range(3))
        g2 = grad_ref[:, p * 128 : (p + 1) * 128]
        grads = [jnp.zeros((n, 128), f32) for _ in range(3)]
        for own in heads_of(n):
            q_own, g_own = only(own, q2 * scale), only(own, g2)
            logits = jnp.where(allowed, mm(k2, q_own, NT), -1e30)
            exponent = jnp.exp(logits - jnp.max(logits, axis=0, keepdims=True))
            probs = exponent * (1.0 / jnp.sum(exponent, axis=0, keepdims=True))
            grad_probs = mm(v2, g_own, NT)
            inner = jnp.sum(probs * grad_probs, axis=0, keepdims=True)
            grad_logits = (probs * (grad_probs - inner)).astype(bf16)
            grads[0] += mm(grad_logits, only(own, k2 * scale), TN)
            grads[1] += mm(grad_logits, q_own, NN)
            grads[2] += mm(probs.astype(bf16), g_own, NN)
        for i in range(3):
            out_ref[:, i * width + p * 128 : i * width + (p + 1) * 128] = grads[i].astype(bf16)


def attention(kernel, segs, scale, qkv, *more):
    seqs, n = segs.shape
    width = qkv.shape[1] // 3
    out_width = 3 * width if more else width
    rows = lambda w: pl.BlockSpec((n, w), lambda s: (s, 0))
    matmuls = (5 if more else 2) * 2 * seqs * n * n * width
    return pl.pallas_call(
        functools.partial(kernel, scale),
        grid=(seqs,),
        out_shape=jax.ShapeDtypeStruct((seqs * n, out_width), bf16),
        in_specs=[full((seqs, n)), rows(3 * width)]
        + [rows(width)] * len(more),
        out_specs=rows(out_width),
        name="attention_backward" if more else "attention",
        **params(8, 10 * matmuls, 2 * seqs * n * (3 * width + out_width), seqs * HEADS * n * n),
    )(segs, qkv, *more)


def full(shape):
    return pl.BlockSpec(shape, lambda *_: (0,) * len(shape))


def params(room, flops, moved, transcendentals=0):
    return dict(
        compiler_params=pltpu.CompilerParams(vmem_limit_bytes=int(room * 2**20)),
        cost_estimate=pl.CostEstimate(flops=flops // COST, transcendentals=transcendentals // COST, bytes_accessed=moved // COST),
    )


def mib(*shapes):
    return sum(math.prod(v.shape) * v.dtype.itemsize for v in shapes) / 2**20


def fetched(name, kernel, shapes, arrays, scratch=()):
    count = len(arrays)

    def body(*refs):
        outs, held, sems = refs[count : count + len(shapes)], refs[count + len(shapes) : 2 * count + len(shapes)], refs[2 * count + len(shapes)]
        copies = [pltpu.make_async_copy(src, dst, sems.at[i]) for i, (src, dst) in enumerate(zip(refs[:count], held))]
        for copy in copies:
            copy.start()
        for copy in copies:
            copy.wait()
        kernel(*held, *outs, *refs[2 * count + len(shapes) + 1 :])

    return pl.pallas_call(
        body,
        out_shape=shapes,
        in_specs=[pl.BlockSpec(memory_space=pltpu.HBM)] * count,
        out_specs=[pl.BlockSpec(memory_space=pltpu.VMEM)] * len(shapes),
        scratch_shapes=[pltpu.VMEM(v.shape, v.dtype) for v in arrays] + [pltpu.SemaphoreType.DMA((count,))] + [pltpu.VMEM(v.shape, v.dtype) for v in scratch],
        name=name,
        **params(58, 0, sum(v.size for v in arrays) * 4),
    )(*arrays)


def whole(name, kernel, shapes, arrays, scratch=(), pos=None, room=4):
    vmem = pl.BlockSpec(memory_space=pltpu.VMEM)
    lead = [] if pos is None else [pos]
    limit = 1.2 * mib(*arrays, *shapes, *scratch) + room if room == 4 else 1.1 * mib(*scratch) + room
    return pl.pallas_call(
        kernel,
        out_shape=shapes,
        in_specs=[pl.BlockSpec(memory_space=pltpu.SMEM)] * len(lead) + [vmem] * len(arrays),
        out_specs=[vmem] * len(shapes),
        scratch_shapes=[pltpu.VMEM(v.shape, v.dtype) for v in scratch],
        name=name,
        **params(limit, 0, sum(v.size for v in arrays) * 4),
    )(*lead, *arrays)


def pack(qkv, router, gains, out):
    rows, width = out.shape
    if rows % 8:
        small = jnp.concatenate([router.T, gains.T, jnp.zeros((rows, SMALL - 3), f32)], axis=1)
        return jnp.concatenate([qkv[0], qkv[1], qkv[2], small, out], axis=1).astype(bf16)

    def kernel(qkv_ref, router_ref, gains_ref, out_ref, to_ref, turn_ref):
        for i in range(3):
            to_ref[:, i * width : (i + 1) * width] = qkv_ref[i].astype(bf16)
        turn_ref[...] = jnp.zeros_like(turn_ref)
        turn_ref[0:1, :rows] = router_ref[...]
        turn_ref[1:3, :rows] = gains_ref[...]
        to_ref[:, 3 * width : 3 * width + SMALL] = turn_ref[...].T[:rows].astype(bf16)
        to_ref[:, 3 * width + SMALL :] = out_ref[...].astype(bf16)

    shape = [jax.ShapeDtypeStruct((rows, 4 * width + SMALL), bf16)]
    return fetched("pack", kernel, shape, [qkv, router, gains, out], scratch=[jax.ShapeDtypeStruct((SMALL, SMALL), f32)])[0]


def pack_rest(up, down):
    rows = up.shape[0]
    width, fold = down.shape[1], down.shape[0] // rows
    if rows % 8:
        return up.astype(bf16), jnp.concatenate([down[i * rows : (i + 1) * rows] for i in range(fold)], axis=1).astype(bf16)

    def kernel(up_ref, down_ref, first_ref, second_ref):
        first_ref[...] = up_ref[...].astype(bf16)
        for i in range(fold):
            second_ref[:, i * width : (i + 1) * width] = down_ref[i * rows : (i + 1) * rows].astype(bf16)

    return whole("pack_rest", kernel, [jax.ShapeDtypeStruct(up.shape, bf16), jax.ShapeDtypeStruct((rows, fold * width), bf16)], [up, down])


def like(count, width, kind):
    return jax.ShapeDtypeStruct((count, width), kind)


def project(picked, back_cot, w_qkv, w_small, room=8):
    count, width = picked.shape

    def kernel(picked_ref, cot_ref, w_ref, small_ref, hidden_ref, out_ref, score_ref, rows_ref, back_ref):
        rows = small_ref[:, :128].astype(f32).T[:8]
        rows_ref[...] = rows
        value = picked_ref[...].astype(f32)
        score = mm(picked_ref[...], small_ref[:, :128], NN)[:, :1]
        score_ref[...] = score
        back_ref[...] = (score * cot_ref[...].astype(f32)).astype(bf16)
        hidden_ref[...] = (value * norm_of(value) * rows[1:2]).astype(bf16)
        for j in range(3):
            cut = slice(j * width, (j + 1) * width)
            out_ref[:, cut] = mm(hidden_ref[...], w_ref[:, cut], NN).astype(bf16)

    shapes = [like(count, width, bf16), like(count, 3 * width, bf16), like(count, 1, f32), like(8, width, f32), like(count, width, bf16)]
    return whole("project", kernel, shapes, [picked, back_cot, w_qkv, w_small], room=room)


def devices_of(pos, steps, sizes):
    y, c, a, b = (lax.rem(pos[i] + steps[i], n) for i, n in enumerate((sizes["y"], 2, sizes["a"], sizes["b"])))
    return y, c, a, b


def weight_grad(left, right, jobs, shape, rows, pos, sizes):
    ny, na, nb = sizes["y"], sizes["a"], sizes["b"]
    blocks = ny * na * nb
    count, wide = left[0].shape[0], max(job[1] for job in jobs)

    def kernel(pos_ref, left_ref, left_other, right_ref, right_other, *refs):
        outs, acc, turned = refs[:4], refs[4], refs[5]
        chunk = na * nb * rows

        def columns(ref, y):
            if chunk % 128 == 0:
                return ref[:, pl.ds(pl.multiple_of((2 * y + pos_ref[1]) * chunk, 128), chunk)]
            both = ref[:, 2 * y * chunk : 2 * (y + 1) * chunk]
            return jnp.where(pos_ref[1] == 0, both[:, :chunk], both[:, chunk:])

        for side, ref in enumerate((left_ref, left_other)):
            for y in range(ny):
                chosen = ref.shape[1] == ny * chunk
                turned[side, y * chunk : (y + 1) * chunk, :] = (ref[:, y * chunk : (y + 1) * chunk] if chosen else columns(ref, y)).T
        for start, width, spots in jobs:
            total = mm(turned[0], right_ref[:, start : start + width], NN)
            total += mm(turned[1], right_other[:, start : start + width], NN)
            acc[:, :, :width] = total.reshape(blocks, rows, width)
            for ky in range(ny):
                for ka in range(na):
                    for kb in range(nb):
                        y, _, a, b = devices_of(pos_ref, (ky, 0, ka, kb), sizes)
                        value = acc[(y * na + a) * nb + b, :, :width].astype(bf16)
                        for column, some, part, row, to in spots:
                            if part == 0:
                                ref = outs[0].at[ky, ka] if kb == 0 else outs[1].at[kb - 1, ky, ka]
                            else:
                                ref = outs[2].at[kb, ka] if ky == 0 else outs[3].at[ky - 1, kb, ka]
                            ref[row : row + rows, to : to + some] = value[:, column : column + some]

    leads = [(ny, na), (nb - 1, ny, na), (nb, na), (ny - 1, nb, na)]
    outs = [jax.ShapeDtypeStruct(v + shape, bf16) for v in leads]
    scratch = [jax.ShapeDtypeStruct((blocks, rows, wide), f32), jax.ShapeDtypeStruct((2, blocks * rows, count), bf16)]
    vmem = pl.BlockSpec(memory_space=pltpu.VMEM)
    arrays = list(left) + list(right)
    return pl.pallas_call(
        kernel,
        out_shape=outs,
        in_specs=[pl.BlockSpec(memory_space=pltpu.SMEM)] + [vmem] * 4,
        out_specs=[vmem] * 4,
        scratch_shapes=[pltpu.VMEM(v.shape, v.dtype) for v in scratch],
        name="weight_grad",
        **params(mib(*scratch) * 1.1 + 9, 4 * count * blocks * rows * right[0].shape[1], sum(v.size for v in arrays) * 2),
    )(pos, *arrays)


def weight_grad_plain(left, right, jobs, shape, rows, pos, sizes):
    ny, na, nb = sizes["y"], sizes["a"], sizes["b"]
    left = [v if v.shape[1] == ny * na * nb * rows else columns_of(v, pos[1], sizes) for v in left]
    total = sum(dot(a, b, "rd,re->de") for a, b in zip(left, right)).astype(bf16).reshape(ny, na, nb, rows, -1)
    for axis, at in ((0, 0), (1, 2), (2, 3)):
        total = jnp.roll(total, -pos[at], axis)
    done = [jnp.zeros((ny, na, nb) + shape, bf16) for _ in range(2)]
    for start, _, spots in jobs:
        for column, some, part, row, to in spots:
            done[part] = done[part].at[..., row : row + rows, to : to + some].set(total[..., start + column : start + column + some])
    first, second = done[0].transpose(2, 0, 1, 3, 4), done[1].transpose(0, 2, 1, 3, 4)
    return first[0], first[1:], second[0], second[1:]


def weight_grad_own(lefts, rights, narrow, halves, pos, sizes):
    ny, na, nb = sizes["y"], sizes["a"], sizes["b"]
    blocks = 2 * ny * na * nb
    count, model = lefts[0].shape
    rows = model // blocks
    wide = max(w for part in halves for _, _, w in part)
    leads = [(nb, ny, na), (ny, nb, na)]
    shapes = [v + (rows, sum(w for _, _, w in part)) for v, part in zip(leads, halves)]
    if rows % 8:
        return weight_grad_own_plain(lefts, rights, narrow, halves, pos, sizes)

    def kernel(pos_ref, *refs):
        ins, outs, acc, turned = refs[: 2 * len(lefts) + 1], refs[2 * len(lefts) + 1 : -2], refs[-2], refs[-1]
        for i in range(len(lefts)):
            turned[i] = ins[i][...].T
        for part, some in enumerate(halves):
            to = 0
            for i, start, width in some:
                if i < 0:
                    value = ins[-1][...]
                    total = jnp.concatenate([value, jnp.zeros((width - value.shape[0], model), f32)]).T
                else:
                    total = mm(turned[i], ins[len(lefts) + i][:, start : start + width], NN)
                acc[:, :, :width] = total.reshape(blocks, rows, width)
                for kc in range(2):
                    for ky in range(ny):
                        for ka in range(na):
                            for kb in range(nb):
                                y, c, a, b = devices_of(pos_ref, (ky, kc, ka, kb), sizes)
                                ref = outs[2 * kc + part]
                                ref = ref.at[kb, ky, ka] if part == 0 else ref.at[ky, kb, ka]
                                ref[:, to : to + width] = acc[((y * 2 + c) * na + a) * nb + b, :, :width].astype(bf16)
                to += width

    outs = [jax.ShapeDtypeStruct(v, bf16) for v in shapes] * 2
    scratch = [jax.ShapeDtypeStruct((blocks, rows, wide), f32), jax.ShapeDtypeStruct((len(lefts), model, count), bf16)]
    vmem = pl.BlockSpec(memory_space=pltpu.VMEM)
    arrays = list(lefts) + list(rights) + [narrow]
    done = pl.pallas_call(
        kernel,
        out_shape=outs,
        in_specs=[pl.BlockSpec(memory_space=pltpu.SMEM)] + [vmem] * len(arrays),
        out_specs=[vmem] * 4,
        scratch_shapes=[pltpu.VMEM(v.shape, v.dtype) for v in scratch],
        name="weight_grad_own",
        **params(mib(*scratch) * 1.1 + 9, 2 * count * model * sum(v.shape[1] for v in rights), sum(v.size for v in arrays) * 2),
    )(pos, *arrays)
    return done[:2], done[2:]


def weight_grad_own_plain(lefts, rights, narrow, halves, pos, sizes):
    ny, na, nb = sizes["y"], sizes["a"], sizes["b"]
    done = []
    for part in halves:
        pieces = []
        for i, start, width in part:
            if i < 0:
                pieces.append(jnp.pad(narrow.T, ((0, 0), (0, width - narrow.shape[0]))))
            else:
                pieces.append(dot(lefts[i], rights[i][:, start : start + width], "rd,re->de"))
        total = jnp.concatenate(pieces, axis=1).astype(bf16)
        total = total.reshape(ny, 2, na, nb, -1, total.shape[1])
        for axis in range(4):
            total = jnp.roll(total, -pos[axis], axis)
        done.append(total)
    return [(done[0][:, kc].transpose(2, 0, 1, 3, 4), done[1][:, kc].transpose(0, 2, 1, 3, 4)) for kc in range(2)]


def norm_of(value):
    return lax.rsqrt(jnp.mean(value * value, axis=-1, keepdims=True) + norm_eps)


def feed_forward(mixed, picked, score, gain, w_out, w_up, pos, ny, room=9):
    count, width = picked.shape
    hidden = w_up.shape[1]

    def kernel(pos_ref, mixed_ref, picked_ref, score_ref, gain_ref, wo_ref, w_ref, attended_ref, first_ref, hidden_ref, activ_ref, slope_ref, cross_ref):
        attended = mm(mixed_ref[...], wo_ref[...], NN)
        first = picked_ref[...].astype(f32) + score_ref[...] * attended
        attended_ref[...] = attended
        first_ref[...] = first
        hidden_ref[...] = (first * norm_of(first) * gain_ref[2:3, :]).astype(bf16)
        c0 = (2.0 / math.pi) ** 0.5
        step = width // 2
        for j in range(hidden // step):
            cut = slice(j * step, (j + 1) * step)
            v = mm(hidden_ref[...], w_ref[:, cut], NN)
            square = v * v
            t = jnp.tanh(v * (c0 + (c0 * 0.044715) * square))
            cdf = 0.5 + 0.5 * t
            activ_ref[:, cut] = (v * cdf).astype(bf16)
            slope_ref[:, cut] = cdf + (cdf - cdf * cdf) * (v * (2.0 * c0 + (6.0 * 0.044715 * c0) * square))
        chunk = hidden // (2 * ny)
        for y in range(ny):
            start = pl.multiple_of((2 * y + 1 - pos_ref[1]) * chunk, 128)
            cross_ref[:, y * chunk : (y + 1) * chunk] = activ_ref[:, pl.ds(start, chunk)]

    shapes = [like(count, width, f32), like(count, width, f32), like(count, width, bf16), like(count, hidden, bf16), like(count, hidden, f32)]
    shapes += [like(count, hidden // 2, bf16)]
    return whole("feed_forward", kernel, shapes, [mixed, picked, score, gain, w_out, w_up], pos=pos, room=room)


def down_both(activ, slope, grad_out, w_down, first, score, back_cot, room=8):
    count, width = first.shape
    hidden = activ.shape[1]

    def kernel(activ_ref, slope_ref, grad_ref, w_ref, first_ref, score_ref, cot_ref, pre_ref, second_ref, dr_ref):
        step = width
        for j in range(hidden // step):
            cut = slice(j * step, (j + 1) * step)
            pre_ref[:, cut] = (mm(grad_ref[...], w_ref[cut, :], NT) * slope_ref[:, cut]).astype(bf16)
        total = mm(activ_ref[...], w_ref[...], NN)
        second_ref[...] = (first_ref[...] + score_ref[...] * total).astype(bf16)
        dr_ref[...] = jnp.sum(cot_ref[...].astype(f32) * total, axis=-1, keepdims=True)

    shapes = [like(count, hidden, bf16), like(count, width, bf16), like(count, 1, f32)]
    return whole("down_both", kernel, shapes, [activ, slope, grad_out, w_down, first, score, back_cot], room=room)


def back_of_norm(grad, value, gain):
    inv = norm_of(value)
    normed = value * inv
    scaled = grad * gain
    mean = jnp.mean(scaled * normed, axis=-1, keepdims=True)
    return (scaled - normed * mean) * inv, jnp.sum(grad * normed, axis=0, keepdims=True)


def up_back(grad_pre, w_out, w_up, first, attended, score, back_cot, gain, room=9):
    count, width = first.shape

    def kernel(pre_ref, wo_ref, w_ref, first_ref, attended_ref, score_ref, cot_ref, gain_ref, out_ref, low_ref, mixed_ref, dr_ref, dgain_ref):
        grad, dgain = back_of_norm(mm(pre_ref[...], w_ref[...], NT), first_ref[...], gain_ref[2:3, :])
        grad = cot_ref[...].astype(f32) + grad
        low = (score_ref[...] * grad).astype(bf16)
        out_ref[...] = grad
        low_ref[...] = low
        dgain_ref[...] = dgain
        dr_ref[...] = jnp.sum(grad * attended_ref[...], axis=-1, keepdims=True)
        mixed_ref[...] = mm(low, wo_ref[...], NT).astype(bf16)

    shapes = [like(count, width, f32), like(count, width, bf16), like(count, width, bf16), like(count, 1, f32), like(1, width, f32)]
    return whole("up_back", kernel, shapes, [grad_pre, w_out, w_up, first, attended, score, back_cot, gain], room=room)


def project_back(grad_projected, w_qkv, picked, rows, grad_first, drs, dgain_two, room=9):
    count, width = picked.shape

    def kernel(grad_ref, w_ref, picked_ref, rows_ref, first_ref, dr_ref, more_ref, two_ref, out_ref, narrow_ref):
        value, dr = picked_ref[...].astype(f32), dr_ref[...] + more_ref[...]
        grad, dgain = back_of_norm(mm(grad_ref[...], w_ref[...], NT), value, rows_ref[1:2, :])
        out_ref[...] = (first_ref[...] + grad + dr * rows_ref[0:1, :]).astype(bf16)
        drouter = jnp.sum(dr * value, axis=0, keepdims=True)
        narrow_ref[...] = jnp.concatenate([drouter, dgain, two_ref[...], jnp.zeros((5, width), f32)])

    shapes = [like(count, width, bf16), like(8, width, f32)]
    return whole("project_back", kernel, shapes, [grad_projected, w_qkv, picked, rows, grad_first, *drs, dgain_two], room=room)


def body(sizes, *args):
    tokens, cotangent, segment_ids, routed = args[:4]
    states = [args[4 + 4 * i : 8 + 4 * i] for i in range(6)]
    qkv_state, out_state, up_state, down_state, router_state, gains_state = states
    seqs, length, width = tokens.shape
    capacity = routed.shape[1]
    count = seqs * capacity
    rows = out_state[0].shape[0]
    hidden = up_state[0].shape[1]
    fold = down_state[0].shape[0] // rows
    scale = (width // HEADS) ** (-0.5)
    pos = jnp.stack([lax.axis_index(n) for n in ("y", "c", "a", "b")]).astype(jnp.int32)

    low = lambda v: v.astype(bf16)
    barrier = lax.optimization_barrier
    room = () if rows % 8 == 0 else (40,)
    send_qkv = pack(after(qkv_state[0], pos), router_state[0][None, :], gains_state[0], out_state[0])
    way_qkv = gather_axis(send_qkv, "a", sizes)
    send_up, send_down = pack_rest(up_state[0], down_state[0])

    here = routed[:, :, None] == jnp.arange(length, dtype=jnp.int32)[None, None, :]
    pick = here.astype(bf16)
    is_routed = jnp.any(here, axis=1)
    picked = dot(pick, tokens, "sct,std->scd").astype(bf16).reshape(count, width)
    back_cot = dot(pick, cotangent, "sct,std->scd").astype(bf16).reshape(count, width)
    way_qkv = stacked(halves_of(after(way_qkv, picked, back_cot)))
    way_qkv, send_up, send_down = barrier((way_qkv, send_up, send_down))
    way_qkv = go_second(way_qkv, sizes)
    far_up = paired(send_up, 2, sizes)
    segs = jnp.sum(jnp.where(here, segment_ids[:, None, :], 0), axis=-1).astype(f32)
    way_qkv, far_up, segs = hold(way_qkv, far_up, segs)
    way_qkv = stacked(way_qkv)
    (first_up,) = stacked([[send_up, far_up]])
    way_qkv, first_up = barrier((way_qkv, first_up))
    way_qkv = go_third(way_qkv, sizes)
    second_up = paired(first_up, 1, sizes)
    far_down = paired(send_down, 2, sizes)
    way_qkv, second_up, far_down = hold(way_qkv, second_up, far_down)
    (first_down,) = stacked([[send_down, far_down]])
    got = side_by_side(way_qkv)
    got = got, [shifted(v, "c", sizes, 1) for v in got]
    way_up = go_second((first_up, second_up), sizes)
    second_down = paired(first_down, 1, sizes)

    w_qkv, w_small, w_out = assemble(*got, after(pos, first_down), sizes, [(0, 3 * width), (3 * width, SMALL), (3 * width + SMALL, width)])
    w_out = w_out.reshape(width, width)
    w_qkv = w_qkv.reshape(width, 3 * width)
    hidden_one, projected, score, narrow, grad_down_out = project(picked, back_cot, w_qkv, w_small.reshape(width, SMALL), *room)
    way_up, projected = hold(way_up, projected)
    way_up = stacked(way_up)
    projected, way_up = barrier((projected, way_up))
    early_up = to_core([[v] for v in way_up], sizes)
    way_up = go_third(way_up, sizes)
    mixed = attention(attend_kernel, segs, scale, projected)
    way_down = go_second(after((first_down, second_down), mixed), sizes)
    way_up, mixed = hold(way_up, mixed)
    late_up = to_core([v[1:] for v in way_up], sizes)
    came_down = after([v[1:] for v in way_down], [v[1:] for v in way_up])
    way_down = stacked([v[:1] + c for v, c in zip(way_down, came_down)])
    early_down = to_core([[v] for v in way_down], sizes)
    down_there, pos_up = barrier((way_down, pos))
    way_down = go_third(way_down, sizes)
    got_up = joined(way_up, early_up, late_up)
    (w_up,) = assemble(*got_up, pos_up, sizes, [(0, hidden)], crossed=True)
    w_up = w_up.reshape(width, hidden)
    attended, first, hidden_two, activ_low, slope, activ_cross = feed_forward(
        mixed, picked, score, narrow, w_out, w_up, pos, sizes["y"], *room
    )

    way_down, activ_low = hold(way_down, activ_low)
    got_down = joined(way_down, early_down, to_core([v[1:] for v in way_down], sizes))
    activ_pair = [activ_low, shifted(after(activ_cross, got_down), "c", sizes, 1)]
    grad_down_pair = swapped(after(grad_down_out, got_down), sizes)
    hidden_two_pair = swapped(hidden_two, sizes)
    (w_down,) = assemble(*got_down, pos, sizes, [(i * width, width) for i in range(fold)], fold, crossed=True)
    w_down = w_down.reshape(hidden, width)
    grad_pre, second, dr_second = down_both(activ_low, slope, grad_down_out, w_down, first, score, back_cot, *room)

    (activ_pair, hidden_two_pair, grad_down_pair), grad_pre = hold([activ_pair, hidden_two_pair, grad_down_pair], grad_pre)
    grad_pre_pair = swapped(grad_pre, sizes)
    half = width // 2
    split = fold * rows
    make = weight_grad if rows % 8 == 0 else weight_grad_plain
    jobs = [(i * half, half, [(0, half, i, 0, 0)]) for i in range(2)]
    grad_2 = make(activ_pair, grad_down_pair, jobs, (split, half), split, pos, sizes)
    came_2 = sum_first(grad_2, sizes)
    grad_pre_pair = grad_pre_pair[:1] + after(grad_pre_pair[1:], grad_2)
    spot = lambda i: (i // fold, (i % fold) * rows, 0)
    jobs = [(i * width, width, [(0, half) + spot(2 * i), (half, half) + spot(2 * i + 1)]) for i in range(fold)]
    grad_1 = make(hidden_two_pair, grad_pre_pair, jobs, (split, half), rows, pos, sizes)
    came_1 = sum_first(grad_1, sizes)
    grad_pre = after(grad_pre, grad_1)
    grad_first, grad_attended, grad_mixed, dr_first, grad_gain_two = up_back(grad_pre, w_out, w_up, first, attended, score, back_cot, narrow, *room)
    grad_projected = attention(attend_back_kernel, segs, scale, projected, after(grad_mixed, came_2))
    grad_projected, came_1, came_2 = barrier((grad_projected, came_1, came_2))
    more_12 = sum_second([grad_2, grad_1], [came_2, came_1])
    grad_projected, more_12 = barrier((grad_projected, more_12))
    more_12 = send_second(more_12, sizes)
    grad_rows, grad_narrow = project_back(
        grad_projected, w_qkv, picked, narrow, grad_first, (dr_second, dr_first), grad_gain_two, *room
    )

    halves = [(0, 0, width), (0, width, width), (-1, 0, SMALL)], [(0, 2 * width, width), (1, 0, width)]
    own_0, other_0 = weight_grad_own([hidden_one, mixed], [grad_projected, grad_attended], grad_narrow, halves, pos, sizes)
    came_first = shifted(other_0[0], "c", sizes, 1)
    more_12 = after(more_12, own_0)
    own_12, part_12, next_2, cross_2 = sum_third_mixed([grad_2, grad_1], [came_2, came_1], more_12, pos)
    came_0 = [came_first, shifted(after(other_0[1], part_12), "c", sizes, 1)]
    came_0, part_12 = barrier((came_0, part_12))
    cross_2 = paired(cross_2, 1, sizes)
    last_1 = [paired(v, k + 1, sizes) for k, v in enumerate(part_12)]
    grad_0 = sum_core(own_0, came_0)
    came_0 = sum_first(grad_0, sizes)
    shape = (seqs, capacity, width)
    second = after(second, grad_0)
    block_out = jnp.where(is_routed[:, :, None], low(dot(pick, second.reshape(shape), "sct,scd->std")), tokens)
    came_0, grad_rows, block_out, cross_2 = barrier((came_0, grad_rows, block_out, cross_2))
    last_2 = [paired(sum_fourth(next_2, cross_2), 2, sizes)]
    more_0 = sum_second([grad_0], [came_0])
    more_0, grad_rows = barrier((more_0, grad_rows))
    more_0 = send_second(more_0, sizes)
    tokens_grad = jnp.where(is_routed[:, :, None], low(dot(pick, grad_rows.reshape(shape), "sct,scd->std")), cotangent)
    more_0, tokens_grad, last_1, last_2 = barrier((more_0, tokens_grad, last_1, last_2))
    own_0, part_0 = sum_third([grad_0], [came_0], more_0, pos)
    last_0 = [paired(v, k + 1, sizes) for k, v in enumerate(part_0)]
    last_1, last_2, cross_2 = after((last_1, last_2, cross_2), part_0)
    sum_down, folded = add_up(own_12[0], [cross_2[0]] + last_2), add_up(own_12[1], last_1)
    sum_up = jnp.concatenate([folded[i * rows : (i + 1) * rows, j * half : (j + 1) * half] for j in range(2) for i in range(fold)], axis=1)
    new_qkv, new_out, new_gains, grad_router = finish(own_0, last_0, qkv_state, out_state, gains_state, 2 * width)
    new_up = adamw(up_state, sum_up, decay_rate, learn_rates[2])
    new_down = adamw(down_state, sum_down, decay_rate, learn_rates[3])
    new_router = adamw(router_state, grad_router[0], 0.0, learn_rates[4])
    return (block_out, tokens_grad, *new_qkv, *new_out, *new_up, *new_down, *new_router, *new_gains)


def solution(mesh):
    lead = mesh.shape["dp"] // 2
    inner = mesh.shape["fsdp"] // 4
    names = ("y", "c", "a", "b")
    fine = Mesh(mesh.devices.reshape(lead, 2, 4, inner), names)
    sizes = dict(zip(names, (lead, 2, 4, inner)))
    head, second, only = P(names, None, None), P(None, names, None), P(names, None)
    weights = (second,) * 4 + (only,) * 12 + (P(names),) * 4 + (P(None, names),) * 4
    return jax.shard_map(
        functools.partial(body, sizes),
        mesh=fine,
        in_specs=(head, head, only, only) + weights,
        out_specs=(head, head) + weights,
        check_vma=False,
    )
```
